32 devices in a mesh: dp: 4 (over z), expert: 8 (over y, x, core).
Axes of the slice: x: 2, y: 2, z: 4, core: 2. Of those that a mesh axis runs over, the one named last changes fastest.
Arguments:
- tokens: bfloat16 [8192, 2048], P(('dp', 'expert')), may hold values from -6 to 6
- cotangent: bfloat16 [8192, 2048], P(('dp', 'expert')), may hold values from -6 to 6
- lengths: int32 [32], P(('dp', 'expert')), may hold values from 64 to 256, as said below
- deal_order: int32 [8, 4], replicated, may hold values from 0 to 3, each once within a row
- routes: int32 [8192, 8], P(('dp', 'expert')), may hold values from 0 to 15, all different within a row; in each aligned block of 256 rows (0 to 255, 256 to 511, ...) at most 144 rows name the same one
- balance_coef: float32 [1], replicated, may hold values from 0.5 to 2
- w_query: bfloat16 [2048, 2048], P('expert'), may hold values from -0.125 to 0.125
- w_key: bfloat16 [2048, 2048], P('expert'), may hold values from -0.125 to 0.125
- w_value: bfloat16 [2048, 2048], P('expert'), may hold values from -0.125 to 0.125
- w_out: bfloat16 [2048, 2048], P('expert'), may hold values from -1.5 to 1.5
- w_router: bfloat16 [2048, 16], P('expert'), may hold values from -0.0625 to 0.0625
- attn_gain: bfloat16 [2048], P('expert'), may hold values from 0.099609375 to 1.8984375
- mlp_gain: bfloat16 [2048], P('expert'), may hold values from 0.099609375 to 1.8984375
- query_gain: bfloat16 [128], P('expert'), may hold values from 0.099609375 to 1.8984375
- key_gain: bfloat16 [128], P('expert'), may hold values from 0.099609375 to 1.8984375
- w_gate: bfloat16 [16, 2048, 1024], P('expert'), may hold values from -0.125 to 0.125
- w_up: bfloat16 [16, 2048, 1024], P('expert'), may hold values from -0.125 to 0.125
- w_down: bfloat16 [16, 1024, 2048], P('expert'), may hold values from -0.75 to 0.75
Outputs:
- output: bfloat16 [8192, 2048], P(('dp', 'expert'))
- balance_loss: float32 [1], replicated
- grad_input: float32 [8192, 2048], P(('dp', 'expert'))
- grad_query: float32 [2048, 2048], P('expert')
- grad_key: float32 [2048, 2048], P('expert')
- grad_value: float32 [2048, 2048], P('expert')
- grad_out: float32 [2048, 2048], P('expert')
- grad_router: float32 [2048, 16], P('expert')
- grad_attn_gain: float32 [2048], P('expert')
- grad_mlp_gain: float32 [2048], P('expert')
- grad_query_gain: float32 [128], P('expert')
- grad_key_gain: float32 [128], P('expert')
- grad_gate: float32 [16, 2048, 1024], P('expert', 'dp')
- grad_up: float32 [16, 2048, 1024], P('expert', 'dp')
- grad_down: float32 [16, 1024, 2048], P('expert', 'dp')
The draws below stay inside these ranges and needn't reach their ends.
Inputs may be any that keep to these rules, and one draw needn't show every extreme that they name: Each sequence's live tokens are its first lengths[s] rows; the rest are padding. The first sequence has 64 live tokens and the last is full. Each row of deal_order names every dp index once. Within the rows of one sequence no expert is named by more than 144 routes; some expert reaches 144. A token names 8 different experts.
All inputs are finite; a program needn't handle non-finite values.
Results may differ from the reference program's by a relative error of at most 0.022.
Values may be sent and summed in bfloat16 or wider, within the bound.
A program may use at most 320 MiB of HBM per device.

```python
import math
import jax
import jax.numpy as jnp
import numpy as np
from jax import lax

D = 2048
HEADS = 16
HEAD_DIM = 128
HD = 2048
FF = 1024
TOP = 8
EXPERTS = 16
TOK_DEV = 256
RANKS = 4
COLUMNS = 8
SEQS = 32
TOKENS = 8192
CAP = 144
N_DP = 4
N_EXPERT = 8


def draw_lengths(key, part):
    low_len = TOK_DEV // 4
    rising = low_len + 3 * low_len * jnp.arange(SEQS, dtype=jnp.int32) // (SEQS - 1)
    jitter = jax.random.randint(key, (SEQS,), -(TOK_DEV // 16), TOK_DEV // 16 + 1)
    lengths_all = jnp.clip(rising + jitter, low_len, TOK_DEV)
    lengths_all = lengths_all.at[0].set(low_len)
    lengths_all = lengths_all.at[SEQS - 1].set(TOK_DEV)
    return lengths_all.astype(jnp.int32)


def shard_levels(rng, dims, split, smallest, largest):
    def one(axis_at, blocks):
        heights = jax.random.uniform(jax.random.fold_in(jax.random.fold_in(rng, 6), axis_at), (blocks,), jnp.float32, smallest / len(split), largest / len(split))
        return jnp.repeat(jnp.exp(heights), dims[axis_at] // blocks).reshape((-1,) + (1,) * (len(dims) - axis_at - 1))

    gain = one(*split[0])
    for cut in split[1:]:
        gain = gain * one(*cut)
    return gain


def deal_out(rng, own, number, rows, count, top, reach, slope):
    ranking = jax.random.permutation(rng, count)
    crowded, common = load_shares(count, rows * top, reach, slope, True), load_shares(count, rows * top, reach, slope, False)
    places = jnp.arange(count)

    def named(tallies, turn):
        used = int((tallies > 0).sum())
        fixed = max(1, used // 4)
        passed = fixed + (places - fixed + turn * (used - fixed)) % max(1, count - fixed)
        return jnp.zeros((count,), jnp.int32).at[ranking[jnp.where(places < fixed, places, passed)]].set(jnp.asarray(tallies, jnp.int32))

    tallies = jnp.where(number % 4 == 0, named(crowded, number // 4), named(common, number - number // 4 - 1))
    mixed = jax.random.permutation(jax.random.fold_in(own, 3), count)
    source_of, receiver = mixed[0:count // 2 * 2:2], mixed[1:count // 2 * 2:2]
    slack = jnp.minimum(tallies[source_of] - 1, reach - tallies[receiver]) // 2
    slack = jnp.where((source_of == ranking[0]) | (receiver == ranking[0]) | (tallies[receiver] == 0), 0, jnp.maximum(slack, 0))
    passed = jax.random.randint(jax.random.fold_in(own, 4), (count // 2,), 0, 1 << 20) % (slack + 1)
    tallies = tallies.at[source_of].add(-passed).at[receiver].add(passed)
    items = jnp.searchsorted(jnp.cumsum(tallies), jnp.arange(rows * top), side="right").astype(jnp.int32)
    grid = items.reshape(top, rows).T
    grid = grid[jax.random.permutation(jax.random.fold_in(own, 1), rows)]
    turn = jax.random.randint(jax.random.fold_in(own, 2), (rows, 1), 0, top)
    return jnp.take_along_axis(grid, (jnp.arange(top)[None, :] + turn) % top, axis=1)


def load_shares(count, total, limit, lean, full):
    weights = [(1 << 20) // math.isqrt(rank ** lean) + 1 for rank in range(1, count + 1)]
    largest = limit if full else min(limit, max(-(-total // count), total * weights[0] // sum(weights)))
    least = 1 if total - largest >= count - 1 else 0
    holding, spare = [largest] + [least] * (count - 1), total - largest - least * (count - 1)
    while spare > 0:
        movable = [i for i in range(1, count) if holding[i] < largest] or [i for i in range(1, count) if holding[i] < limit]
        mass, remaining = sum([weights[i] for i in movable]), spare
        for i in movable:
            extra = min(limit - holding[i], max(1, remaining * weights[i] // mass), spare)
            holding[i] = holding[i] + extra
            spare = spare - extra
    return np.array(holding)


def scatter_about(key, dims, spread, limit, split=(), kind=jnp.bfloat16):
    gain = shard_levels(key, dims, split, -0.22, 0.18) if split else 1.0
    drawn = jax.random.normal(key, dims, jnp.float32) * spread * gain
    return jnp.minimum(jnp.maximum(drawn, -limit), limit).astype(kind)


def setup_inputs(seed: int = 0) -> dict:
    splits = jax.random.split(jax.random.key(seed), 19)
    tokens = scatter_about(splits[0], (TOKENS, D), 1.0, 6.0, ((0, 32),))
    cotangent = scatter_about(splits[1], (TOKENS, D), 1.0, 6.0, ((0, 32),))
    lengths = draw_lengths(jax.random.fold_in(splits[18], 71), 0)
    deal_order = jax.vmap(lambda own: jax.random.permutation(own, RANKS))(jax.random.split(splits[3], COLUMNS)).reshape((COLUMNS, RANKS)).astype(jnp.int32)
    routes_keys = jax.random.split(jax.random.fold_in(splits[4], 1), TOKENS // TOK_DEV)
    routes_turns = jax.random.permutation(jax.random.fold_in(splits[4], 3), TOKENS // TOK_DEV)
    routes = jax.vmap(lambda own, number: deal_out(jax.random.fold_in(splits[4], 2), own, number, TOK_DEV, EXPERTS, TOP, CAP, 1))(routes_keys, routes_turns).reshape((TOKENS, TOP))
    balance_coef = jnp.clip(jnp.exp(jax.random.uniform(splits[5], (1,), jnp.float32, math.log(0.5), math.log(2.0))), 0.5, 2.0)
    w_query = scatter_about(splits[6], (D, HD), D ** -0.5, 0.125, ((0, 8),))
    w_key = scatter_about(splits[7], (D, HD), D ** -0.5, 0.125, ((0, 8),))
    w_value = scatter_about(splits[8], (D, HD), D ** -0.5, 0.125, ((0, 8),))
    w_out = scatter_about(splits[9], (HD, D), (HD // 128) ** -0.5, 1.5, ((0, 8),))
    w_router = scatter_about(splits[10], (D, EXPERTS), (4 * D) ** -0.5, 0.0625, ((0, 8),))
    attn_gain = jnp.clip(1.0 + 0.18 * jax.random.normal(splits[11], (D,), jnp.float32), 0.099609375, 1.8984375).astype(jnp.bfloat16)
    mlp_gain = jnp.clip(1.0 + 0.18 * jax.random.normal(splits[12], (D,), jnp.float32), 0.099609375, 1.8984375).astype(jnp.bfloat16)
    query_gain = jnp.clip(1.0 + 0.18 * jax.random.normal(splits[13], (HEAD_DIM,), jnp.float32), 0.099609375, 1.8984375).astype(jnp.bfloat16)
    key_gain = jnp.clip(1.0 + 0.18 * jax.random.normal(splits[14], (HEAD_DIM,), jnp.float32), 0.099609375, 1.8984375).astype(jnp.bfloat16)
    w_gate = scatter_about(splits[15], (EXPERTS, D, FF), D ** -0.5, 0.125, ((0, 8),))
    w_up = scatter_about(splits[16], (EXPERTS, D, FF), D ** -0.5, 0.125, ((0, 8),))
    w_down = scatter_about(splits[17], (EXPERTS, FF, D), (FF // 16) ** -0.5, 0.75, ((0, 8),))
    return dict(tokens=tokens, cotangent=cotangent, lengths=lengths, deal_order=deal_order, routes=routes, balance_coef=balance_coef, w_query=w_query, w_key=w_key, w_value=w_value, w_out=w_out, w_router=w_router, attn_gain=attn_gain, mlp_gain=mlp_gain, query_gain=query_gain, key_gain=key_gain, w_gate=w_gate, w_up=w_up, w_down=w_down)


@jax.custom_vjp
def low(v):
    return lax.optimization_barrier(v.astype(jnp.bfloat16)).astype(jnp.float32)

@jax.custom_vjp
def low_back(v):
    return v

def low_keep(v):
    return (low(v), None)

def low_pass(kept, grad):
    return (grad,)

def back_keep(v):
    return (v, None)

def back_low(kept, grad):
    return (low(grad),)
low.defvjp(low_keep, low_pass)
low_back.defvjp(back_keep, back_low)
norm_eps = 1e-06
rope_base = 50000.0
big_negative = -1e+30
highest = lax.Precision.HIGHEST

def rms_scale(values, scales):
    inverse = lax.rsqrt(lax.optimization_barrier(jnp.mean(values * values, axis=-1, keepdims=True)) + norm_eps)
    return values * inverse * scales

def rotary(values):
    half_dim = HEAD_DIM // 2
    positions = jnp.arange(TOK_DEV, dtype=jnp.int32).astype(jnp.float32)
    frequency = rope_base ** (-jnp.arange(half_dim, dtype=jnp.int32).astype(jnp.float32) * 2.0 / HEAD_DIM)
    angles = positions[:, None] * frequency[None, :]
    cosine = jnp.concatenate([jnp.cos(angles), jnp.cos(angles)], axis=-1)[:, None, :]
    sine_table = jnp.concatenate([jnp.sin(angles), jnp.sin(angles)], axis=-1)[:, None, :]
    front_half = values[..., :half_dim]
    back_half = values[..., half_dim:]
    turned = jnp.concatenate([-back_half, front_half], axis=-1)
    return values * cosine + turned * sine_table

def to_sequences(values, deal_order):
    block_rows = TOK_DEV // N_DP
    width = values.shape[-1]
    blocks = values.reshape(N_DP, N_EXPERT, N_DP, block_rows, width)
    matched = (deal_order[:, :, None] == jnp.arange(N_DP, dtype=jnp.int32)[None, None, :]).astype(jnp.int32)
    inverse_order = lax.optimization_barrier(jnp.sum(matched * jnp.arange(N_DP, dtype=jnp.int32)[None, :, None], axis=1)).astype(jnp.int32)
    index_full = jnp.broadcast_to(inverse_order[None, :, :, None, None], blocks.shape)
    taken = jnp.take_along_axis(blocks, index_full, axis=2)
    return jnp.transpose(taken, (2, 1, 0, 3, 4)).reshape(TOKENS, width)

def to_source(values, deal_order):
    block_rows = TOK_DEV // N_DP
    width = values.shape[-1]
    laid = jnp.transpose(values.reshape(N_DP, N_EXPERT, N_DP, block_rows, width), (2, 1, 0, 3, 4))
    index_full = jnp.broadcast_to(deal_order.astype(jnp.int32)[None, :, :, None, None], laid.shape)
    return jnp.take_along_axis(laid, index_full, axis=2).reshape(TOKENS, width)

def reference(tokens, cotangent, lengths, deal_order, routes, balance_coef, w_query, w_key, w_value, w_out, w_router, attn_gain, mlp_gain, query_gain, key_gain, w_gate, w_up, w_down):
    seq_tokens = to_sequences(tokens.astype(jnp.float32), deal_order)
    seq_cot = to_sequences(cotangent.astype(jnp.float32), deal_order)
    live_rows = (jnp.arange(TOK_DEV, dtype=jnp.int32)[None, :] < lengths[:, None]).astype(jnp.float32)
    live_flat = live_rows.reshape(TOKENS)
    picked = (routes[:, :, None] == jnp.arange(EXPERTS, dtype=jnp.int32)[None, None, :]).astype(jnp.int32)
    per_device = picked.reshape(SEQS, TOK_DEV * TOP, EXPERTS)
    slot_rank = lax.optimization_barrier(jnp.sum((jnp.cumsum(per_device, axis=1) - per_device) * per_device, axis=-1))
    slot_index = (slot_rank + jnp.arange(SEQS, dtype=jnp.int32)[:, None] * CAP).reshape(TOKENS * TOP).astype(jnp.int32)
    route_ids = routes.reshape(TOKENS * TOP).astype(jnp.int32)
    route_rows = jnp.arange(TOKENS * TOP, dtype=jnp.int32)
    slot_route = jnp.zeros((EXPERTS, SEQS * CAP), jnp.int32).at[route_ids, slot_index].set(route_rows)
    slot_live = jnp.zeros((EXPERTS, SEQS * CAP), jnp.float32).at[route_ids, slot_index].set(1.0)
    slot_token = slot_route // TOP
    counts = lax.optimization_barrier(jnp.sum(picked.astype(jnp.float32) * live_flat[:, None, None], axis=(0, 1)))
    valid_total = jnp.sum(live_flat)
    fraction = counts / (valid_total * TOP)
    score_scale = 1.0 / jnp.sqrt(jnp.float32(HEAD_DIM))

    def forward(inputs, query_w, key_w, value_w, out_w, router_w, attn_g, mlp_g, query_g, key_g, gate_w, up_w, down_w):
        attn_in = low(rms_scale(inputs, attn_g))
        q_lin = low_back(jnp.dot(attn_in, query_w, precision=highest)).reshape(SEQS, TOK_DEV, HEADS, HEAD_DIM)
        k_lin = low_back(jnp.dot(attn_in, key_w, precision=highest)).reshape(SEQS, TOK_DEV, HEADS, HEAD_DIM)
        v_heads = low_back(low(jnp.dot(attn_in, value_w, precision=highest))).reshape(SEQS, TOK_DEV, HEADS, HEAD_DIM)
        q_rot = low(rotary(rms_scale(q_lin, query_g)))
        k_rot = low(rotary(rms_scale(k_lin, key_g)))
        scores = low_back(jnp.einsum('sthd,suhd->shtu', q_rot, k_rot, precision=highest) * score_scale)
        masked = jnp.where(live_rows[:, None, None, :] > 0.5, scores, big_negative)
        attn_probs = low(jax.nn.softmax(masked, axis=-1))
        mixed_heads = low_back(low(jnp.einsum('shtu,suhd->sthd', attn_probs, v_heads, precision=highest))).reshape(TOKENS, HD)
        hidden = inputs + low_back(jnp.dot(mixed_heads, out_w, precision=highest))
        mlp_in = low(rms_scale(hidden, mlp_g))
        logits = low_back(jnp.dot(mlp_in, router_w, precision=highest))
        router = jax.nn.softmax(logits, axis=-1)
        chosen = jnp.take_along_axis(router, routes, axis=1)
        route_gates = (chosen / lax.optimization_barrier(jnp.sum(chosen, axis=1, keepdims=True))).reshape(TOKENS * TOP)

        def expert_step(running, expert_id):
            slot_rows = low_back(mlp_in[slot_token[expert_id]] * slot_live[expert_id][:, None])
            gate_in = low_back(jnp.dot(slot_rows, gate_w[expert_id], precision=highest))
            up_in = low_back(jnp.dot(slot_rows, up_w[expert_id], precision=highest))
            act_low = low(jax.nn.silu(gate_in) * up_in)
            result = low_back(low(jnp.dot(act_low, down_w[expert_id], precision=highest)))
            slot_weight = route_gates[slot_route[expert_id]] * slot_live[expert_id]
            return (running.at[slot_token[expert_id]].add(slot_weight[:, None] * result), None)
        expert_sum, unused = lax.scan(jax.checkpoint(expert_step), jnp.zeros((TOKENS, D), jnp.float32), jnp.arange(EXPERTS, dtype=jnp.int32))
        out_seq = live_flat[:, None] * (hidden + expert_sum)
        mean_prob = lax.optimization_barrier(jnp.sum(router * live_flat[:, None], axis=0)) / jnp.float32(TOKENS)
        balance_loss = balance_coef * (EXPERTS * jnp.sum(fraction * mean_prob))
        return (out_seq, balance_loss)
    primal, pullback = jax.vjp(forward, seq_tokens, w_query.astype(jnp.float32), w_key.astype(jnp.float32), w_value.astype(jnp.float32), w_out.astype(jnp.float32), w_router.astype(jnp.float32), attn_gain.astype(jnp.float32), mlp_gain.astype(jnp.float32), query_gain.astype(jnp.float32), key_gain.astype(jnp.float32), w_gate.astype(jnp.float32), w_up.astype(jnp.float32), w_down.astype(jnp.float32))
    grads = pullback((seq_cot, jnp.ones((1,), jnp.float32)))
    output = to_source(primal[0], deal_order).astype(jnp.bfloat16)
    grad_input = to_source(grads[0], deal_order)
    return (output, primal[1], grad_input, grads[1], grads[2], grads[3], grads[4], grads[5], grads[6], grads[7], grads[8], grads[9], grads[10], grads[11], grads[12])
```

```python
import math

import jax
import jax.numpy as jnp
from jax import lax
from jax.sharding import PartitionSpec as P

norm_eps = 1e-06
rope_base = 50000.0
big_negative = -1e30
bf16 = jnp.bfloat16
f32 = jnp.float32


def norm_fwd(values, scales):
    inverse = lax.rsqrt(jnp.mean(values * values, axis=-1, keepdims=True) + norm_eps)
    return (values * inverse * scales, inverse)


def norm_back(values, inverse, scales, grad_out, sum_axes):
    scaled = grad_out * scales
    grad_in = inverse * (
        scaled - values * inverse * inverse * jnp.mean(scaled * values, axis=-1, keepdims=True)
    )
    grad_scale = jnp.sum(grad_out * values * inverse, axis=sum_axes)
    return (grad_in, grad_scale)


def rotary_tables(tok_rows, head_dim):
    half_dim = head_dim // 2
    positions = jnp.arange(tok_rows, dtype=jnp.int32).astype(f32)
    frequency = rope_base ** (-jnp.arange(half_dim, dtype=jnp.int32).astype(f32) * 2.0 / head_dim)
    angles = positions[:, None] * frequency[None, :]
    cosine = jnp.concatenate([jnp.cos(angles), jnp.cos(angles)], axis=-1)[:, None, :]
    sine_table = jnp.concatenate([jnp.sin(angles), jnp.sin(angles)], axis=-1)[:, None, :]
    return (cosine, sine_table)


def turn_half(values):
    half_dim = values.shape[-1] // 2
    return jnp.concatenate([-values[..., half_dim:], values[..., :half_dim]], axis=-1)


def rotary(values, cosine, sine_table):
    return values * cosine + turn_half(values) * sine_table


def rotary_back(grad_out, cosine, sine_table):
    return grad_out * cosine - turn_half(grad_out * sine_table)


def einf(spec, left, right):
    return jnp.einsum(spec, left, right, preferred_element_type=f32)


def body(
    tokens,
    cotangent,
    lengths,
    deal_order,
    routes,
    balance_coef,
    w_query,
    w_key,
    w_value,
    w_out,
    w_router,
    attn_gain,
    mlp_gain,
    query_gain,
    key_gain,
    w_gate,
    w_up,
    w_down,
):
    groups = lax.axis_size("expert")
    replicas = lax.axis_size("dp")
    me = lax.axis_index("expert")
    tok_rows, width = tokens.shape
    block_rows = tok_rows // replicas
    total_slots = float(tok_rows * replicas * groups)
    shard_rows = w_query.shape[0]
    local_experts = w_gate.shape[0]
    experts = local_experts * groups
    top_k = routes.shape[1]
    capacity = tok_rows * top_k * 9 // (8 * experts)

    order_row = lax.dynamic_index_in_dim(deal_order, me, 0, keepdims=False)
    dp_ids = jnp.arange(replicas, dtype=jnp.int32)
    matched = (order_row[:, None] == dp_ids[None, :]).astype(jnp.int32)
    inverse_order = jnp.sum(matched * dp_ids[:, None], axis=0)

    def deal(values):
        blocks = values.reshape(replicas, block_rows, width)[inverse_order]
        return lax.all_to_all(blocks, "dp", split_axis=0, concat_axis=0, tiled=True).reshape(
            tok_rows, width
        )

    def undeal(values):
        back = lax.all_to_all(
            values.reshape(replicas, block_rows, width), "dp", split_axis=0, concat_axis=0, tiled=True
        )
        return back[order_row].reshape(tok_rows, width)

    seq_tokens = deal(tokens)
    seq_cot = deal(cotangent)

    small = jnp.concatenate(
        [w_router.reshape(-1), attn_gain, mlp_gain, query_gain, key_gain]
    )
    small_all = lax.all_gather(small, "expert", axis=0, tiled=False)
    n_router = shard_rows * experts
    cuts = [0, n_router]
    for gain in (attn_gain, mlp_gain, query_gain, key_gain):
        cuts.append(cuts[-1] + gain.shape[0])
    router_full = small_all[:, :n_router].reshape(width, experts)
    attn_g, mlp_g, query_g, key_g = (
        small_all[:, cuts[i] : cuts[i + 1]].reshape(-1).astype(f32) for i in range(1, 5)
    )
    head_dim = query_g.shape[0]
    local_width = w_query.shape[1] // groups
    local_heads = local_width // head_dim
    score_scale = 1.0 / math.sqrt(head_dim)

    ints = jnp.concatenate([routes.reshape(-1), jnp.broadcast_to(lengths, (top_k,))])
    ints_all = lax.all_gather(ints, "expert", axis=0, tiled=False)
    routes_all = ints_all[:, : tok_rows * top_k].reshape(groups, tok_rows, top_k)
    lengths_all = ints_all[:, tok_rows * top_k]
    positions = jnp.arange(tok_rows, dtype=jnp.int32)
    live_all = (positions[None, :] < lengths_all[:, None]).astype(f32)
    live_rows = (positions < lengths[0]).astype(f32)

    def columns(weight):
        return weight.reshape(shard_rows, groups, local_width).transpose(1, 0, 2)

    w_send = jnp.concatenate([columns(w_query), columns(w_key), columns(w_value)], axis=2)
    w_qkv = lax.all_to_all(w_send, "expert", split_axis=0, concat_axis=0, tiled=True).reshape(
        width, 3 * local_width
    )
    wo_full = lax.all_gather(w_out, "expert", axis=0, tiled=True)

    inputs = seq_tokens.astype(f32)
    normed, inv_first = norm_fwd(inputs, attn_g)
    attn_in = normed.astype(bf16)
    attn_all = lax.all_gather(attn_in, "expert", axis=0, tiled=True)
    grad_output = seq_cot.astype(f32) * live_rows[:, None]
    cot_all = lax.all_gather(grad_output.astype(bf16), "expert", axis=0, tiled=False)

    qkv = jnp.dot(attn_all, w_qkv, preferred_element_type=f32)
    heads_shape = (groups, tok_rows, local_heads, head_dim)
    q_lin = qkv[:, :local_width].reshape(heads_shape)
    k_lin = qkv[:, local_width : 2 * local_width].reshape(heads_shape)
    v_heads = qkv[:, 2 * local_width :].astype(bf16).reshape(heads_shape)
    cosine, sine_table = rotary_tables(tok_rows, head_dim)
    q_normed, q_inverse = norm_fwd(q_lin, query_g)
    k_normed, k_inverse = norm_fwd(k_lin, key_g)
    q_rot = rotary(q_normed, cosine, sine_table).astype(bf16)
    k_rot = rotary(k_normed, cosine, sine_table).astype(bf16)
    scores = einf("sthd,suhd->shtu", q_rot, k_rot) * score_scale
    masked = jnp.where(live_all[:, None, None, :] > 0.5, scores, big_negative)
    row_max = jnp.max(masked, axis=-1, keepdims=True)
    raised = jnp.exp(masked - row_max)
    attn_probs = raised / jnp.sum(raised, axis=-1, keepdims=True)
    probs_low = attn_probs.astype(bf16)
    mixed = (
        einf("shtu,suhd->sthd", probs_low, v_heads).astype(bf16).reshape(groups, tok_rows, local_width)
    )
    mixed_here = lax.all_to_all(mixed, "expert", split_axis=0, concat_axis=0, tiled=True)
    hidden = inputs + einf("xtm,xmd->td", mixed_here, wo_full.reshape(groups, local_width, width))
    mlp_normed, inv_second = norm_fwd(hidden, mlp_g)
    mlp_in = mlp_normed.astype(bf16)
    mlp_all = lax.all_gather(mlp_in, "expert", axis=0, tiled=False)

    logits = einf("std,de->ste", mlp_all, router_full)
    router = jax.nn.softmax(logits, axis=-1)
    expert_ids = jnp.arange(experts, dtype=jnp.int32)
    picked = jnp.sum(
        (routes_all[:, :, :, None] == expert_ids).astype(f32), axis=2
    )
    chosen_sum = jnp.sum(picked * router, axis=-1, keepdims=True)
    gates = picked * router / chosen_sum
    counts = jnp.sum(picked * live_all[:, :, None], axis=(0, 1))
    prob_sums = jnp.sum(router * live_all[:, :, None], axis=(0, 1))
    live_count = jnp.sum(live_all)[None]
    sums = lax.psum(jnp.concatenate([counts, prob_sums, live_count]), "dp")
    counts, prob_sums, live_count = sums[:experts], sums[experts : 2 * experts], sums[2 * experts :]
    fraction = counts / (live_count * top_k)
    balance_loss = balance_coef * (experts * jnp.sum(fraction * prob_sums / total_slots))

    first = me * local_experts
    own_picked = lax.dynamic_slice_in_dim(picked, first, local_experts, 2)
    own_gates = lax.dynamic_slice_in_dim(gates, first, local_experts, 2)
    before = (positions[:, None] > positions[None, :]).astype(bf16)
    rank = einf("tu,suj->jst", before, own_picked.astype(bf16))
    own_picked = own_picked.transpose(2, 0, 1)
    own_gates = own_gates.transpose(2, 0, 1)
    slot_of = jnp.where(own_picked > 0.5, rank.astype(jnp.int32), -1)
    slot_ids = jnp.arange(capacity, dtype=jnp.int32)
    is_slot = slot_of[:, :, None, :] == slot_ids[None, None, :, None]
    one_hot = is_slot.astype(bf16)
    slot_gate = jnp.sum(jnp.where(is_slot, own_gates[:, :, None, :], 0.0), axis=-1)
    n_slots = groups * capacity

    expert_in = einf("jsct,std->jscd", one_hot, mlp_all).astype(bf16).reshape(
        local_experts, n_slots, width
    )
    gate_in = einf("jrd,jdf->jrf", expert_in, w_gate)
    up_in = einf("jrd,jdf->jrf", expert_in, w_up)
    sigmoid_gate = jax.nn.sigmoid(gate_in)
    activated = gate_in * sigmoid_gate
    act_low = (activated * up_in).astype(bf16)
    cot_slots = einf("jsct,std->jscd", one_hot, cot_all).astype(bf16)
    grad_recv = (
        (slot_gate[..., None] * cot_slots.astype(f32)).astype(bf16).reshape(local_experts, n_slots, width)
    )
    grad_down_w = einf("jrf,jrd->jfd", act_low, grad_recv)
    total_down = lax.psum_scatter(
        grad_down_w.astype(bf16), "dp", scatter_dimension=1, tiled=True
    ).astype(f32)

    expert_out = einf("jrf,jfd->jrd", act_low, w_down).astype(bf16).reshape(
        local_experts, groups, capacity, width
    )
    grad_gate_slot = jnp.sum(cot_slots.astype(f32) * expert_out.astype(f32), axis=-1)
    own_grad_gates = jnp.sum(jnp.where(is_slot, grad_gate_slot[..., None], 0.0), axis=2)
    weighted = (slot_gate[..., None] * expert_out.astype(f32)).astype(bf16)
    sum_part = einf("jsct,jscd->std", one_hot, weighted).astype(bf16)

    grad_act = einf("jrd,jfd->jrf", grad_recv, w_down)
    grad_up_in = (grad_act * activated).astype(bf16)
    grad_gate_in = (
        grad_act * up_in * sigmoid_gate * (1.0 + gate_in * (1.0 - sigmoid_gate))
    ).astype(bf16)
    grad_rows = (
        (einf("jrf,jdf->jrd", grad_gate_in, w_gate) + einf("jrf,jdf->jrd", grad_up_in, w_up))
        .astype(bf16)
        .reshape(local_experts, groups, capacity, width)
    )
    grad_part = einf("jsct,jscd->std", one_hot, grad_rows).astype(bf16)
    grad_mlp_in = lax.psum_scatter(grad_part, "expert", scatter_dimension=0, tiled=True).astype(f32)
    grad_mlp_in = grad_mlp_in.reshape(tok_rows, width)

    grad_gate_w = einf("jrd,jrf->jdf", expert_in, grad_gate_in)
    grad_up_w = einf("jrd,jrf->jdf", expert_in, grad_up_in)
    total_gate, total_up = (
        lax.psum_scatter(value.astype(bf16), "dp", scatter_dimension=1, tiled=True).astype(f32)
        for value in (grad_gate_w, grad_up_w)
    )

    gate_back = lax.all_to_all(
        own_grad_gates.transpose(1, 0, 2), "expert", split_axis=0, concat_axis=0, tiled=True
    )
    grad_gates = gate_back.reshape(experts, tok_rows).T
    my_router = lax.dynamic_index_in_dim(router, me, 0, keepdims=False)
    my_picked = lax.dynamic_index_in_dim(picked, me, 0, keepdims=False)
    my_gates = lax.dynamic_index_in_dim(gates, me, 0, keepdims=False)
    my_sum = lax.dynamic_index_in_dim(chosen_sum, me, 0, keepdims=False)
    grad_prob = (
        my_picked * (grad_gates - jnp.sum(grad_gates * my_gates, axis=1, keepdims=True)) / my_sum
        + live_rows[:, None] * (balance_coef * experts / total_slots) * fraction[None, :]
    )
    grad_logits = (
        my_router * (grad_prob - jnp.sum(my_router * grad_prob, axis=-1, keepdims=True))
    ).astype(bf16)
    grad_router_w = einf("td,te->de", mlp_in, grad_logits)
    grad_mlp_in = grad_mlp_in + einf("te,de->td", grad_logits, router_full)

    grad_hidden_norm, grad_mlp_g = norm_back(hidden, inv_second, mlp_g, grad_mlp_in, 0)
    grad_hidden = grad_output + grad_hidden_norm
    grad_hidden_low = grad_hidden.astype(bf16)
    hidden_all = lax.all_gather(grad_hidden_low, "expert", axis=0, tiled=True)

    grad_out_w = einf("rm,rd->md", mixed.reshape(groups * tok_rows, local_width), hidden_all)
    grad_mixed = einf("rd,md->rm", hidden_all, w_out).astype(bf16).reshape(heads_shape)
    grad_probs = einf("sthd,suhd->shtu", grad_mixed, v_heads)
    grad_scores = (
        attn_probs * (grad_probs - jnp.sum(attn_probs * grad_probs, axis=-1, keepdims=True))
    ).astype(bf16)
    grad_q_rot = einf("shtu,suhd->sthd", grad_scores, k_rot) * score_scale
    grad_k_rot = einf("shtu,sthd->suhd", grad_scores, q_rot) * score_scale
    grad_values = einf("shtu,sthd->suhd", probs_low, grad_mixed).astype(bf16)
    grad_q_lin, grad_query_g = norm_back(
        q_lin, q_inverse, query_g, rotary_back(grad_q_rot, cosine, sine_table), (0, 1, 2)
    )
    grad_k_lin, grad_key_g = norm_back(
        k_lin, k_inverse, key_g, rotary_back(grad_k_rot, cosine, sine_table), (0, 1, 2)
    )
    flat = (groups * tok_rows, local_width)
    grad_qkv = jnp.concatenate(
        [
            grad_q_lin.astype(bf16).reshape(flat),
            grad_k_lin.astype(bf16).reshape(flat),
            grad_values.reshape(flat),
        ],
        axis=1,
    )
    grad_attn_part = einf("rm,dm->rd", grad_qkv, w_qkv).astype(bf16)
    grad_attn_in = lax.psum_scatter(
        grad_attn_part, "expert", scatter_dimension=0, tiled=True
    ).astype(f32)
    grad_qkv_w = einf("rd,rm->dm", attn_all, grad_qkv).astype(bf16)
    w_back = lax.all_to_all(
        grad_qkv_w.reshape(groups, shard_rows, 3 * local_width),
        "expert",
        split_axis=0,
        concat_axis=0,
        tiled=True,
    )
    attn_w = jnp.concatenate(
        [
            w_back[:, :, i * local_width : (i + 1) * local_width]
            .transpose(1, 0, 2)
            .reshape(shard_rows, groups * local_width)
            for i in range(3)
        ]
        + [grad_out_w.astype(bf16)],
        axis=0,
    )
    attn_sum = lax.psum(attn_w, "dp").astype(f32)
    sum_q, sum_k, sum_v, sum_o = (
        attn_sum[i * shard_rows : (i + 1) * shard_rows] for i in range(4)
    )

    grad_input_norm, grad_attn_g = norm_back(inputs, inv_first, attn_g, grad_attn_in, 0)
    grad_input = undeal((grad_hidden + grad_input_norm).astype(bf16)).astype(f32)

    expert_sum = lax.psum_scatter(sum_part, "expert", scatter_dimension=0, tiled=True)
    expert_sum = expert_sum.reshape(tok_rows, width).astype(f32)
    output = undeal((live_rows[:, None] * (hidden + expert_sum)).astype(bf16))

    pieces = [grad_router_w.astype(bf16).reshape(groups, n_router)] + [
        value.astype(bf16).reshape(groups, -1)
        for value in (grad_attn_g, grad_mlp_g, grad_query_g, grad_key_g)
    ]
    part_small = lax.psum_scatter(
        jnp.concatenate(pieces, axis=1), "expert", scatter_dimension=0, tiled=True
    )
    sum_small = lax.psum(part_small.reshape(-1), "dp").astype(f32)
    sum_r = sum_small[:n_router].reshape(shard_rows, experts)
    sum_ga, sum_gm, sum_gq, sum_gk = (sum_small[cuts[i] : cuts[i + 1]] for i in range(1, 5))
    return (
        output,
        balance_loss,
        grad_input,
        sum_q,
        sum_k,
        sum_v,
        sum_o,
        sum_r,
        sum_ga,
        sum_gm,
        sum_gq,
        sum_gk,
        total_gate,
        total_up,
        total_down,
    )


def solution(mesh):
    rows = P(("dp", "expert"), None)
    weight = P("expert", None)
    gain = P("expert")
    cube = P("expert", None, None)
    cube_out = P("expert", "dp", None)
    return jax.shard_map(
        body,
        mesh=mesh,
        in_specs=(
            (rows, rows, P(("dp", "expert")), P(), rows, P())
            + (weight,) * 5
            + (gain,) * 4
            + (cube,) * 3
        ),
        out_specs=(
            (rows, P(), rows) + (weight,) * 5 + (gain,) * 4 + (cube_out,) * 3
        ),
        check_vma=False,
    )
```

```python
import functools
import math

import jax
import jax.numpy as jnp
from jax import lax
from jax.experimental import pallas as pl
from jax.experimental.pallas import tpu as pltpu
from jax.sharding import PartitionSpec as P

norm_eps = 1e-06
rope_base = 50000.0
big_negative = -1e30
bf16 = jnp.bfloat16
f32 = jnp.float32
MESH = pl.DeviceIdType.MESH
DMA = pltpu.SemaphoreType.DMA


def norm_fwd(values, scales):
    inverse = lax.rsqrt(jnp.mean(values * values, axis=-1, keepdims=True) + norm_eps)
    return (values * inverse * scales, inverse)


def norm_back(values, inverse, scales, grad_out, sum_axes):
    scaled = grad_out * scales
    grad_in = inverse * (
        scaled - values * inverse * inverse * jnp.mean(scaled * values, axis=-1, keepdims=True)
    )
    grad_scale = jnp.sum(grad_out * values * inverse, axis=sum_axes)
    return (grad_in, grad_scale)


def rotary_tables(tok_rows, head_dim):
    half_dim = head_dim // 2
    positions = jnp.arange(tok_rows, dtype=jnp.int32).astype(f32)
    frequency = rope_base ** (-jnp.arange(half_dim, dtype=jnp.int32).astype(f32) * 2.0 / head_dim)
    angles = positions[:, None] * frequency[None, :]
    cosine = jnp.concatenate([jnp.cos(angles), jnp.cos(angles)], axis=-1)
    signed_sine = jnp.concatenate([-jnp.sin(angles), jnp.sin(angles)], axis=-1)
    return (cosine, signed_sine)


def peer(index):
    return {"expert": index}


def remote(src, dst, send, recv, to):
    return pltpu.make_async_remote_copy(
        src_ref=src, dst_ref=dst, send_sem=send, recv_sem=recv, device_id=peer(to), device_id_type=MESH
    )


def greet(n, me):
    barrier = pltpu.get_barrier_semaphore()
    for k in range(1, n):
        pl.semaphore_signal(
            barrier, inc=1, device_id=peer(lax.rem(me + k, n)), device_id_type=MESH
        )
    pl.semaphore_wait(barrier, n - 1)


def quad_places(me):
    core = lax.rem(me, 2)
    chip = me // 2
    x = lax.rem(chip, 2)
    y = chip // 2

    def at(px, py, pc):
        return (py * 2 + px) * 2 + pc

    spots = ((x, y), (1 - x, y), (x, 1 - y), (1 - x, 1 - y))
    return [at(px, py, core) for px, py in spots], [at(px, py, 1 - core) for px, py in spots]


def any_places(n, me):
    core = lax.rem(me, 2)
    chip = me // 2
    chips = n // 2
    chip_of = [lax.rem(chip + k, chips) for k in range(chips)]
    chip_from = [lax.rem(chip - k + chips, chips) for k in range(chips)]
    return (
        [c * 2 + core for c in chip_of],
        [c * 2 + 1 - core for c in chip_of],
        [c * 2 + core for c in chip_from],
        [c * 2 + 1 - core for c in chip_from],
    )


def small_kernel(n, *refs):
    ins, outs, (send_sem, recv_sem) = refs[: len(refs) // 2 - 1], refs[len(refs) // 2 - 1 : -2], refs[-2:]
    me = lax.axis_index("expert")
    for src, out in zip(ins, outs):
        out[me] = src[...]
    greet(n, me)
    copies = []
    for k in range(1, n):
        for i, (src, out) in enumerate(zip(ins, outs)):
            copy = remote(
                src, out.at[me], send_sem.at[i, k], recv_sem.at[i, k], lax.rem(me + k, n)
            )
            copy.start()
            copies.append(copy)
    for copy in copies:
        copy.wait()


def gather_small(n, collective_id, *values):
    vmem = pl.BlockSpec(memory_space=pltpu.VMEM)
    return pl.pallas_call(
        functools.partial(small_kernel, n),
        out_shape=[jax.ShapeDtypeStruct((n,) + v.shape, v.dtype) for v in values],
        in_specs=[vmem] * len(values),
        out_specs=[vmem] * len(values),
        scratch_shapes=[DMA((len(values), n)), DMA((len(values), n))],
        compiler_params=pltpu.CompilerParams(collective_id=collective_id, has_side_effects=True),
        name="gather_small",
    )(*values)


def quad_gather_kernel(parts, x_ref, o_ref, own_sem, send_sem, recv_sem, pass_sem, pair_send, pair_recv):
    me = lax.axis_index("expert")
    same, other = quad_places(me)
    step = x_ref.shape[0] // parts
    half = parts // 2
    own = pltpu.make_async_copy(x_ref, o_ref.at[me], own_sem)
    own.start()
    greet(8, me)
    started = []

    def go(copy):
        copy.start()
        started.append(copy)

    def piece(p):
        return pl.ds(p * step, step)

    low, high = list(range(half)), list(range(half, parts))
    turns = [(k, seq[i]) for i in range(parts) for k, seq in ((1, high + low), (2, low + high))]
    for k, p in turns:
        go(remote(x_ref.at[piece(p)], o_ref.at[me, piece(p)], send_sem.at[k, p], recv_sem.at[k, p], same[k]))
    for p in range(parts):
        go(remote(x_ref.at[piece(p)], o_ref.at[me, piece(p)], pair_send.at[0, p], pair_recv.at[0, p], other[0]))

    def arrive(k, p):
        block = o_ref.at[same[k], piece(p)]
        remote(block, block, send_sem.at[k, p], recv_sem.at[k, p], other[0]).wait_recv()
        return block

    for k, p in turns:
        block = arrive(k, p)
        if (p >= half) == (k == 1):
            go(remote(block, block, pass_sem.at[p], recv_sem.at[3, p], same[3 - k]))
        go(remote(block, block, pair_send.at[k, p], pair_recv.at[k, p], other[0]))
    for pair in zip(low, high):
        for p in pair:
            block = arrive(3, p)
            go(remote(block, block, pair_send.at[3, p], pair_recv.at[3, p], other[0]))
    for k in range(4):
        for p in range(parts):
            block = o_ref.at[other[k], piece(p)]
            remote(block, block, pair_send.at[k, p], pair_recv.at[k, p], other[0]).wait_recv()
    for copy in started:
        copy.wait_send()
    own.wait()


def any_gather_kernel(n, x_ref, o_ref, own_sem, send_sem, recv_sem, pair_send, pair_recv):
    me = lax.axis_index("expert")
    same, other, same_from, other_from = any_places(n, me)
    own = pltpu.make_async_copy(x_ref, o_ref.at[me], own_sem)
    own.start()
    greet(n, me)
    started = []
    for k in range(n // 2):
        if k:
            copy = remote(x_ref, o_ref.at[me], send_sem.at[k], recv_sem.at[k], same[k])
        else:
            copy = remote(x_ref, o_ref.at[me], pair_send.at[0], pair_recv.at[0], other[0])
        copy.start()
        started.append(copy)
    for k in range(1, n // 2):
        block = o_ref.at[same_from[k]]
        remote(block, block, send_sem.at[k], recv_sem.at[k], other[0]).wait_recv()
        copy = remote(block, block, pair_send.at[k], pair_recv.at[k], other[0])
        copy.start()
        started.append(copy)
    for k in range(n // 2):
        block = o_ref.at[other_from[k]]
        remote(block, block, pair_send.at[k], pair_recv.at[k], other[0]).wait_recv()
    for copy in started:
        copy.wait_send()
    own.wait()


def gather_rows(x, n, collective_id, parts=4):
    chips = n // 2
    if n == 8:
        kernel = functools.partial(quad_gather_kernel, parts)
        sems = [DMA, DMA((4, parts)), DMA((4, parts)), DMA((parts,)), DMA((4, parts)), DMA((4, parts))]
    else:
        kernel = functools.partial(any_gather_kernel, n)
        sems = [DMA, DMA((chips,)), DMA((chips,)), DMA((chips,)), DMA((chips,))]
    return pl.pallas_call(
        kernel,
        out_shape=jax.ShapeDtypeStruct((n,) + x.shape, x.dtype),
        in_specs=[pl.BlockSpec(memory_space=pl.ANY)],
        out_specs=pl.BlockSpec(memory_space=pl.ANY),
        scratch_shapes=sems,
        compiler_params=pltpu.CompilerParams(collective_id=collective_id, has_side_effects=True),
        cost_estimate=pl.CostEstimate(flops=0, transcendentals=0, bytes_accessed=n * x.size * 16),
        name=f"gather_rows_{collective_id}",
    )(x)


def add_rows(total, first, rows, chunk, *terms):
    @pl.loop(0, rows // chunk)
    def _(i):
        s = pl.ds(first + i * chunk, chunk)
        value = terms[0][s].astype(f32)
        for term in terms[1:]:
            value = value + term[s].astype(f32)
        total[s] = value.astype(total.dtype)


def quad_scatter_kernel(
    parts, p_ref, o_ref, mine, theirs, transit, got, load_sem, pair_send, pair_recv, over_send, over_recv, send_sem, recv_sem
):
    me = lax.axis_index("expert")
    same, other = quad_places(me)
    step = p_ref.shape[1] // parts
    half = parts // 2
    low, high = list(range(half)), list(range(half, parts))
    mix = [p for pair in zip(low, high) for p in pair]
    order = (3, 1, 2, 0)

    def piece(p):
        return pl.ds(p * step, step)

    loads = {}
    for k in order:
        for p in mix:
            loads[k, p] = pltpu.make_async_copy(
                p_ref.at[same[k], piece(p)], mine.at[k, piece(p)], load_sem.at[k, p]
            )
            loads[k, p].start()
    greet(8, me)
    started = []

    def go(copy):
        copy.start()
        started.append(copy)

    for k in order:
        for p in mix:
            go(
                remote(
                    p_ref.at[other[k], piece(p)],
                    theirs.at[k, piece(p)],
                    pair_send.at[k, p],
                    pair_recv.at[k, p],
                    other[0],
                )
            )

    def fold(k, p):
        loads[k, p].wait()
        spot = theirs.at[k, piece(p)]
        remote(spot, spot, pair_send.at[k, p], pair_recv.at[k, p], other[0]).wait_recv()
        add_rows(mine.at[k], p * step, step, 32, mine.at[k], theirs.at[k])

    def ship(k, p):
        go(
            remote(
                mine.at[k, piece(p)],
                got.at[k - 1, piece(p)],
                send_sem.at[k - 1, p],
                recv_sem.at[k - 1, p],
                same[k],
            )
        )

    for p in mix:
        fold(3, p)
        to = same[1] if p < half else same[2]
        go(remote(mine.at[3, piece(p)], transit.at[piece(p)], over_send.at[p], over_recv.at[p], to))
    for a, b in zip(low, high):
        for k, p in ((1, a), (2, b)):
            fold(k, p)
            ship(k, p)
    for a, b in zip(low, high):
        for k, p in ((2, a), (1, b)):
            fold(k, p)
            spot = transit.at[piece(p)]
            remote(spot, spot, over_send.at[p], over_recv.at[p], other[0]).wait_recv()
            add_rows(mine.at[k], p * step, step, 32, mine.at[k], transit)
            ship(k, p)
    for p in mix:
        fold(0, p)
    for p in mix:
        for k in (0, 1):
            spot = got.at[k, piece(p)]
            remote(spot, spot, send_sem.at[k, p], recv_sem.at[k, p], other[0]).wait_recv()
        add_rows(o_ref, p * step, step, 32, mine.at[0], got.at[0], got.at[1])
    for copy in started:
        copy.wait_send()


def any_scatter_kernel(n, p_ref, o_ref, mine, theirs, got, load_sem, pair_send, pair_recv, send_sem, recv_sem):
    me = lax.axis_index("expert")
    same, other, _, _ = any_places(n, me)
    rows = p_ref.shape[1]
    order = list(range(1, n // 2)) + [0]
    loads = {}
    for k in order:
        loads[k] = pltpu.make_async_copy(p_ref.at[same[k]], mine.at[k], load_sem.at[k])
        loads[k].start()
    greet(n, me)
    started = []
    for k in order:
        copy = remote(p_ref.at[other[k]], theirs.at[k], pair_send.at[k], pair_recv.at[k], other[0])
        copy.start()
        started.append(copy)
    for k in order:
        loads[k].wait()
        remote(theirs.at[k], theirs.at[k], pair_send.at[k], pair_recv.at[k], other[0]).wait_recv()
        add_rows(mine.at[k], 0, rows, 32, mine.at[k], theirs.at[k])
        if k:
            copy = remote(mine.at[k], got.at[k], send_sem.at[k], recv_sem.at[k], same[k])
            copy.start()
            started.append(copy)
    for k in range(1, n // 2):
        remote(got.at[k], got.at[k], send_sem.at[k], recv_sem.at[k], other[0]).wait_recv()
    add_rows(o_ref, 0, rows, 32, mine.at[0], *[got.at[k] for k in range(1, n // 2)])
    for copy in started:
        copy.wait_send()


def scatter_sum(x, n, collective_id, parts=4):
    chips = n // 2
    shape = x.shape[1:]
    blocks = pltpu.VMEM((chips,) + shape, bf16)
    if n == 8:
        kernel = functools.partial(quad_scatter_kernel, parts)
        scratch = [blocks, blocks, pltpu.VMEM(shape, bf16), pltpu.VMEM((2,) + shape, bf16)]
        scratch += [DMA((4, parts))] * 3 + [DMA((parts,))] * 2 + [DMA((2, parts))] * 2
    else:
        kernel = functools.partial(any_scatter_kernel, n)
        scratch = [blocks] * 3 + [DMA((chips,))] * 5
    return pl.pallas_call(
        kernel,
        out_shape=jax.ShapeDtypeStruct(shape, f32),
        in_specs=[pl.BlockSpec(memory_space=pl.ANY)],
        out_specs=pl.BlockSpec(memory_space=pltpu.VMEM),
        scratch_shapes=scratch,
        compiler_params=pltpu.CompilerParams(
            collective_id=collective_id, has_side_effects=True, vmem_limit_bytes=(3 * chips + 12) << 20
        ),
        cost_estimate=pl.CostEstimate(flops=0, transcendentals=0, bytes_accessed=x.size * 16),
        name=f"scatter_sum_{collective_id}",
    )(x)


def dot(left, right, left_dim=1, right_dim=0):
    return lax.dot_general(
        left, right, (((left_dim,), (right_dim,)), ((), ())), preferred_element_type=f32
    )


def head_values(lin, gain, cosine, signed_sine):
    inverse = lax.rsqrt(jnp.mean(lin * lin, axis=-1, keepdims=True) + norm_eps)
    normed = lin * inverse * gain
    half = lin.shape[1] // 2
    turned = normed * cosine + pltpu.roll(normed, half, 1) * signed_sine
    return inverse, turned.astype(bf16)


def head_probs(q_rot, k_rot, length, score_scale):
    scores = dot(q_rot, k_rot, 1, 1) * score_scale
    key = lax.broadcasted_iota(jnp.int32, scores.shape, 1)
    masked = jnp.where(key < length, scores, big_negative)
    raised = jnp.exp(masked - jnp.max(masked, axis=-1, keepdims=True))
    return raised / jnp.sum(raised, axis=-1, keepdims=True)


def attend_kernel(heads, head_dim, lengths_ref, x_ref, w_ref, qg_ref, kg_ref, cos_ref, sin_ref, mixed_ref):
    length = lengths_ref[pl.program_id(0)]
    wide = heads * head_dim
    qkv = dot(x_ref[0], w_ref[...])
    for h in range(heads):
        at = h * head_dim
        _, q_rot = head_values(qkv[:, at : at + head_dim], qg_ref[...], cos_ref[...], sin_ref[...])
        _, k_rot = head_values(
            qkv[:, wide + at : wide + at + head_dim], kg_ref[...], cos_ref[...], sin_ref[...]
        )
        v = qkv[:, 2 * wide + at : 2 * wide + at + head_dim].astype(bf16)
        probs = head_probs(q_rot, k_rot, length, 1.0 / math.sqrt(head_dim))
        mixed_ref[0, :, at : at + head_dim] = dot(probs.astype(bf16), v).astype(bf16)


def attend(lengths, x, w_qkv, query_g, key_g, cosine, signed_sine):
    seqs, rows, width = x.shape
    head_dim = query_g.shape[0]
    wide = w_qkv.shape[1] // 3
    whole = lambda s, lens: (0, 0)
    table = pl.BlockSpec((rows, head_dim), whole)
    gain = pl.BlockSpec((1, head_dim), whole)
    return pl.pallas_call(
        functools.partial(attend_kernel, wide // head_dim, head_dim),
        out_shape=jax.ShapeDtypeStruct((seqs, rows, wide), bf16),
        grid_spec=pltpu.PrefetchScalarGridSpec(
            num_scalar_prefetch=1,
            grid=(seqs,),
            in_specs=[
                pl.BlockSpec((1, rows, width), lambda s, lens: (s, 0, 0)),
                pl.BlockSpec((width, 3 * wide), whole),
                gain,
                gain,
                table,
                table,
            ],
            out_specs=pl.BlockSpec((1, rows, wide), lambda s, lens: (s, 0, 0)),
        ),
        compiler_params=pltpu.CompilerParams(vmem_limit_bytes=32 << 20),
        cost_estimate=pl.CostEstimate(
            flops=2 * seqs * rows * (width * 3 * wide + 2 * rows * wide),
            transcendentals=seqs * rows * rows * wide // head_dim,
            bytes_accessed=2 * (x.size + w_qkv.size),
        ),
        name="attend",
    )(lengths, x, w_qkv, query_g[None, :], key_g[None, :], cosine, signed_sine)


def attend_back_kernel(
    heads,
    head_dim,
    lengths_ref,
    x_ref,
    g_ref,
    mixed_ref,
    w_ref,
    wo_ref,
    qg_ref,
    kg_ref,
    cos_ref,
    sin_ref,
    part_ref,
    dw_ref,
    dwo_ref,
    dgain_ref,
    dw_acc,
    dwo_acc,
    gain_acc,
    gqkv_ref,
):
    step = pl.program_id(0)
    length = lengths_ref[step]
    wide = heads * head_dim
    scale = 1.0 / math.sqrt(head_dim)
    cosine, signed_sine = cos_ref[...], sin_ref[...]

    @pl.when(step == 0)
    def _():
        dw_acc[...] = jnp.zeros_like(dw_acc)
        dwo_acc[...] = jnp.zeros_like(dwo_acc)
        gain_acc[...] = jnp.zeros_like(gain_acc)

    qkv = dot(x_ref[0], w_ref[...])
    g_mixed = dot(g_ref[0], wo_ref[...], 1, 1).astype(bf16)
    dwo_acc[...] += dot(mixed_ref[0], g_ref[0], 0, 0)
    for h in range(heads):
        at = h * head_dim
        q_lin = qkv[:, at : at + head_dim]
        k_lin = qkv[:, wide + at : wide + at + head_dim]
        v = qkv[:, 2 * wide + at : 2 * wide + at + head_dim].astype(bf16)
        q_inv, q_rot = head_values(q_lin, qg_ref[...], cosine, signed_sine)
        k_inv, k_rot = head_values(k_lin, kg_ref[...], cosine, signed_sine)
        probs = head_probs(q_rot, k_rot, length, scale)
        gm = g_mixed[:, at : at + head_dim]
        g_probs = dot(gm, v, 1, 1)
        g_scores = (probs * (g_probs - jnp.sum(probs * g_probs, axis=-1, keepdims=True))).astype(bf16)
        g_v = dot(probs.astype(bf16), gm, 0, 0)
        for i, (g_rot, lin, inv, gain) in enumerate(
            (
                (dot(g_scores, k_rot) * scale, q_lin, q_inv, qg_ref[...]),
                (dot(g_scores, q_rot, 0, 0) * scale, k_lin, k_inv, kg_ref[...]),
            )
        ):
            w = g_rot * cosine - pltpu.roll(g_rot, head_dim // 2, 1) * signed_sine
            u = w * gain
            g_lin = inv * (u - lin * inv * inv * jnp.mean(u * lin, axis=-1, keepdims=True))
            gain_acc[i : i + 1, :] += jnp.sum(w * lin * inv, axis=0, keepdims=True)
            gqkv_ref[:, i * wide + at : i * wide + at + head_dim] = g_lin.astype(bf16)
        gqkv_ref[:, 2 * wide + at : 2 * wide + at + head_dim] = g_v.astype(bf16)
    gqkv = gqkv_ref[...]
    part_ref[0] = dot(gqkv, w_ref[...], 1, 1).astype(bf16)
    dw_acc[...] += dot(x_ref[0], gqkv, 0, 0)

    @pl.when(step == pl.num_programs(0) - 1)
    def _():
        dw_ref[...] = dw_acc[...].astype(bf16)
        dwo_ref[...] = dwo_acc[...].astype(bf16)
        dgain_ref[...] = gain_acc[...]


def attend_back(lengths, x, g, mixed, w_qkv, w_out, query_g, key_g, cosine, signed_sine):
    seqs, rows, width = x.shape
    head_dim = query_g.shape[0]
    wide = w_qkv.shape[1] // 3
    whole = lambda s, lens: (0, 0)
    block = lambda s, lens: (s, 0, 0)
    table = pl.BlockSpec((rows, head_dim), whole)
    gain = pl.BlockSpec((1, head_dim), whole)
    return pl.pallas_call(
        functools.partial(attend_back_kernel, wide // head_dim, head_dim),
        out_shape=(
            jax.ShapeDtypeStruct((seqs, rows, width), bf16),
            jax.ShapeDtypeStruct((width, 3 * wide), bf16),
            jax.ShapeDtypeStruct((wide, width), bf16),
            jax.ShapeDtypeStruct((8, head_dim), f32),
        ),
        grid_spec=pltpu.PrefetchScalarGridSpec(
            num_scalar_prefetch=1,
            grid=(seqs,),
            in_specs=[
                pl.BlockSpec((1, rows, width), block),
                pl.BlockSpec((1, rows, width), block),
                pl.BlockSpec((1, rows, wide), block),
                pl.BlockSpec((width, 3 * wide), whole),
                pl.BlockSpec((wide, width), whole),
                gain,
                gain,
                table,
                table,
            ],
            out_specs=(
                pl.BlockSpec((1, rows, width), block),
                pl.BlockSpec((width, 3 * wide), whole),
                pl.BlockSpec((wide, width), whole),
                pl.BlockSpec((8, head_dim), whole),
            ),
            scratch_shapes=[
                pltpu.VMEM((width, 3 * wide), f32),
                pltpu.VMEM((wide, width), f32),
                pltpu.VMEM((8, head_dim), f32),
                pltpu.VMEM((rows, 3 * wide), bf16),
            ],
        ),
        compiler_params=pltpu.CompilerParams(vmem_limit_bytes=48 << 20),
        cost_estimate=pl.CostEstimate(
            flops=2 * seqs * rows * (width * 11 * wide + 5 * rows * wide),
            transcendentals=seqs * rows * rows * wide // head_dim,
            bytes_accessed=2 * (3 * x.size + w_qkv.size * 2),
        ),
        name="attend_back",
    )(lengths, x, g, mixed, w_qkv, w_out, query_g[None, :], key_g[None, :], cosine, signed_sine)


def pad_rows(flat, tile):
    rows = -(-flat.shape[0] // (128 * tile)) * tile
    return jnp.pad(flat, (0, rows * 128 - flat.shape[0])).reshape(rows, 128)


def einf(spec, left, right):
    return jnp.einsum(spec, left, right, preferred_element_type=f32)


def body(
    tokens,
    cotangent,
    lengths,
    deal_order,
    routes,
    balance_coef,
    w_query,
    w_key,
    w_value,
    w_out,
    w_router,
    attn_gain,
    mlp_gain,
    query_gain,
    key_gain,
    w_gate,
    w_up,
    w_down,
):
    groups = lax.axis_size("expert")
    replicas = lax.axis_size("dp")
    me = lax.axis_index("expert")
    tok_rows, width = tokens.shape
    block_rows = tok_rows // replicas
    total_slots = float(tok_rows * replicas * groups)
    shard_rows = w_query.shape[0]
    local_experts = w_gate.shape[0]
    experts = local_experts * groups
    top_k = routes.shape[1]
    capacity = tok_rows * top_k * 9 // (8 * experts)

    order_row = lax.dynamic_index_in_dim(deal_order, me, 0, keepdims=False)
    dp_ids = jnp.arange(replicas, dtype=jnp.int32)
    matched = (order_row[:, None] == dp_ids[None, :]).astype(jnp.int32)
    inverse_order = jnp.sum(matched * dp_ids[:, None], axis=0)

    def deal(values):
        blocks = values.reshape(replicas, block_rows, width)[inverse_order]
        return lax.all_to_all(blocks, "dp", split_axis=0, concat_axis=0, tiled=True).reshape(
            tok_rows, width
        )

    def undeal(values):
        back = lax.all_to_all(
            values.reshape(replicas, block_rows, width), "dp", split_axis=0, concat_axis=0, tiled=True
        )
        return back[order_row].reshape(tok_rows, width)

    seq_tokens = deal(tokens)
    seq_cot = deal(cotangent)

    small = jnp.concatenate(
        [w_router.reshape(-1), attn_gain, mlp_gain, query_gain, key_gain]
    )
    ints = jnp.concatenate([routes.reshape(-1), jnp.broadcast_to(lengths, (top_k,))])
    small_all, ints_all = gather_small(groups, 0, pad_rows(small, 16), pad_rows(ints, 8))
    small_all, ints_all = small_all.reshape(groups, -1), ints_all.reshape(groups, -1)
    n_router = shard_rows * experts
    cuts = [0, n_router]
    for gain in (attn_gain, mlp_gain, query_gain, key_gain):
        cuts.append(cuts[-1] + gain.shape[0])
    router_full = small_all[:, :n_router].reshape(width, experts)
    attn_g, mlp_g, query_g, key_g = (
        small_all[:, cuts[i] : cuts[i + 1]].reshape(-1).astype(f32) for i in range(1, 5)
    )
    head_dim = query_g.shape[0]
    local_width = w_query.shape[1] // groups

    routes_all = ints_all[:, : tok_rows * top_k].reshape(groups, tok_rows, top_k)
    lengths_all = ints_all[:, tok_rows * top_k]
    positions = jnp.arange(tok_rows, dtype=jnp.int32)
    live_all = (positions[None, :] < lengths_all[:, None]).astype(f32)
    live_rows = (positions < lengths[0]).astype(f32)

    def columns(weight):
        return weight.reshape(shard_rows, groups, local_width).transpose(1, 0, 2)

    w_send = jnp.concatenate([columns(w_query), columns(w_key), columns(w_value)], axis=2)
    w_qkv = lax.all_to_all(w_send, "expert", split_axis=0, concat_axis=0, tiled=True).reshape(
        width, 3 * local_width
    )
    wo_full = lax.all_gather(w_out, "expert", axis=0, tiled=True)

    inputs = seq_tokens.astype(f32)
    normed, inv_first = norm_fwd(inputs, attn_g)
    attn_in = normed.astype(bf16)
    attn_all = gather_rows(attn_in, groups, 1)
    grad_output = seq_cot.astype(f32) * live_rows[:, None]
    cot_all = lax.all_gather(grad_output.astype(bf16), "expert", axis=0, tiled=False)

    cosine, signed_sine = rotary_tables(tok_rows, head_dim)
    mixed = attend(lengths_all, attn_all, w_qkv, query_g, key_g, cosine, signed_sine)
    mixed_here = lax.all_to_all(mixed, "expert", split_axis=0, concat_axis=0, tiled=True)
    hidden = inputs + einf("xtm,xmd->td", mixed_here, wo_full.reshape(groups, local_width, width))
    mlp_normed, inv_second = norm_fwd(hidden, mlp_g)
    mlp_in = mlp_normed.astype(bf16)
    mlp_all = gather_rows(mlp_in, groups, 2)

    logits = einf("std,de->ste", mlp_all, router_full)
    router = jax.nn.softmax(logits, axis=-1)
    expert_ids = jnp.arange(experts, dtype=jnp.int32)
    picked = jnp.sum(
        (routes_all[:, :, :, None] == expert_ids).astype(f32), axis=2
    )
    chosen_sum = jnp.sum(picked * router, axis=-1, keepdims=True)
    gates = picked * router / chosen_sum
    counts = jnp.sum(picked * live_all[:, :, None], axis=(0, 1))
    prob_sums = jnp.sum(router * live_all[:, :, None], axis=(0, 1))
    live_count = jnp.sum(live_all)[None]
    sums = lax.psum(jnp.concatenate([counts, prob_sums, live_count]), "dp")
    counts, prob_sums, live_count = sums[:experts], sums[experts : 2 * experts], sums[2 * experts :]
    fraction = counts / (live_count * top_k)
    balance_loss = balance_coef * (experts * jnp.sum(fraction * prob_sums / total_slots))

    first = me * local_experts
    own_picked = lax.dynamic_slice_in_dim(picked, first, local_experts, 2)
    own_gates = lax.dynamic_slice_in_dim(gates, first, local_experts, 2)
    before = (positions[:, None] > positions[None, :]).astype(bf16)
    rank = einf("tu,suj->jst", before, own_picked.astype(bf16))
    own_picked = own_picked.transpose(2, 0, 1)
    own_gates = own_gates.transpose(2, 0, 1)
    slot_of = jnp.where(own_picked > 0.5, rank.astype(jnp.int32), -1)
    slot_ids = jnp.arange(capacity, dtype=jnp.int32)
    is_slot = slot_of[:, :, None, :] == slot_ids[None, None, :, None]
    one_hot = is_slot.astype(bf16)
    slot_gate = jnp.sum(jnp.where(is_slot, own_gates[:, :, None, :], 0.0), axis=-1)
    n_slots = groups * capacity

    expert_in = einf("jsct,std->jscd", one_hot, mlp_all).astype(bf16).reshape(
        local_experts, n_slots, width
    )
    gate_in = einf("jrd,jdf->jrf", expert_in, w_gate)
    up_in = einf("jrd,jdf->jrf", expert_in, w_up)
    sigmoid_gate = jax.nn.sigmoid(gate_in)
    activated = gate_in * sigmoid_gate
    act_low = (activated * up_in).astype(bf16)
    cot_slots = einf("jsct,std->jscd", one_hot, cot_all).astype(bf16)
    grad_recv = (
        (slot_gate[..., None] * cot_slots.astype(f32)).astype(bf16).reshape(local_experts, n_slots, width)
    )
    grad_down_w = einf("jrf,jrd->jfd", act_low, grad_recv)
    act_low, grad_recv, grad_down_w = lax.optimization_barrier((act_low, grad_recv, grad_down_w))
    total_down = lax.psum_scatter(
        grad_down_w.astype(bf16), "dp", scatter_dimension=1, tiled=True
    ).astype(f32)

    expert_out = einf("jrf,jfd->jrd", act_low, w_down).astype(bf16).reshape(
        local_experts, groups, capacity, width
    )
    grad_gate_slot = jnp.sum(cot_slots.astype(f32) * expert_out.astype(f32), axis=-1)
    own_grad_gates = jnp.sum(jnp.where(is_slot, grad_gate_slot[..., None], 0.0), axis=2)
    weighted = (slot_gate[..., None] * expert_out.astype(f32)).astype(bf16)
    sum_part = einf("jsct,jscd->std", one_hot, weighted).astype(bf16)

    grad_act = einf("jrd,jfd->jrf", grad_recv, w_down)
    grad_up_in = (grad_act * activated).astype(bf16)
    grad_gate_in = (
        grad_act * up_in * sigmoid_gate * (1.0 + gate_in * (1.0 - sigmoid_gate))
    ).astype(bf16)
    grad_gate_w = einf("jrd,jrf->jdf", expert_in, grad_gate_in)
    grad_up_w = einf("jrd,jrf->jdf", expert_in, grad_up_in)
    grad_gate_in, grad_up_in, grad_gate_w, grad_up_w = lax.optimization_barrier(
        (grad_gate_in, grad_up_in, grad_gate_w.astype(bf16), grad_up_w.astype(bf16))
    )
    grad_rows = (
        (einf("jrf,jdf->jrd", grad_gate_in, w_gate) + einf("jrf,jdf->jrd", grad_up_in, w_up))
        .astype(bf16)
        .reshape(local_experts, groups, capacity, width)
    )
    grad_part = einf("jsct,jscd->std", one_hot, grad_rows).astype(bf16)
    grad_mlp_in = scatter_sum(grad_part, groups, 3)

    total_gate, total_up = (
        lax.psum_scatter(value.astype(bf16), "dp", scatter_dimension=1, tiled=True).astype(f32)
        for value in (grad_gate_w, grad_up_w)
    )

    gate_back = lax.all_to_all(
        own_grad_gates.transpose(1, 0, 2), "expert", split_axis=0, concat_axis=0, tiled=True
    )
    grad_gates = gate_back.reshape(experts, tok_rows).T
    my_router = lax.dynamic_index_in_dim(router, me, 0, keepdims=False)
    my_picked = lax.dynamic_index_in_dim(picked, me, 0, keepdims=False)
    my_gates = lax.dynamic_index_in_dim(gates, me, 0, keepdims=False)
    my_sum = lax.dynamic_index_in_dim(chosen_sum, me, 0, keepdims=False)
    grad_prob = (
        my_picked * (grad_gates - jnp.sum(grad_gates * my_gates, axis=1, keepdims=True)) / my_sum
        + live_rows[:, None] * (balance_coef * experts / total_slots) * fraction[None, :]
    )
    grad_logits = (
        my_router * (grad_prob - jnp.sum(my_router * grad_prob, axis=-1, keepdims=True))
    ).astype(bf16)
    grad_router_w = einf("td,te->de", mlp_in, grad_logits)
    grad_mlp_in = grad_mlp_in + einf("te,de->td", grad_logits, router_full)

    grad_hidden_norm, grad_mlp_g = norm_back(hidden, inv_second, mlp_g, grad_mlp_in, 0)
    grad_hidden = grad_output + grad_hidden_norm
    grad_hidden_low = grad_hidden.astype(bf16)
    hidden_all = gather_rows(grad_hidden_low, groups, 4)
    grad_attn_part, grad_qkv_w, grad_out_w, grad_gains = attend_back(
        lengths_all, attn_all, hidden_all, mixed, w_qkv, w_out, query_g, key_g, cosine, signed_sine
    )
    grad_query_g, grad_key_g = grad_gains[0], grad_gains[1]
    grad_attn_part, total_down = lax.optimization_barrier((grad_attn_part, total_down))
    grad_attn_in = scatter_sum(grad_attn_part, groups, 5)
    w_back = lax.all_to_all(
        grad_qkv_w.reshape(groups, shard_rows, 3 * local_width),
        "expert",
        split_axis=0,
        concat_axis=0,
        tiled=True,
    )
    attn_w = jnp.concatenate(
        [
            w_back[:, :, i * local_width : (i + 1) * local_width]
            .transpose(1, 0, 2)
            .reshape(shard_rows, groups * local_width)
            for i in range(3)
        ]
        + [grad_out_w],
        axis=0,
    )
    attn_w, total_up = lax.optimization_barrier((attn_w, total_up))
    attn_sum = lax.psum(attn_w, "dp").astype(f32)
    sum_q, sum_k, sum_v, sum_o = (
        attn_sum[i * shard_rows : (i + 1) * shard_rows] for i in range(4)
    )

    grad_attn_in, total_gate = lax.optimization_barrier((grad_attn_in, total_gate))
    grad_input_norm, grad_attn_g = norm_back(inputs, inv_first, attn_g, grad_attn_in, 0)
    grad_input = undeal((grad_hidden + grad_input_norm).astype(bf16)).astype(f32)

    expert_sum = scatter_sum(sum_part, groups, 6)
    output = undeal((live_rows[:, None] * (hidden + expert_sum)).astype(bf16))

    pieces = [grad_router_w.astype(bf16).reshape(groups, n_router)] + [
        value.astype(bf16).reshape(groups, -1)
        for value in (grad_attn_g, grad_mlp_g, grad_query_g, grad_key_g)
    ]
    part_small = lax.psum_scatter(
        jnp.concatenate(pieces, axis=1), "expert", scatter_dimension=0, tiled=True
    )
    sum_small = lax.psum(part_small.reshape(-1), "dp").astype(f32)
    sum_r = sum_small[:n_router].reshape(shard_rows, experts)
    sum_ga, sum_gm, sum_gq, sum_gk = (sum_small[cuts[i] : cuts[i + 1]] for i in range(1, 5))
    return (
        output,
        balance_loss,
        grad_input,
        sum_q,
        sum_k,
        sum_v,
        sum_o,
        sum_r,
        sum_ga,
        sum_gm,
        sum_gq,
        sum_gk,
        total_gate,
        total_up,
        total_down,
    )


def solution(mesh):
    rows = P(("dp", "expert"), None)
    weight = P("expert", None)
    gain = P("expert")
    cube = P("expert", None, None)
    cube_out = P("expert", "dp", None)
    return jax.shard_map(
        body,
        mesh=mesh,
        in_specs=(
            (rows, rows, P(("dp", "expert")), P(), rows, P())
            + (weight,) * 5
            + (gain,) * 4
            + (cube,) * 3
        ),
        out_specs=(
            (rows, P(), rows) + (weight,) * 5 + (gain,) * 4 + (cube_out,) * 3
        ),
        check_vma=False,
    )
```

```python
import functools
import math

import jax
import jax.numpy as jnp
from jax import lax
from jax.experimental import pallas as pl
from jax.experimental.pallas import tpu as pltpu
from jax.sharding import PartitionSpec as P

norm_eps = 1e-06
rope_base = 50000.0
big_negative = -1e30
bf16 = jnp.bfloat16
f32 = jnp.float32
MESH = pl.DeviceIdType.MESH
DMA = pltpu.SemaphoreType.DMA
small_cost = pl.CostEstimate(flops=0, transcendentals=0, bytes_accessed=1024)


def norm_fwd(values, scales):
    inverse = lax.rsqrt(jnp.mean(values * values, axis=-1, keepdims=True) + norm_eps)
    return (values * inverse * scales, inverse)


def norm_back(values, inverse, scales, grad_out, sum_axes):
    scaled = grad_out * scales
    grad_in = inverse * (
        scaled - values * inverse * inverse * jnp.mean(scaled * values, axis=-1, keepdims=True)
    )
    grad_scale = jnp.sum(grad_out * values * inverse, axis=sum_axes)
    return (grad_in, grad_scale)


def rotary_tables(tok_rows, head_dim):
    half_dim = head_dim // 2
    positions = jnp.arange(tok_rows, dtype=jnp.int32).astype(f32)
    frequency = rope_base ** (-jnp.arange(half_dim, dtype=jnp.int32).astype(f32) * 2.0 / head_dim)
    angles = positions[:, None] * frequency[None, :]
    cosine = jnp.concatenate([jnp.cos(angles), jnp.cos(angles)], axis=-1)
    signed_sine = jnp.concatenate([-jnp.sin(angles), jnp.sin(angles)], axis=-1)
    return (cosine, signed_sine)


def peer(index):
    return {"expert": index}


def remote(src, dst, send, recv, to):
    return pltpu.make_async_remote_copy(
        src_ref=src, dst_ref=dst, send_sem=send, recv_sem=recv, device_id=peer(to), device_id_type=MESH
    )


def greet(n, me, replicas=1):
    barrier = pltpu.get_barrier_semaphore()
    for k in range(1, n):
        pl.semaphore_signal(
            barrier, inc=1, device_id=peer(lax.rem(me + k, n)), device_id_type=MESH
        )
    for k in range(1, replicas):
        other = lax.rem(lax.axis_index("dp") + k, replicas)
        pl.semaphore_signal(barrier, inc=1, device_id={"dp": other}, device_id_type=MESH)
    pl.semaphore_wait(barrier, n + replicas - 2)


def quad_places(me):
    core = lax.rem(me, 2)
    chip = me // 2
    x = lax.rem(chip, 2)
    y = chip // 2

    def at(px, py, pc):
        return (py * 2 + px) * 2 + pc

    spots = ((x, y), (1 - x, y), (x, 1 - y), (1 - x, 1 - y))
    return [at(px, py, core) for px, py in spots], [at(px, py, 1 - core) for px, py in spots]


def any_places(n, me):
    core = lax.rem(me, 2)
    chip = me // 2
    chips = n // 2
    chip_of = [lax.rem(chip + k, chips) for k in range(chips)]
    chip_from = [lax.rem(chip - k + chips, chips) for k in range(chips)]
    return (
        [c * 2 + core for c in chip_of],
        [c * 2 + 1 - core for c in chip_of],
        [c * 2 + core for c in chip_from],
        [c * 2 + 1 - core for c in chip_from],
    )


def deal_copies(replicas, src, dst, own_sem, send_sem, recv_sem):
    here = lax.axis_index("dp")
    rows = src.shape[1]
    mine = pl.ds(here * rows, rows)
    own = pltpu.make_async_copy(src.at[here], dst.at[mine], own_sem)
    away = []
    for k in range(1, replicas):
        to = lax.rem(here + k, replicas)
        away.append(
            pltpu.make_async_remote_copy(
                src_ref=src.at[to],
                dst_ref=dst.at[mine],
                send_sem=send_sem.at[k],
                recv_sem=recv_sem.at[k],
                device_id={"dp": to},
                device_id_type=MESH,
            )
        )
    return own, away


def front_kernel(
    n,
    replicas,
    small,
    ints,
    blocks,
    wq,
    wk,
    wv,
    small_all,
    ints_all,
    seq,
    w_all,
    small_send,
    small_recv,
    own_sem,
    deal_send,
    deal_recv,
    w_own,
    w_send,
    w_recv,
):
    me = lax.axis_index("expert")
    wide = wq.shape[1] // n
    small_all[me] = small[...]
    ints_all[me] = ints[...]
    own, away = deal_copies(replicas, blocks, seq, own_sem, deal_send, deal_recv)
    own.start()

    def columns(weight, index):
        return weight.at[:, pl.ds(pl.multiple_of(index * wide, wide), wide)]

    kept = []
    for i, weight in enumerate((wq, wk, wv)):
        copy = pltpu.make_async_copy(
            columns(weight, me), w_all.at[me, :, pl.ds(i * wide, wide)], w_own.at[i]
        )
        copy.start()
        kept.append(copy)
    greet(n, me, replicas)
    copies = []

    def go(copy):
        copy.start()
        copies.append(copy)

    for k in range(1, n):
        to = lax.rem(me + k, n)
        go(remote(small, small_all.at[me], small_send.at[0, k], small_recv.at[0, k], to))
        go(remote(ints, ints_all.at[me], small_send.at[1, k], small_recv.at[1, k], to))
    for copy in away:
        go(copy)
    for k in range(1, n):
        to = lax.rem(me + k, n)
        for i, weight in enumerate((wq, wk, wv)):
            go(
                remote(
                    columns(weight, to),
                    w_all.at[me, :, pl.ds(i * wide, wide)],
                    w_send.at[i, k],
                    w_recv.at[i, k],
                    to,
                )
            )
    for copy in copies:
        copy.wait()
    own.wait()
    for copy in kept:
        copy.wait()


def front(n, replicas, collective_id, small, ints, blocks, wq, wk, wv):
    vmem = pl.BlockSpec(memory_space=pltpu.VMEM)
    away = pl.BlockSpec(memory_space=pl.ANY)
    rows, width = wq.shape
    return pl.pallas_call(
        functools.partial(front_kernel, n, replicas),
        out_shape=[
            jax.ShapeDtypeStruct((n,) + small.shape, small.dtype),
            jax.ShapeDtypeStruct((n,) + ints.shape, ints.dtype),
            jax.ShapeDtypeStruct((replicas * blocks.shape[1], width), bf16),
            jax.ShapeDtypeStruct((n, rows, 3 * (width // n)), bf16),
        ],
        in_specs=[vmem, vmem, away, away, away, away],
        out_specs=[vmem, vmem, away, away],
        scratch_shapes=[
            DMA((2, n)),
            DMA((2, n)),
            DMA,
            DMA((replicas,)),
            DMA((replicas,)),
            DMA((3,)),
            DMA((3, n)),
            DMA((3, n)),
        ],
        compiler_params=pltpu.CompilerParams(collective_id=collective_id, has_side_effects=True),
        cost_estimate=small_cost,
        name="front",
    )(small, ints, blocks, wq, wk, wv)


def small_sum_kernel(n, replicas, x_ref, o_ref, got, total, send_sem, recv_sem, over_send, over_recv):
    me = lax.axis_index("expert")
    here = lax.axis_index("dp")
    greet(n, me, replicas)
    copies = []
    for k in range(1, n):
        to = lax.rem(me + k, n)
        copy = remote(x_ref.at[to], got.at[me], send_sem.at[k], recv_sem.at[k], to)
        copy.start()
        copies.append(copy)
    got[me] = x_ref[me]
    for copy in copies:
        copy.wait()
    value = got[0]
    for k in range(1, n):
        value = value + got[k]
    total[here] = value
    copies = []
    for k in range(1, replicas):
        copy = pltpu.make_async_remote_copy(
            src_ref=total.at[here],
            dst_ref=total.at[here],
            send_sem=over_send.at[k],
            recv_sem=over_recv.at[k],
            device_id={"dp": lax.rem(here + k, replicas)},
            device_id_type=MESH,
        )
        copy.start()
        copies.append(copy)
    for copy in copies:
        copy.wait()
    value = total[0]
    for k in range(1, replicas):
        value = value + total[k]
    o_ref[...] = value


def small_sum(x, replicas, collective_id):
    n = x.shape[0]
    shape = x.shape[1:]
    vmem = pl.BlockSpec(memory_space=pltpu.VMEM)
    return pl.pallas_call(
        functools.partial(small_sum_kernel, n, replicas),
        out_shape=jax.ShapeDtypeStruct(shape, f32),
        in_specs=[vmem],
        out_specs=vmem,
        scratch_shapes=[
            pltpu.VMEM(x.shape, f32),
            pltpu.VMEM((replicas,) + shape, f32),
            DMA((n,)),
            DMA((n,)),
            DMA((replicas,)),
            DMA((replicas,)),
        ],
        compiler_params=pltpu.CompilerParams(collective_id=collective_id, has_side_effects=True),
        name="small_sum",
    )(x)


def quad_gather_kernel(parts, meet, x_ref, o_ref, own_sem, send_sem, recv_sem, pass_sem, pair_send, pair_recv):
    me = lax.axis_index("expert")
    same, other = quad_places(me)
    step = x_ref.shape[0] // parts
    half = parts // 2
    own = pltpu.make_async_copy(x_ref, o_ref.at[me], own_sem)
    own.start()
    meet(me)
    started = []

    def go(copy):
        copy.start()
        started.append(copy)

    def piece(p):
        return pl.ds(p * step, step)

    low, high = list(range(half)), list(range(half, parts))
    turns = [(k, seq[i]) for i in range(parts) for k, seq in ((1, high + low), (2, low + high))]
    for k, p in turns:
        go(remote(x_ref.at[piece(p)], o_ref.at[me, piece(p)], send_sem.at[k, p], recv_sem.at[k, p], same[k]))
    for p in range(parts):
        go(remote(x_ref.at[piece(p)], o_ref.at[me, piece(p)], pair_send.at[0, p], pair_recv.at[0, p], other[0]))

    def arrive(k, p):
        block = o_ref.at[same[k], piece(p)]
        remote(block, block, send_sem.at[k, p], recv_sem.at[k, p], other[0]).wait_recv()
        return block

    for k, p in turns:
        block = arrive(k, p)
        if (p >= half) == (k == 1):
            go(remote(block, block, pass_sem.at[p], recv_sem.at[3, p], same[3 - k]))
        go(remote(block, block, pair_send.at[k, p], pair_recv.at[k, p], other[0]))
    for pair in zip(low, high):
        for p in pair:
            block = arrive(3, p)
            go(remote(block, block, pair_send.at[3, p], pair_recv.at[3, p], other[0]))
    for k in range(4):
        for p in range(parts):
            block = o_ref.at[other[k], piece(p)]
            remote(block, block, pair_send.at[k, p], pair_recv.at[k, p], other[0]).wait_recv()
    for copy in started:
        copy.wait_send()
    own.wait()


def any_gather_kernel(n, meet, x_ref, o_ref, own_sem, send_sem, recv_sem, pair_send, pair_recv):
    me = lax.axis_index("expert")
    same, other, same_from, other_from = any_places(n, me)
    own = pltpu.make_async_copy(x_ref, o_ref.at[me], own_sem)
    own.start()
    meet(me)
    started = []
    for k in range(n // 2):
        if k:
            copy = remote(x_ref, o_ref.at[me], send_sem.at[k], recv_sem.at[k], same[k])
        else:
            copy = remote(x_ref, o_ref.at[me], pair_send.at[0], pair_recv.at[0], other[0])
        copy.start()
        started.append(copy)
    for k in range(1, n // 2):
        block = o_ref.at[same_from[k]]
        remote(block, block, send_sem.at[k], recv_sem.at[k], other[0]).wait_recv()
        copy = remote(block, block, pair_send.at[k], pair_recv.at[k], other[0])
        copy.start()
        started.append(copy)
    for k in range(n // 2):
        block = o_ref.at[other_from[k]]
        remote(block, block, pair_send.at[k], pair_recv.at[k], other[0]).wait_recv()
    for copy in started:
        copy.wait_send()
    own.wait()


def gather_plan(n, parts):
    chips = n // 2
    if n == 8:
        sems = [DMA, DMA((4, parts)), DMA((4, parts)), DMA((parts,)), DMA((4, parts)), DMA((4, parts))]
        return functools.partial(quad_gather_kernel, parts), sems
    sems = [DMA, DMA((chips,)), DMA((chips,)), DMA((chips,)), DMA((chips,))]
    return functools.partial(any_gather_kernel, n), sems


def gather_only(n, kernel, *refs):
    kernel(functools.partial(greet, n), *refs)


def gather_and_deal(n, replicas, kernel, x_ref, blocks, o_ref, seq, own_sem, deal_send, deal_recv, *sems):
    own, away = deal_copies(replicas, blocks, seq, own_sem, deal_send, deal_recv)

    def meet(me):
        own.start()
        greet(n, me, replicas)
        for copy in away:
            copy.start()

    kernel(meet, x_ref, o_ref, *sems)
    for copy in away:
        copy.wait()
    own.wait()


def gather_rows(x, n, collective_id, parts=4, blocks=None):
    kernel, sems = gather_plan(n, parts)
    params = pltpu.CompilerParams(collective_id=collective_id, has_side_effects=True)
    away = pl.BlockSpec(memory_space=pl.ANY)
    shape = jax.ShapeDtypeStruct((n,) + x.shape, x.dtype)
    name = f"gather_rows_{collective_id}"
    if blocks is None:
        return pl.pallas_call(
            functools.partial(gather_only, n, kernel),
            out_shape=shape,
            in_specs=[away],
            out_specs=away,
            scratch_shapes=sems,
            compiler_params=params,
            cost_estimate=small_cost,
            name=name,
        )(x)
    replicas = blocks.shape[0]
    return pl.pallas_call(
        functools.partial(gather_and_deal, n, replicas, kernel),
        out_shape=[shape, jax.ShapeDtypeStruct((replicas * blocks.shape[1], blocks.shape[2]), bf16)],
        in_specs=[away, away],
        out_specs=[away, away],
        scratch_shapes=[DMA, DMA((replicas,)), DMA((replicas,))] + sems,
        compiler_params=params,
        cost_estimate=small_cost,
        name=name,
    )(x, blocks)


def add_rows(total, first, rows, chunk, *terms):
    @pl.loop(0, rows // chunk)
    def _(i):
        s = pl.ds(first + i * chunk, chunk)
        value = terms[0][s].astype(f32)
        for term in terms[1:]:
            value = value + term[s].astype(f32)
        total[s] = value.astype(total.dtype)


class Riders:
    def __init__(self, n, replicas, gates, stats, gates_out, stats_out, got, sems):
        self.n, self.replicas = n, replicas
        self.refs = (gates, stats, gates_out, stats_out, got)
        self.sems = sems

    def start(self, me):
        gates, stats, gates_out, _, got = self.refs
        here = lax.axis_index("dp")
        gates_out[me] = gates[me]
        got[here] = stats[...]
        greet(self.n, me, self.replicas)
        self.copies = []
        for k in range(1, self.n):
            to = lax.rem(me + k, self.n)
            self.copies.append(
                remote(gates.at[to], gates_out.at[me], self.sems[0].at[k], self.sems[1].at[k], to)
            )
        for k in range(1, self.replicas):
            self.copies.append(
                pltpu.make_async_remote_copy(
                    src_ref=stats,
                    dst_ref=got.at[here],
                    send_sem=self.sems[2].at[k],
                    recv_sem=self.sems[3].at[k],
                    device_id={"dp": lax.rem(here + k, self.replicas)},
                    device_id_type=MESH,
                )
            )
        for copy in self.copies:
            copy.start()

    def finish(self):
        _, _, _, stats_out, got = self.refs
        for copy in self.copies:
            copy.wait()
        value = got[0]
        for k in range(1, self.replicas):
            value = value + got[k]
        stats_out[...] = value


def quad_scatter_kernel(
    parts, meet, p_ref, o_ref, mine, theirs, transit, got, load_sem, pair_send, pair_recv, over_send, over_recv, send_sem, recv_sem
):
    me = lax.axis_index("expert")
    same, other = quad_places(me)
    step = p_ref.shape[1] // parts
    half = parts // 2
    low, high = list(range(half)), list(range(half, parts))
    mix = [p for pair in zip(low, high) for p in pair]
    order = (3, 1, 2, 0)

    def piece(p):
        return pl.ds(p * step, step)

    loads = {}
    for k in order:
        for p in mix:
            loads[k, p] = pltpu.make_async_copy(
                p_ref.at[same[k], piece(p)], mine.at[k, piece(p)], load_sem.at[k, p]
            )
            loads[k, p].start()
    meet(me)
    started = []

    def go(copy):
        copy.start()
        started.append(copy)

    for k in order:
        for p in mix:
            go(
                remote(
                    p_ref.at[other[k], piece(p)],
                    theirs.at[k, piece(p)],
                    pair_send.at[k, p],
                    pair_recv.at[k, p],
                    other[0],
                )
            )

    def fold(k, p):
        loads[k, p].wait()
        spot = theirs.at[k, piece(p)]
        remote(spot, spot, pair_send.at[k, p], pair_recv.at[k, p], other[0]).wait_recv()
        add_rows(mine.at[k], p * step, step, 32, mine.at[k], theirs.at[k])

    def ship(k, p):
        go(
            remote(
                mine.at[k, piece(p)],
                got.at[k - 1, piece(p)],
                send_sem.at[k - 1, p],
                recv_sem.at[k - 1, p],
                same[k],
            )
        )

    for p in mix:
        fold(3, p)
        to = same[1] if p < half else same[2]
        go(remote(mine.at[3, piece(p)], transit.at[piece(p)], over_send.at[p], over_recv.at[p], to))
    for a, b in zip(low, high):
        for k, p in ((1, a), (2, b)):
            fold(k, p)
            ship(k, p)
    for a, b in zip(low, high):
        for k, p in ((2, a), (1, b)):
            fold(k, p)
            spot = transit.at[piece(p)]
            remote(spot, spot, over_send.at[p], over_recv.at[p], other[0]).wait_recv()
            add_rows(mine.at[k], p * step, step, 32, mine.at[k], transit)
            ship(k, p)
    for p in mix:
        fold(0, p)
    for p in mix:
        for k in (0, 1):
            spot = got.at[k, piece(p)]
            remote(spot, spot, send_sem.at[k, p], recv_sem.at[k, p], other[0]).wait_recv()
        add_rows(o_ref, p * step, step, 32, mine.at[0], got.at[0], got.at[1])
    for copy in started:
        copy.wait_send()


def any_scatter_kernel(n, meet, p_ref, o_ref, mine, theirs, got, load_sem, pair_send, pair_recv, send_sem, recv_sem):
    me = lax.axis_index("expert")
    same, other, _, _ = any_places(n, me)
    rows = p_ref.shape[1]
    order = list(range(1, n // 2)) + [0]
    loads = {}
    for k in order:
        loads[k] = pltpu.make_async_copy(p_ref.at[same[k]], mine.at[k], load_sem.at[k])
        loads[k].start()
    meet(me)
    started = []
    for k in order:
        copy = remote(p_ref.at[other[k]], theirs.at[k], pair_send.at[k], pair_recv.at[k], other[0])
        copy.start()
        started.append(copy)
    for k in order:
        loads[k].wait()
        remote(theirs.at[k], theirs.at[k], pair_send.at[k], pair_recv.at[k], other[0]).wait_recv()
        add_rows(mine.at[k], 0, rows, 32, mine.at[k], theirs.at[k])
        if k:
            copy = remote(mine.at[k], got.at[k], send_sem.at[k], recv_sem.at[k], same[k])
            copy.start()
            started.append(copy)
    for k in range(1, n // 2):
        remote(got.at[k], got.at[k], send_sem.at[k], recv_sem.at[k], other[0]).wait_recv()
    add_rows(o_ref, 0, rows, 32, mine.at[0], *[got.at[k] for k in range(1, n // 2)])
    for copy in started:
        copy.wait_send()


def scatter_only(n, kernel, *refs):
    kernel(functools.partial(greet, n), *refs)


def scatter_and_ride(n, replicas, kernel, p_ref, gates, stats, o_ref, gates_out, stats_out, got, *rest):
    riders = Riders(n, replicas, gates, stats, gates_out, stats_out, got, rest[:4])
    kernel(riders.start, p_ref, o_ref, *rest[4:])
    riders.finish()


def scatter_sum(x, n, collective_id, parts=4, replicas=1, riders=None):
    chips = n // 2
    shape = x.shape[1:]
    blocks = pltpu.VMEM((chips,) + shape, bf16)
    if n == 8:
        kernel = functools.partial(quad_scatter_kernel, parts)
        scratch = [blocks, blocks, pltpu.VMEM(shape, bf16), pltpu.VMEM((2,) + shape, bf16)]
        scratch += [DMA((4, parts))] * 3 + [DMA((parts,))] * 2 + [DMA((2, parts))] * 2
    else:
        kernel = functools.partial(any_scatter_kernel, n)
        scratch = [blocks] * 3 + [DMA((chips,))] * 5
    vmem = pl.BlockSpec(memory_space=pltpu.VMEM)
    away = pl.BlockSpec(memory_space=pl.ANY)
    common = dict(
        compiler_params=pltpu.CompilerParams(
            collective_id=collective_id, has_side_effects=True, vmem_limit_bytes=(3 * chips + 12) << 20
        ),
        cost_estimate=small_cost,
        name=f"scatter_sum_{collective_id}",
    )
    out = jax.ShapeDtypeStruct(shape, f32)
    if riders is None:
        return pl.pallas_call(
            functools.partial(scatter_only, n, kernel),
            out_shape=out,
            in_specs=[away],
            out_specs=vmem,
            scratch_shapes=scratch,
            **common,
        )(x)
    gates, stats = riders
    return pl.pallas_call(
        functools.partial(scatter_and_ride, n, replicas, kernel),
        out_shape=[
            out,
            jax.ShapeDtypeStruct(gates.shape, f32),
            jax.ShapeDtypeStruct(stats.shape, f32),
        ],
        in_specs=[away, vmem, vmem],
        out_specs=[vmem, vmem, vmem],
        scratch_shapes=[
            pltpu.VMEM((replicas,) + stats.shape, f32),
            DMA((n,)),
            DMA((n,)),
            DMA((replicas,)),
            DMA((replicas,)),
        ]
        + scratch,
        **common,
    )(x, gates, stats)


def dot(left, right, left_dim=1, right_dim=0):
    return lax.dot_general(
        left, right, (((left_dim,), (right_dim,)), ((), ())), preferred_element_type=f32
    )


def head_values(lin, gain, cosine, signed_sine):
    inverse = lax.rsqrt(jnp.mean(lin * lin, axis=-1, keepdims=True) + norm_eps)
    normed = lin * inverse * gain
    half = lin.shape[1] // 2
    turned = normed * cosine + pltpu.roll(normed, half, 1) * signed_sine
    return inverse, turned.astype(bf16)


def head_probs(q_rot, k_rot, length, score_scale):
    scores = dot(q_rot, k_rot, 1, 1) * score_scale
    key = lax.broadcasted_iota(jnp.int32, scores.shape, 1)
    masked = jnp.where(key < length, scores, big_negative)
    raised = jnp.exp(masked - jnp.max(masked, axis=-1, keepdims=True))
    return raised / jnp.sum(raised, axis=-1, keepdims=True)


def attend_kernel(heads, head_dim, lengths_ref, x_ref, w_ref, qg_ref, kg_ref, cos_ref, sin_ref, mixed_ref):
    length = lengths_ref[pl.program_id(0)]
    wide = heads * head_dim
    qkv = dot(x_ref[0], w_ref[...])
    for h in range(heads):
        at = h * head_dim
        _, q_rot = head_values(qkv[:, at : at + head_dim], qg_ref[...], cos_ref[...], sin_ref[...])
        _, k_rot = head_values(
            qkv[:, wide + at : wide + at + head_dim], kg_ref[...], cos_ref[...], sin_ref[...]
        )
        v = qkv[:, 2 * wide + at : 2 * wide + at + head_dim].astype(bf16)
        probs = head_probs(q_rot, k_rot, length, 1.0 / math.sqrt(head_dim))
        mixed_ref[0, :, at : at + head_dim] = dot(probs.astype(bf16), v).astype(bf16)


def attend(lengths, x, w_qkv, query_g, key_g, cosine, signed_sine):
    seqs, rows, width = x.shape
    head_dim = query_g.shape[0]
    wide = w_qkv.shape[1] // 3
    whole = lambda s, lens: (0, 0)
    table = pl.BlockSpec((rows, head_dim), whole)
    gain = pl.BlockSpec((1, head_dim), whole)
    return pl.pallas_call(
        functools.partial(attend_kernel, wide // head_dim, head_dim),
        out_shape=jax.ShapeDtypeStruct((seqs, rows, wide), bf16),
        grid_spec=pltpu.PrefetchScalarGridSpec(
            num_scalar_prefetch=1,
            grid=(seqs,),
            in_specs=[
                pl.BlockSpec((1, rows, width), lambda s, lens: (s, 0, 0)),
                pl.BlockSpec((width, 3 * wide), whole),
                gain,
                gain,
                table,
                table,
            ],
            out_specs=pl.BlockSpec((1, rows, wide), lambda s, lens: (s, 0, 0)),
        ),
        compiler_params=pltpu.CompilerParams(vmem_limit_bytes=32 << 20),
        cost_estimate=small_cost,
        name="attend",
    )(lengths, x, w_qkv, query_g[None, :], key_g[None, :], cosine, signed_sine)


def attend_back_kernel(
    heads,
    head_dim,
    lengths_ref,
    x_ref,
    g_ref,
    mixed_ref,
    w_ref,
    wo_ref,
    qg_ref,
    kg_ref,
    cos_ref,
    sin_ref,
    part_ref,
    dw_ref,
    dwo_ref,
    dgain_ref,
    dw_acc,
    dwo_acc,
    gain_acc,
    gqkv_ref,
):
    step = pl.program_id(0)
    length = lengths_ref[step]
    wide = heads * head_dim
    scale = 1.0 / math.sqrt(head_dim)
    cosine, signed_sine = cos_ref[...], sin_ref[...]

    @pl.when(step == 0)
    def _():
        dw_acc[...] = jnp.zeros_like(dw_acc)
        dwo_acc[...] = jnp.zeros_like(dwo_acc)
        gain_acc[...] = jnp.zeros_like(gain_acc)

    qkv = dot(x_ref[0], w_ref[...])
    g_mixed = dot(g_ref[0], wo_ref[...], 1, 1).astype(bf16)
    dwo_acc[...] += dot(mixed_ref[0], g_ref[0], 0, 0)
    for h in range(heads):
        at = h * head_dim
        q_lin = qkv[:, at : at + head_dim]
        k_lin = qkv[:, wide + at : wide + at + head_dim]
        v = qkv[:, 2 * wide + at : 2 * wide + at + head_dim].astype(bf16)
        q_inv, q_rot = head_values(q_lin, qg_ref[...], cosine, signed_sine)
        k_inv, k_rot = head_values(k_lin, kg_ref[...], cosine, signed_sine)
        probs = head_probs(q_rot, k_rot, length, scale)
        gm = g_mixed[:, at : at + head_dim]
        g_probs = dot(gm, v, 1, 1)
        g_scores = (probs * (g_probs - jnp.sum(probs * g_probs, axis=-1, keepdims=True))).astype(bf16)
        g_v = dot(probs.astype(bf16), gm, 0, 0)
        for i, (g_rot, lin, inv, gain) in enumerate(
            (
                (dot(g_scores, k_rot) * scale, q_lin, q_inv, qg_ref[...]),
                (dot(g_scores, q_rot, 0, 0) * scale, k_lin, k_inv, kg_ref[...]),
            )
        ):
            w = g_rot * cosine - pltpu.roll(g_rot, head_dim // 2, 1) * signed_sine
            u = w * gain
            g_lin = inv * (u - lin * inv * inv * jnp.mean(u * lin, axis=-1, keepdims=True))
            gain_acc[i : i + 1, :] += jnp.sum(w * lin * inv, axis=0, keepdims=True)
            gqkv_ref[:, i * wide + at : i * wide + at + head_dim] = g_lin.astype(bf16)
        gqkv_ref[:, 2 * wide + at : 2 * wide + at + head_dim] = g_v.astype(bf16)
    gqkv = gqkv_ref[...]
    part_ref[0] = dot(gqkv, w_ref[...], 1, 1).astype(bf16)
    dw_acc[...] += dot(x_ref[0], gqkv, 0, 0)

    @pl.when(step == pl.num_programs(0) - 1)
    def _():
        dw_ref[...] = dw_acc[...].astype(bf16)
        dwo_ref[...] = dwo_acc[...].astype(bf16)
        dgain_ref[...] = gain_acc[...]


def attend_back(lengths, x, g, mixed, w_qkv, w_out, query_g, key_g, cosine, signed_sine):
    seqs, rows, width = x.shape
    head_dim = query_g.shape[0]
    wide = w_qkv.shape[1] // 3
    whole = lambda s, lens: (0, 0)
    block = lambda s, lens: (s, 0, 0)
    table = pl.BlockSpec((rows, head_dim), whole)
    gain = pl.BlockSpec((1, head_dim), whole)
    return pl.pallas_call(
        functools.partial(attend_back_kernel, wide // head_dim, head_dim),
        out_shape=(
            jax.ShapeDtypeStruct((seqs, rows, width), bf16),
            jax.ShapeDtypeStruct((width, 3 * wide), bf16),
            jax.ShapeDtypeStruct((wide, width), bf16),
            jax.ShapeDtypeStruct((8, head_dim), f32),
        ),
        grid_spec=pltpu.PrefetchScalarGridSpec(
            num_scalar_prefetch=1,
            grid=(seqs,),
            in_specs=[
                pl.BlockSpec((1, rows, width), block),
                pl.BlockSpec((1, rows, width), block),
                pl.BlockSpec((1, rows, wide), block),
                pl.BlockSpec((width, 3 * wide), whole),
                pl.BlockSpec((wide, width), whole),
                gain,
                gain,
                table,
                table,
            ],
            out_specs=(
                pl.BlockSpec((1, rows, width), block),
                pl.BlockSpec((width, 3 * wide), whole),
                pl.BlockSpec((wide, width), whole),
                pl.BlockSpec((8, head_dim), whole),
            ),
            scratch_shapes=[
                pltpu.VMEM((width, 3 * wide), f32),
                pltpu.VMEM((wide, width), f32),
                pltpu.VMEM((8, head_dim), f32),
                pltpu.VMEM((rows, 3 * wide), bf16),
            ],
        ),
        compiler_params=pltpu.CompilerParams(vmem_limit_bytes=48 << 20),
        cost_estimate=small_cost,
        name="attend_back",
    )(lengths, x, g, mixed, w_qkv, w_out, query_g[None, :], key_g[None, :], cosine, signed_sine)


def slot_matrix(slot_row, capacity):
    return lax.broadcasted_iota(jnp.int32, (capacity, slot_row.shape[1]), 0) == slot_row


def stack(pieces):
    return pieces[0] if len(pieces) == 1 else jnp.concatenate(pieces, axis=0)


def expert_in_kernel(capacity, x_ref, cot_ref, slot_ref, gate_ref, wg_ref, wu_ref, in_ref, gr_ref, act_ref, g_ref, u_ref):
    for j in range(wg_ref.shape[0]):
        rows, grads = [], []
        for s in range(x_ref.shape[0]):
            chosen = slot_matrix(slot_ref[j, s], capacity)
            one_hot = jnp.where(chosen, 1.0, 0.0).astype(bf16)
            weight = jnp.sum(jnp.where(chosen, gate_ref[j, s], 0.0), axis=1, keepdims=True)
            rows.append(dot(one_hot, x_ref[s]))
            grads.append(weight * dot(one_hot, cot_ref[s]))
        taken = stack(rows).astype(bf16)
        in_ref[j] = taken
        gr_ref[j] = stack(grads).astype(bf16)
        gate_in = dot(taken, wg_ref[j])
        up_in = dot(taken, wu_ref[j])
        g_ref[j] = gate_in
        u_ref[j] = up_in
        act_ref[j] = (gate_in * jax.nn.sigmoid(gate_in) * up_in).astype(bf16)


def step_rows(groups):
    return 2 if groups % 2 == 0 else 1


def expert_forward(mlp_all, cot_all, slot_of, gates, w_gate, w_up, capacity):
    groups, tok_rows, width = mlp_all.shape
    local, _, ff = w_gate.shape
    seqs = step_rows(groups)
    slots = seqs * capacity
    tok = pl.BlockSpec((seqs, tok_rows, width), lambda i: (i, 0, 0))
    route = pl.BlockSpec((local, seqs, 1, tok_rows), lambda i: (0, i, 0, 0))
    weight = pl.BlockSpec((local, width, ff), lambda i: (0, 0, 0), pipeline_mode=pl.Buffered(1))
    wide = pl.BlockSpec((local, slots, width), lambda i: (0, i, 0))
    slim = pl.BlockSpec((local, slots, ff), lambda i: (0, i, 0))
    total = groups * capacity
    return pl.pallas_call(
        functools.partial(expert_in_kernel, capacity),
        out_shape=[
            jax.ShapeDtypeStruct((local, total, width), bf16),
            jax.ShapeDtypeStruct((local, total, width), bf16),
            jax.ShapeDtypeStruct((local, total, ff), bf16),
            jax.ShapeDtypeStruct((local, total, ff), f32),
            jax.ShapeDtypeStruct((local, total, ff), f32),
        ],
        grid=(groups // seqs,),
        in_specs=[tok, tok, route, route, weight, weight],
        out_specs=[wide, wide, slim, slim, slim],
        compiler_params=pltpu.CompilerParams(vmem_limit_bytes=60 << 20),
        cost_estimate=small_cost,
        name="expert_forward",
    )(mlp_all, cot_all, slot_of[:, :, None, :], gates[:, :, None, :], w_gate, w_up)


def expert_out_kernel(capacity, act_ref, cot_ref, slot_ref, gate_ref, wd_ref, sum_ref, gg_ref):
    parts = [None] * cot_ref.shape[0]
    for j in range(wd_ref.shape[0]):
        out = dot(act_ref[j], wd_ref[j])
        for s in range(cot_ref.shape[0]):
            one_hot = jnp.where(slot_matrix(slot_ref[j, s], capacity), 1.0, 0.0).astype(bf16)
            here = dot(one_hot, out[s * capacity : (s + 1) * capacity].astype(bf16), 0, 0)
            gg_ref[j, s] = jnp.sum(here * cot_ref[s].astype(f32), axis=1, keepdims=True)
            term = gate_ref[j, s] * here
            parts[s] = term if j == 0 else parts[s] + term
    for s in range(cot_ref.shape[0]):
        sum_ref[s] = parts[s].astype(bf16)


def expert_combine(act, cot_all, slot_of, gates, w_down, capacity):
    groups, tok_rows, width = cot_all.shape
    local, ff, _ = w_down.shape
    seqs = step_rows(groups)
    tok = pl.BlockSpec((seqs, tok_rows, width), lambda i: (i, 0, 0))
    route = pl.BlockSpec((local, seqs, 1, tok_rows), lambda i: (0, i, 0, 0))
    column = pl.BlockSpec((local, seqs, tok_rows, 1), lambda i: (0, i, 0, 0))
    weight = pl.BlockSpec((local, ff, width), lambda i: (0, 0, 0), pipeline_mode=pl.Buffered(1))
    slim = pl.BlockSpec((local, seqs * capacity, ff), lambda i: (0, i, 0))
    return pl.pallas_call(
        functools.partial(expert_out_kernel, capacity),
        out_shape=[
            jax.ShapeDtypeStruct((groups, tok_rows, width), bf16),
            jax.ShapeDtypeStruct((local, groups, tok_rows, 1), f32),
        ],
        grid=(groups // seqs,),
        in_specs=[slim, tok, route, column, weight],
        out_specs=[tok, column],
        compiler_params=pltpu.CompilerParams(vmem_limit_bytes=60 << 20),
        cost_estimate=small_cost,
        name="expert_combine",
    )(act, cot_all, slot_of[:, :, None, :], gates[:, :, :, None], w_down)


def expert_back_kernel(capacity, gr_ref, g_ref, u_ref, slot_ref, wg_ref, wu_ref, wd_ref, gg_ref, gu_ref, part_ref):
    seqs = part_ref.shape[0]
    parts = [None] * seqs
    for j in range(wd_ref.shape[0]):
        grad_act = dot(gr_ref[j], wd_ref[j], 1, 1)
        gate_in = g_ref[j]
        sigma = jax.nn.sigmoid(gate_in)
        grad_up = (grad_act * (gate_in * sigma)).astype(bf16)
        grad_gate = (grad_act * u_ref[j] * sigma * (1.0 + gate_in * (1.0 - sigma))).astype(bf16)
        gg_ref[j] = grad_gate
        gu_ref[j] = grad_up
        rows = dot(grad_gate, wg_ref[j], 1, 1) + dot(grad_up, wu_ref[j], 1, 1)
        for s in range(seqs):
            one_hot = jnp.where(slot_matrix(slot_ref[j, s], capacity), 1.0, 0.0).astype(bf16)
            term = dot(one_hot, rows[s * capacity : (s + 1) * capacity].astype(bf16), 0, 0)
            parts[s] = term if j == 0 else parts[s] + term
    for s in range(seqs):
        part_ref[s] = parts[s].astype(bf16)


def expert_back(grad_recv, gate_in, up_in, slot_of, w_gate, w_up, w_down, groups, tok_rows, capacity):
    local, width, ff = w_gate.shape
    seqs = step_rows(groups)
    slots = seqs * capacity
    total = groups * capacity
    tok = pl.BlockSpec((seqs, tok_rows, width), lambda i: (i, 0, 0))
    route = pl.BlockSpec((local, seqs, 1, tok_rows), lambda i: (0, i, 0, 0))
    once = pl.Buffered(1)
    weight = pl.BlockSpec((local, width, ff), lambda i: (0, 0, 0), pipeline_mode=once)
    down = pl.BlockSpec((local, ff, width), lambda i: (0, 0, 0), pipeline_mode=once)
    wide = pl.BlockSpec((local, slots, width), lambda i: (0, i, 0))
    slim = pl.BlockSpec((local, slots, ff), lambda i: (0, i, 0))
    return pl.pallas_call(
        functools.partial(expert_back_kernel, capacity),
        out_shape=[
            jax.ShapeDtypeStruct((local, total, ff), bf16),
            jax.ShapeDtypeStruct((local, total, ff), bf16),
            jax.ShapeDtypeStruct((groups, tok_rows, width), bf16),
        ],
        grid=(groups // seqs,),
        in_specs=[wide, slim, slim, route, weight, weight, down],
        out_specs=[slim, slim, tok],
        compiler_params=pltpu.CompilerParams(vmem_limit_bytes=63 << 20),
        cost_estimate=small_cost,
        name="expert_back",
    )(grad_recv, gate_in, up_in, slot_of[:, :, None, :], w_gate, w_up, w_down)


def pad_rows(flat, tile):
    rows = -(-flat.shape[0] // (128 * tile)) * tile
    return jnp.pad(flat, (0, rows * 128 - flat.shape[0])).reshape(rows, 128)


def einf(spec, left, right):
    return jnp.einsum(spec, left, right, preferred_element_type=f32)


def body(
    tokens,
    cotangent,
    lengths,
    deal_order,
    routes,
    balance_coef,
    w_query,
    w_key,
    w_value,
    w_out,
    w_router,
    attn_gain,
    mlp_gain,
    query_gain,
    key_gain,
    w_gate,
    w_up,
    w_down,
):
    groups = lax.axis_size("expert")
    replicas = lax.axis_size("dp")
    me = lax.axis_index("expert")
    tok_rows, width = tokens.shape
    block_rows = tok_rows // replicas
    total_slots = float(tok_rows * replicas * groups)
    shard_rows = w_query.shape[0]
    local_experts = w_gate.shape[0]
    experts = local_experts * groups
    top_k = routes.shape[1]
    capacity = tok_rows * top_k * 9 // (8 * experts)

    order_row = lax.dynamic_index_in_dim(deal_order, me, 0, keepdims=False)
    dp_ids = jnp.arange(replicas, dtype=jnp.int32)
    matched = (order_row[:, None] == dp_ids[None, :]).astype(jnp.int32)
    inverse_order = jnp.sum(matched * dp_ids[:, None], axis=0)

    def blocks_to_deal(values):
        return values.reshape(replicas, block_rows, width)[inverse_order]

    def undeal(values):
        back = lax.all_to_all(
            values.reshape(replicas, block_rows, width), "dp", split_axis=0, concat_axis=0, tiled=True
        )
        return back[order_row].reshape(tok_rows, width)

    small = jnp.concatenate(
        [w_router.reshape(-1), attn_gain, mlp_gain, query_gain, key_gain]
    )
    ints = jnp.concatenate([routes.reshape(-1), jnp.broadcast_to(lengths, (top_k,))])
    small_all, ints_all, seq_tokens, w_qkv = front(
        groups,
        replicas,
        0,
        pad_rows(small, 16),
        pad_rows(ints, 8),
        blocks_to_deal(tokens),
        w_query,
        w_key,
        w_value,
    )
    small_all, ints_all = small_all.reshape(groups, -1), ints_all.reshape(groups, -1)
    w_qkv = w_qkv.reshape(width, -1)
    n_router = shard_rows * experts
    cuts = [0, n_router]
    for gain in (attn_gain, mlp_gain, query_gain, key_gain):
        cuts.append(cuts[-1] + gain.shape[0])
    router_full = small_all[:, :n_router].reshape(width, experts)
    attn_g, mlp_g, query_g, key_g = (
        small_all[:, cuts[i] : cuts[i + 1]].reshape(-1).astype(f32) for i in range(1, 5)
    )
    head_dim = query_g.shape[0]
    local_width = w_query.shape[1] // groups

    routes_all = ints_all[:, : tok_rows * top_k].reshape(groups, tok_rows, top_k)
    lengths_all = ints_all[:, tok_rows * top_k]
    positions = jnp.arange(tok_rows, dtype=jnp.int32)
    live_all = (positions[None, :] < lengths_all[:, None]).astype(f32)
    live_rows = (positions < lengths[0]).astype(f32)

    wo_full = lax.all_gather(w_out, "expert", axis=0, tiled=True)

    inputs = seq_tokens.astype(f32)
    normed, inv_first = norm_fwd(inputs, attn_g)
    attn_in = normed.astype(bf16)
    attn_all, seq_cot = gather_rows(attn_in, groups, 1, blocks=blocks_to_deal(cotangent))
    grad_output = seq_cot.astype(f32) * live_rows[:, None]
    cot_all = lax.all_gather(grad_output.astype(bf16), "expert", axis=0, tiled=False)

    cosine, signed_sine = rotary_tables(tok_rows, head_dim)
    mixed = attend(lengths_all, attn_all, w_qkv, query_g, key_g, cosine, signed_sine)
    mixed_here = lax.all_to_all(mixed, "expert", split_axis=0, concat_axis=0, tiled=True)
    hidden = inputs + einf("xtm,xmd->td", mixed_here, wo_full.reshape(groups, local_width, width))
    mlp_normed, inv_second = norm_fwd(hidden, mlp_g)
    mlp_in = mlp_normed.astype(bf16)
    mlp_all = gather_rows(mlp_in, groups, 2)

    logits = einf("std,de->ste", mlp_all, router_full)
    router = jax.nn.softmax(logits, axis=-1)
    expert_ids = jnp.arange(experts, dtype=jnp.int32)
    picked = jnp.sum(
        (routes_all[:, :, :, None] == expert_ids).astype(f32), axis=2
    )
    chosen_sum = jnp.sum(picked * router, axis=-1, keepdims=True)
    gates = picked * router / chosen_sum
    counts = jnp.sum(picked * live_all[:, :, None], axis=(0, 1))
    prob_sums = jnp.sum(router * live_all[:, :, None], axis=(0, 1))
    live_count = jnp.sum(live_all)[None]
    stats = pad_rows(jnp.concatenate([counts, prob_sums, live_count]), 8)

    first = me * local_experts
    own_picked = lax.dynamic_slice_in_dim(picked, first, local_experts, 2)
    own_gates = lax.dynamic_slice_in_dim(gates, first, local_experts, 2)
    before = (positions[:, None] > positions[None, :]).astype(bf16)
    rank = einf("tu,suj->jst", before, own_picked.astype(bf16))
    own_picked = own_picked.transpose(2, 0, 1)
    own_gates = own_gates.transpose(2, 0, 1)
    slot_of = jnp.where(own_picked > 0.5, rank.astype(jnp.int32), -1)
    expert_in, grad_recv, act_low, gate_in, up_in = expert_forward(
        mlp_all, cot_all, slot_of, own_gates, w_gate, w_up, capacity
    )
    grad_down_w = einf("jrf,jrd->jfd", act_low, grad_recv)
    act_low, grad_recv, grad_down_w = lax.optimization_barrier(
        (act_low, grad_recv, grad_down_w.astype(bf16))
    )
    total_down = lax.psum_scatter(grad_down_w, "dp", scatter_dimension=1, tiled=True).astype(f32)
    grad_gate_in, grad_up_in, grad_part = expert_back(
        grad_recv, gate_in, up_in, slot_of, w_gate, w_up, w_down, groups, tok_rows, capacity
    )
    grad_gate_w = einf("jrd,jrf->jdf", expert_in, grad_gate_in)
    grad_up_w = einf("jrd,jrf->jdf", expert_in, grad_up_in)
    grad_part, act_low, grad_gate_w, grad_up_w = lax.optimization_barrier(
        (grad_part, act_low, grad_gate_w.astype(bf16), grad_up_w.astype(bf16))
    )
    total_gate, total_up = (
        lax.psum_scatter(value, "dp", scatter_dimension=1, tiled=True).astype(f32)
        for value in (grad_gate_w, grad_up_w)
    )
    sum_part, own_grad_gates = expert_combine(act_low, cot_all, slot_of, own_gates, w_down, capacity)
    gate_rows = own_grad_gates.transpose(1, 0, 2, 3).reshape(groups, -1, 128)
    grad_mlp_in, gate_back, sums = scatter_sum(
        grad_part, groups, 3, replicas=replicas, riders=(gate_rows, stats)
    )
    sums = sums.reshape(-1)
    counts, prob_sums = sums[:experts], sums[experts : 2 * experts]
    live_count = sums[2 * experts : 2 * experts + 1]
    fraction = counts / (live_count * top_k)
    balance_loss = balance_coef * (experts * jnp.sum(fraction * prob_sums / total_slots))

    grad_gates = gate_back.reshape(experts, tok_rows).T
    my_router = lax.dynamic_index_in_dim(router, me, 0, keepdims=False)
    my_picked = lax.dynamic_index_in_dim(picked, me, 0, keepdims=False)
    my_gates = lax.dynamic_index_in_dim(gates, me, 0, keepdims=False)
    my_sum = lax.dynamic_index_in_dim(chosen_sum, me, 0, keepdims=False)
    grad_prob = (
        my_picked * (grad_gates - jnp.sum(grad_gates * my_gates, axis=1, keepdims=True)) / my_sum
        + live_rows[:, None] * (balance_coef * experts / total_slots) * fraction[None, :]
    )
    grad_logits = (
        my_router * (grad_prob - jnp.sum(my_router * grad_prob, axis=-1, keepdims=True))
    ).astype(bf16)
    grad_router_w = einf("td,te->de", mlp_in, grad_logits)
    grad_mlp_in = grad_mlp_in + einf("te,de->td", grad_logits, router_full)

    grad_hidden_norm, grad_mlp_g = norm_back(hidden, inv_second, mlp_g, grad_mlp_in, 0)
    grad_hidden = grad_output + grad_hidden_norm
    grad_hidden_low = grad_hidden.astype(bf16)
    grad_hidden_low, total_down = lax.optimization_barrier((grad_hidden_low, total_down))
    hidden_all = gather_rows(grad_hidden_low, groups, 4)
    grad_attn_part, grad_qkv_w, grad_out_w, grad_gains = attend_back(
        lengths_all, attn_all, hidden_all, mixed, w_qkv, w_out, query_g, key_g, cosine, signed_sine
    )
    grad_query_g, grad_key_g = grad_gains[0], grad_gains[1]
    grad_attn_in = scatter_sum(grad_attn_part, groups, 5)
    w_back = lax.all_to_all(
        grad_qkv_w.reshape(groups, shard_rows, 3 * local_width),
        "expert",
        split_axis=0,
        concat_axis=0,
        tiled=True,
    )
    attn_w = jnp.concatenate(
        [
            w_back[:, :, i * local_width : (i + 1) * local_width]
            .transpose(1, 0, 2)
            .reshape(shard_rows, groups * local_width)
            for i in range(3)
        ]
        + [grad_out_w],
        axis=0,
    )
    attn_w, total_up = lax.optimization_barrier((attn_w, total_up))
    attn_sum = lax.psum(attn_w, "dp").astype(f32)
    sum_q, sum_k, sum_v, sum_o = (
        attn_sum[i * shard_rows : (i + 1) * shard_rows] for i in range(4)
    )

    grad_attn_in, total_gate = lax.optimization_barrier((grad_attn_in, total_gate))
    grad_input_norm, grad_attn_g = norm_back(inputs, inv_first, attn_g, grad_attn_in, 0)
    grad_input = undeal((grad_hidden + grad_input_norm).astype(bf16)).astype(f32)

    sum_part, grad_input = lax.optimization_barrier((sum_part, grad_input))
    expert_sum = scatter_sum(sum_part, groups, 6)
    output = undeal((live_rows[:, None] * (hidden + expert_sum)).astype(bf16))

    pieces = [grad_router_w.reshape(groups, n_router)] + [
        value.reshape(groups, -1) for value in (grad_attn_g, grad_mlp_g, grad_query_g, grad_key_g)
    ]
    pieces = jnp.concatenate(pieces, axis=1)
    n_small = pieces.shape[1]
    pad = -n_small % 1024
    pieces = jnp.pad(pieces, ((0, 0), (0, pad))).reshape(groups, -1, 128)
    sum_small = small_sum(pieces, replicas, 7).reshape(-1)
    sum_r = sum_small[:n_router].reshape(shard_rows, experts)
    sum_ga, sum_gm, sum_gq, sum_gk = (sum_small[cuts[i] : cuts[i + 1]] for i in range(1, 5))
    return (
        output,
        balance_loss,
        grad_input,
        sum_q,
        sum_k,
        sum_v,
        sum_o,
        sum_r,
        sum_ga,
        sum_gm,
        sum_gq,
        sum_gk,
        total_gate,
        total_up,
        total_down,
    )


def solution(mesh):
    rows = P(("dp", "expert"), None)
    weight = P("expert", None)
    gain = P("expert")
    cube = P("expert", None, None)
    cube_out = P("expert", "dp", None)
    return jax.shard_map(
        body,
        mesh=mesh,
        in_specs=(
            (rows, rows, P(("dp", "expert")), P(), rows, P())
            + (weight,) * 5
            + (gain,) * 4
            + (cube,) * 3
        ),
        out_specs=(
            (rows, P(), rows) + (weight,) * 5 + (gain,) * 4 + (cube_out,) * 3
        ),
        check_vma=False,
    )
```

```python
import functools
import math

import jax
import jax.numpy as jnp
from jax import lax
from jax.experimental import pallas as pl
from jax.experimental.pallas import tpu as pltpu
from jax.sharding import PartitionSpec as P

norm_eps = 1e-06
rope_base = 50000.0
big_negative = -1e30
bf16 = jnp.bfloat16
f32 = jnp.float32
MESH = pl.DeviceIdType.MESH
DMA = pltpu.SemaphoreType.DMA
kernel_vmem = 62 << 20
small_cost = pl.CostEstimate(flops=0, transcendentals=0, bytes_accessed=1024)


def norm_fwd(values, scales):
    inverse = lax.rsqrt(jnp.mean(values * values, axis=-1, keepdims=True) + norm_eps)
    return (values * inverse * scales, inverse)


def norm_back(values, inverse, scales, grad_out, sum_axes):
    scaled = grad_out * scales
    grad_in = inverse * (
        scaled - values * inverse * inverse * jnp.mean(scaled * values, axis=-1, keepdims=True)
    )
    grad_scale = jnp.sum(grad_out * values * inverse, axis=sum_axes)
    return (grad_in, grad_scale)


def rotary_tables(tok_rows, head_dim):
    half_dim = head_dim // 2
    positions = jnp.arange(tok_rows, dtype=jnp.int32).astype(f32)
    frequency = rope_base ** (-jnp.arange(half_dim, dtype=jnp.int32).astype(f32) * 2.0 / head_dim)
    angles = positions[:, None] * frequency[None, :]
    cosine = jnp.concatenate([jnp.cos(angles), jnp.cos(angles)], axis=-1)
    signed_sine = jnp.concatenate([-jnp.sin(angles), jnp.sin(angles)], axis=-1)
    return (cosine, signed_sine)


def peer(index):
    return {"expert": index}


def remote(src, dst, send, recv, to):
    return pltpu.make_async_remote_copy(
        src_ref=src, dst_ref=dst, send_sem=send, recv_sem=recv, device_id=peer(to), device_id_type=MESH
    )


def greet(n, me, replicas=1):
    barrier = pltpu.get_barrier_semaphore()
    for k in range(1, n):
        pl.semaphore_signal(
            barrier, inc=1, device_id=peer(lax.rem(me + k, n)), device_id_type=MESH
        )
    for k in range(1, replicas):
        other = lax.rem(lax.axis_index("dp") + k, replicas)
        pl.semaphore_signal(barrier, inc=1, device_id={"dp": other}, device_id_type=MESH)
    pl.semaphore_wait(barrier, n + replicas - 2)


def quad_places(me):
    core = lax.rem(me, 2)
    chip = me // 2
    x = lax.rem(chip, 2)
    y = chip // 2

    def at(px, py, pc):
        return (py * 2 + px) * 2 + pc

    spots = ((x, y), (1 - x, y), (x, 1 - y), (1 - x, 1 - y))
    return [at(px, py, core) for px, py in spots], [at(px, py, 1 - core) for px, py in spots]


def any_places(n, me):
    core = lax.rem(me, 2)
    chip = me // 2
    chips = n // 2
    chip_of = [lax.rem(chip + k, chips) for k in range(chips)]
    chip_from = [lax.rem(chip - k + chips, chips) for k in range(chips)]
    return (
        [c * 2 + core for c in chip_of],
        [c * 2 + 1 - core for c in chip_of],
        [c * 2 + core for c in chip_from],
        [c * 2 + 1 - core for c in chip_from],
    )


def deal_copies(replicas, src, dst, own_sem, send_sem, recv_sem):
    here = lax.axis_index("dp")
    rows = src.shape[1]
    mine = pl.ds(here * rows, rows)
    own = pltpu.make_async_copy(src.at[here], dst.at[mine], own_sem)
    away = []
    for k in range(1, replicas):
        to = lax.rem(here + k, replicas)
        away.append(
            pltpu.make_async_remote_copy(
                src_ref=src.at[to],
                dst_ref=dst.at[mine],
                send_sem=send_sem.at[k],
                recv_sem=recv_sem.at[k],
                device_id={"dp": to},
                device_id_type=MESH,
            )
        )
    return own, away


def front_kernel(
    n,
    replicas,
    small,
    ints,
    blocks,
    wq,
    wk,
    wv,
    small_all,
    ints_all,
    seq,
    w_all,
    small_send,
    small_recv,
    own_sem,
    deal_send,
    deal_recv,
    w_own,
    w_send,
    w_recv,
):
    me = lax.axis_index("expert")
    wide = wq.shape[1] // n
    small_all[me] = small[...]
    ints_all[me] = ints[...]
    own, away = deal_copies(replicas, blocks, seq, own_sem, deal_send, deal_recv)
    own.start()

    def columns(weight, index):
        return weight.at[:, pl.ds(pl.multiple_of(index * wide, wide), wide)]

    kept = []
    for i, weight in enumerate((wq, wk, wv)):
        copy = pltpu.make_async_copy(
            columns(weight, me), w_all.at[me, :, pl.ds(i * wide, wide)], w_own.at[i]
        )
        copy.start()
        kept.append(copy)
    greet(n, me, replicas)
    copies = []

    def go(copy):
        copy.start()
        copies.append(copy)

    for k in range(1, n):
        to = lax.rem(me + k, n)
        go(remote(small, small_all.at[me], small_send.at[0, k], small_recv.at[0, k], to))
        go(remote(ints, ints_all.at[me], small_send.at[1, k], small_recv.at[1, k], to))
    for copy in away:
        go(copy)
    for k in range(1, n):
        to = lax.rem(me + k, n)
        for i, weight in enumerate((wq, wk, wv)):
            go(
                remote(
                    columns(weight, to),
                    w_all.at[me, :, pl.ds(i * wide, wide)],
                    w_send.at[i, k],
                    w_recv.at[i, k],
                    to,
                )
            )
    for copy in copies:
        copy.wait()
    own.wait()
    for copy in kept:
        copy.wait()


def front(n, replicas, collective_id, small, ints, blocks, wq, wk, wv):
    vmem = pl.BlockSpec(memory_space=pltpu.VMEM)
    away = pl.BlockSpec(memory_space=pl.ANY)
    rows, width = wq.shape
    return pl.pallas_call(
        functools.partial(front_kernel, n, replicas),
        out_shape=[
            jax.ShapeDtypeStruct((n,) + small.shape, small.dtype),
            jax.ShapeDtypeStruct((n,) + ints.shape, ints.dtype),
            jax.ShapeDtypeStruct((replicas * blocks.shape[1], width), bf16),
            jax.ShapeDtypeStruct((n, rows, 3 * (width // n)), bf16),
        ],
        in_specs=[vmem, vmem, away, away, away, away],
        out_specs=[vmem, vmem, away, away],
        scratch_shapes=[
            DMA((2, n)),
            DMA((2, n)),
            DMA,
            DMA((replicas,)),
            DMA((replicas,)),
            DMA((3,)),
            DMA((3, n)),
            DMA((3, n)),
        ],
        compiler_params=pltpu.CompilerParams(
            collective_id=collective_id, has_side_effects=True, vmem_limit_bytes=kernel_vmem
        ),
        cost_estimate=small_cost,
        name="front",
    )(small, ints, blocks, wq, wk, wv)


VMEM_SPEC = pl.BlockSpec(memory_space=pltpu.VMEM)
AWAY_SPEC = pl.BlockSpec(memory_space=pl.ANY)


def along_dp(src, dst, send, recv, to):
    return pltpu.make_async_remote_copy(
        src_ref=src, dst_ref=dst, send_sem=send, recv_sem=recv, device_id={"dp": to}, device_id_type=MESH
    )


class Exchange:
    over_dp = False

    def __init__(self, x, n, replicas, columns=None):
        self.n = n
        self.columns = columns or x.shape[2]
        self.ins = [(x, VMEM_SPEC)]
        self.outs = [(jax.ShapeDtypeStruct(x.shape, x.dtype), VMEM_SPEC)]
        self.scratch = [DMA((n,)), DMA((n,))]

    def start(self, me, src, out, send, recv):
        cols = pl.ds(0, self.columns)
        self.copies = []
        for k in range(1, self.n):
            to = lax.rem(me + k, self.n)
            self.copies.append(
                remote(src.at[to, :, cols], out.at[me, :, cols], send.at[k], recv.at[k], to)
            )
            self.copies[-1].start()
        out[me, :, : self.columns] = src[me, :, : self.columns]
        if self.columns < src.shape[2]:
            out[:, :, self.columns :] = src[:, :, self.columns :]

    def finish(self, me, *refs):
        for copy in self.copies:
            copy.wait()


class DpSum:
    over_dp = True

    def __init__(self, x, n, replicas):
        self.replicas = replicas
        self.ins = [(x, VMEM_SPEC)]
        self.outs = [(jax.ShapeDtypeStruct(x.shape, x.dtype), VMEM_SPEC)]
        self.scratch = [pltpu.VMEM((replicas,) + x.shape, x.dtype), DMA((replicas,)), DMA((replicas,))]

    def start(self, me, src, out, got, send, recv):
        here = lax.axis_index("dp")
        got[here] = src[...]
        self.copies = []
        for k in range(1, self.replicas):
            to = lax.rem(here + k, self.replicas)
            self.copies.append(along_dp(src, got.at[here], send.at[k], recv.at[k], to))
            self.copies[-1].start()

    def finish(self, me, src, out, got, send, recv):
        for copy in self.copies:
            copy.wait()
        value = got[0]
        for k in range(1, self.replicas):
            value = value + got[k]
        out[...] = value


class SmallSum:
    over_dp = True

    def __init__(self, x, n, replicas):
        self.n, self.replicas = n, replicas
        shape = x.shape[1:]
        self.ins = [(x, VMEM_SPEC)]
        self.outs = [(jax.ShapeDtypeStruct(shape, f32), VMEM_SPEC)]
        self.scratch = [pltpu.VMEM(x.shape, f32), pltpu.VMEM((replicas,) + shape, f32)]
        self.scratch += [DMA((n,)), DMA((n,)), DMA((replicas,)), DMA((replicas,))]

    def start(self, me, src, out, got, total, send, recv, over_send, over_recv):
        got[me] = src[me]
        self.copies = []
        for k in range(1, self.n):
            to = lax.rem(me + k, self.n)
            self.copies.append(remote(src.at[to], got.at[me], send.at[k], recv.at[k], to))
            self.copies[-1].start()

    def finish(self, me, src, out, got, total, send, recv, over_send, over_recv):
        here = lax.axis_index("dp")
        for copy in self.copies:
            copy.wait()
        value = got[0]
        for k in range(1, self.n):
            value = value + got[k]
        total[here] = value
        copies = []
        for k in range(1, self.replicas):
            to = lax.rem(here + k, self.replicas)
            copies.append(along_dp(total.at[here], total.at[here], over_send.at[k], over_recv.at[k], to))
            copies[-1].start()
        for copy in copies:
            copy.wait()
        value = total[0]
        for k in range(1, self.replicas):
            value = value + total[k]
        out[...] = value


class Deal:
    over_dp = True

    def __init__(self, blocks, n, replicas):
        self.replicas = replicas
        _, rows, width = blocks.shape
        self.ins = [(blocks, AWAY_SPEC)]
        self.outs = [(jax.ShapeDtypeStruct((replicas * rows, width), blocks.dtype), AWAY_SPEC)]
        self.scratch = [DMA, DMA((replicas,)), DMA((replicas,))]

    def start(self, me, src, out, own, send, recv):
        kept, away = deal_copies(self.replicas, src, out, own, send, recv)
        kept.start()
        for copy in away:
            copy.start()
        self.copies = away + [kept]

    def finish(self, me, *refs):
        for copy in self.copies:
            copy.wait()


class DpGather:
    over_dp = True

    def __init__(self, x, n, replicas, parts=4):
        self.replicas, self.parts = replicas, parts
        self.size = x.shape[0] // parts
        self.ins = [(x, AWAY_SPEC)]
        self.outs = [(jax.ShapeDtypeStruct((replicas,) + x.shape, x.dtype), AWAY_SPEC)]
        self.scratch = [DMA, DMA((2, replicas, parts)), DMA((2, replicas, parts))]

    def piece(self, p):
        return pl.ds(p * self.size, self.size)

    def hop(self, src, out, send, recv, way, k, p):
        here = lax.axis_index("dp")
        step = 1 - 2 * way
        block = out.at[here - step * k, self.piece(p)]
        origin = block if k else src.at[self.piece(p)]
        return along_dp(origin, block, send.at[way, k, p], recv.at[way, k, p], here + step)

    def sends(self, way, k):
        here = lax.axis_index("dp")
        last = self.replicas - 1
        if way == 0:
            return (here >= k) & (here < last), here >= k + 1
        return (here + k <= last) & (here > 0), here + k + 1 <= last

    def start(self, me, src, out, own, send, recv):
        self.copy = pltpu.make_async_copy(src, out.at[lax.axis_index("dp")], own)
        self.copy.start()
        for way in range(2):

            @pl.when(self.sends(way, 0)[0])
            def _():
                for p in range(self.parts):
                    self.hop(src, out, send, recv, way, 0, p).start()

    def steps(self, src, out, own, send, recv):
        here = lax.axis_index("dp")
        for k in range(self.replicas - 1):
            for p in range(self.parts):
                for way in range(2):

                    @pl.when(self.sends(way, k)[1])
                    def _():
                        block = out.at[here - (1 - 2 * way) * (k + 1), self.piece(p)]
                        along_dp(
                            block, block, send.at[way, k, p], recv.at[way, k, p], here
                        ).wait_recv()

                    if k + 1 < self.replicas - 1:

                        @pl.when(self.sends(way, k + 1)[0])
                        def _():
                            self.hop(src, out, send, recv, way, k + 1, p).start()

                yield

        for k in range(self.replicas - 1):
            for way in range(2):

                @pl.when(self.sends(way, k)[0])
                def _():
                    for p in range(self.parts):
                        self.hop(src, out, send, recv, way, k, p).wait_send()

        self.copy.wait()


class LineSum:
    over_dp = True

    def __init__(self, x, n, replicas, parts=4):
        self.replicas, self.parts = replicas, parts
        self.blocks, rows, columns = x.shape
        self.rows = rows // replicas
        self.size = self.rows // parts
        held = pltpu.VMEM((replicas, self.blocks, self.rows, columns), bf16)
        self.ins = [(x, AWAY_SPEC)]
        self.outs = [(jax.ShapeDtypeStruct((self.blocks, self.rows, columns), f32), VMEM_SPEC)]
        sems = DMA((2, replicas, parts))
        self.scratch = [held, held, held, DMA((replicas, parts)), sems, sems]

    def load(self, x, own, sem, c, p):
        rows = pl.ds(pl.multiple_of(c * self.rows + p * self.size, self.size), self.size)
        return pltpu.make_async_copy(
            x.at[:, rows], own.at[c, :, pl.ds(p * self.size, self.size)], sem.at[c, p]
        )

    def hop(self, own, got, send, recv, way, c, p):
        here = lax.axis_index("dp")
        rows = pl.ds(p * self.size, self.size)
        return along_dp(
            own.at[c, :, rows],
            got.at[c, :, rows],
            send.at[way, c, p],
            recv.at[way, c, p],
            here + 1 - 2 * way,
        )

    def add(self, total, got, c, p, widen=None):
        chunk = min(self.size, 32)
        for b in range(self.blocks):

            @pl.loop(0, self.size // chunk)
            def _(i):
                rows = pl.ds(p * self.size + i * chunk, chunk)
                if widen is None:
                    value = total[c, b, rows].astype(f32) + got[c, b, rows].astype(f32)
                    total[c, b, rows] = value.astype(bf16)
                elif got is None:
                    widen[b, rows] = total[c, b, rows].astype(f32)
                else:
                    widen[b, rows] = widen[b, rows] + got[c, b, rows].astype(f32)

    def start(self, me, x, out, own, up, down, loads, send, recv):
        for t in range(self.replicas):
            for p in range(self.parts):
                self.load(x, own, loads, t, p).start()

    def steps(self, x, out, own, up, down, loads, send, recv):
        here = lax.axis_index("dp")
        last = self.replicas - 1
        for t in range(last):
            for p in range(self.parts):
                for way, c, got in ((0, last - t, up), (1, t, down)):
                    bound = here < c if way == 0 else here > c
                    inner = here > 0 if way == 0 else here < last

                    @pl.when(bound)
                    def _():
                        self.load(x, own, loads, c, p).wait()

                        @pl.when(inner)
                        def _():
                            self.hop(own, got, send, recv, way, c, p).wait_recv()
                            self.add(own, got, c, p)

                        self.hop(own, got, send, recv, way, c, p).start()

                yield
        for p in range(self.parts):
            self.load(x, own, loads, here, p).wait()
            self.add(own, None, here, p, out)
            for way, got, inner in ((0, up, here > 0), (1, down, here < last)):

                @pl.when(inner)
                def _():
                    self.hop(own, got, send, recv, way, here, p).wait_recv()
                    self.add(own, got, here, p, out)

        for t in range(last):
            for p in range(self.parts):
                for way, c, got in ((0, last - t, up), (1, t, down)):

                    @pl.when(here < c if way == 0 else here > c)
                    def _():
                        self.hop(own, got, send, recv, way, c, p).wait_send()


def close_kernel(exchange, gather, line, meet, share, x, full, out, rows, *refs):
    swap_refs, refs = refs[:2], refs[2:]
    gather_refs, line_refs = refs[: len(gather.scratch)], refs[len(gather.scratch) :]
    me = lax.axis_index("expert")
    line.start(me, x, out, *line_refs)
    meet(me)
    exchange.start(me, share, rows, *swap_refs)
    running = [line.steps(x, out, *line_refs)]
    next(running[0])
    exchange.finish(me)
    gather.start(me, rows, full, *gather_refs)
    running.append(gather.steps(rows, full, *gather_refs))
    while running:
        running = [r for r in running if next(r, True) is None]


def close(attn_share, columns, grad_up_w, n, replicas, collective_id, riders):
    exchange = Exchange(attn_share, n, replicas, columns)
    gather = DpGather(attn_share, n, replicas)
    line = LineSum(grad_up_w, n, replicas)
    return riding_call(
        n,
        replicas,
        functools.partial(close_kernel, exchange, gather, line),
        exchange.ins + line.ins,
        gather.outs + line.outs,
        [pltpu.VMEM(attn_share.shape, bf16)] + exchange.scratch + gather.scratch + line.scratch,
        riders,
        collective_id,
        "close",
    )


class SmallGather:
    over_dp = False

    def __init__(self, x, n, replicas):
        self.n = n
        self.ins = [(x, VMEM_SPEC)]
        self.outs = [(jax.ShapeDtypeStruct((n,) + x.shape, x.dtype), VMEM_SPEC)]
        self.scratch = [DMA((n,)), DMA((n,))]

    def start(self, me, src, out, send, recv):
        out[me] = src[...]
        self.copies = []
        for k in range(1, self.n):
            to = lax.rem(me + k, self.n)
            self.copies.append(remote(src, out.at[me], send.at[k], recv.at[k], to))
            self.copies[-1].start()

    def finish(self, me, *refs):
        for copy in self.copies:
            copy.wait()


def riding_kernel(n, replicas, main, counts, riders, *refs):
    n_in, n_out, n_scratch = counts
    at = [0]

    def take(count):
        at[0] += count
        return refs[at[0] - count : at[0]]

    main_in = take(n_in)
    rider_in = [take(len(r.ins)) for r in riders]
    main_out = take(n_out)
    rider_out = [take(len(r.outs)) for r in riders]
    main_scratch = take(n_scratch)
    rider_refs = [i + o + take(len(r.scratch)) for r, i, o in zip(riders, rider_in, rider_out)]

    def meet(me):
        greet(n, me, replicas if any(r.over_dp for r in riders) else 1)
        for rider, own in zip(riders, rider_refs):
            rider.start(me, *own)

    main(meet, *main_in, *main_out, *main_scratch)
    me = lax.axis_index("expert")
    for rider, own in zip(riders, rider_refs):
        rider.finish(me, *own)


def riding_call(n, replicas, main, ins, outs, scratch, riders, collective_id, name):
    pairs_in = ins + [pair for r in riders for pair in r.ins]
    pairs_out = outs + [pair for r in riders for pair in r.outs]
    counts = (len(ins), len(outs), len(scratch))
    return pl.pallas_call(
        functools.partial(riding_kernel, n, replicas, main, counts, riders),
        out_shape=[shape for shape, _ in pairs_out],
        in_specs=[spec for _, spec in pairs_in],
        out_specs=[spec for _, spec in pairs_out],
        scratch_shapes=scratch + [shape for r in riders for shape in r.scratch],
        compiler_params=pltpu.CompilerParams(
            collective_id=collective_id, has_side_effects=True, vmem_limit_bytes=kernel_vmem
        ),
        cost_estimate=small_cost,
        name=name,
    )(*[value for value, _ in pairs_in])


def ride_only(meet, *refs):
    meet(lax.axis_index("expert"))


def quad_gather_kernel(parts, meet, x_ref, o_ref, own_sem, send_sem, recv_sem, pass_sem, pair_send, pair_recv):
    me = lax.axis_index("expert")
    same, other = quad_places(me)
    step = x_ref.shape[0] // parts
    half = parts // 2
    own = pltpu.make_async_copy(x_ref, o_ref.at[me], own_sem)
    own.start()
    meet(me)
    started = []

    def go(copy):
        copy.start()
        started.append(copy)

    def piece(p):
        return pl.ds(p * step, step)

    low, high = list(range(half)), list(range(half, parts))
    turns = [(k, seq[i]) for i in range(parts) for k, seq in ((1, high + low), (2, low + high))]
    for k, p in turns:
        go(remote(x_ref.at[piece(p)], o_ref.at[me, piece(p)], send_sem.at[k, p], recv_sem.at[k, p], same[k]))
    for p in range(parts):
        go(remote(x_ref.at[piece(p)], o_ref.at[me, piece(p)], pair_send.at[0, p], pair_recv.at[0, p], other[0]))

    def arrive(k, p):
        block = o_ref.at[same[k], piece(p)]
        remote(block, block, send_sem.at[k, p], recv_sem.at[k, p], other[0]).wait_recv()
        return block

    for k, p in turns:
        block = arrive(k, p)
        if (p >= half) == (k == 1):
            go(remote(block, block, pass_sem.at[p], recv_sem.at[3, p], same[3 - k]))
        go(remote(block, block, pair_send.at[k, p], pair_recv.at[k, p], other[0]))
    for pair in zip(low, high):
        for p in pair:
            block = arrive(3, p)
            go(remote(block, block, pair_send.at[3, p], pair_recv.at[3, p], other[0]))
    for k in range(4):
        for p in range(parts):
            block = o_ref.at[other[k], piece(p)]
            remote(block, block, pair_send.at[k, p], pair_recv.at[k, p], other[0]).wait_recv()
    for copy in started:
        copy.wait_send()
    own.wait()


def any_gather_kernel(n, meet, x_ref, o_ref, own_sem, send_sem, recv_sem, pair_send, pair_recv):
    me = lax.axis_index("expert")
    same, other, same_from, other_from = any_places(n, me)
    own = pltpu.make_async_copy(x_ref, o_ref.at[me], own_sem)
    own.start()
    meet(me)
    started = []
    for k in range(n // 2):
        if k:
            copy = remote(x_ref, o_ref.at[me], send_sem.at[k], recv_sem.at[k], same[k])
        else:
            copy = remote(x_ref, o_ref.at[me], pair_send.at[0], pair_recv.at[0], other[0])
        copy.start()
        started.append(copy)
    for k in range(1, n // 2):
        block = o_ref.at[same_from[k]]
        remote(block, block, send_sem.at[k], recv_sem.at[k], other[0]).wait_recv()
        copy = remote(block, block, pair_send.at[k], pair_recv.at[k], other[0])
        copy.start()
        started.append(copy)
    for k in range(n // 2):
        block = o_ref.at[other_from[k]]
        remote(block, block, pair_send.at[k], pair_recv.at[k], other[0]).wait_recv()
    for copy in started:
        copy.wait_send()
    own.wait()


def gather_plan(n, parts):
    chips = n // 2
    if n == 8:
        sems = [DMA, DMA((4, parts)), DMA((4, parts)), DMA((parts,)), DMA((4, parts)), DMA((4, parts))]
        return functools.partial(quad_gather_kernel, parts), sems
    sems = [DMA, DMA((chips,)), DMA((chips,)), DMA((chips,)), DMA((chips,))]
    return functools.partial(any_gather_kernel, n), sems


def gather_rows(x, n, replicas, collective_id, riders=(), parts=4):
    kernel, sems = gather_plan(n, parts)
    out = jax.ShapeDtypeStruct((n,) + x.shape, x.dtype)
    return riding_call(
        n,
        replicas,
        kernel,
        [(x, AWAY_SPEC)],
        [(out, AWAY_SPEC)],
        sems,
        list(riders),
        collective_id,
        f"gather_rows_{collective_id}",
    )


def add_rows(total, first, rows, chunk, *terms):
    @pl.loop(0, rows // chunk)
    def _(i):
        s = pl.ds(first + i * chunk, chunk)
        value = terms[0][s].astype(f32)
        for term in terms[1:]:
            value = value + term[s].astype(f32)
        total[s] = value.astype(total.dtype)


def quad_scatter_kernel(
    parts, meet, p_ref, o_ref, mine, theirs, transit, got, load_sem, pair_send, pair_recv, over_send, over_recv, send_sem, recv_sem
):
    me = lax.axis_index("expert")
    same, other = quad_places(me)
    step = p_ref.shape[1] // parts
    half = parts // 2
    low, high = list(range(half)), list(range(half, parts))
    mix = [p for pair in zip(low, high) for p in pair]
    order = (3, 1, 2, 0)

    def piece(p):
        return pl.ds(p * step, step)

    loads = {}
    for k in order:
        for p in mix:
            loads[k, p] = pltpu.make_async_copy(
                p_ref.at[same[k], piece(p)], mine.at[k, piece(p)], load_sem.at[k, p]
            )
            loads[k, p].start()
    meet(me)
    started = []

    def go(copy):
        copy.start()
        started.append(copy)

    for k in order:
        for p in mix:
            go(
                remote(
                    p_ref.at[other[k], piece(p)],
                    theirs.at[k, piece(p)],
                    pair_send.at[k, p],
                    pair_recv.at[k, p],
                    other[0],
                )
            )

    def fold(k, p):
        loads[k, p].wait()
        spot = theirs.at[k, piece(p)]
        remote(spot, spot, pair_send.at[k, p], pair_recv.at[k, p], other[0]).wait_recv()
        add_rows(mine.at[k], p * step, step, 32, mine.at[k], theirs.at[k])

    def ship(k, p):
        go(
            remote(
                mine.at[k, piece(p)],
                got.at[k - 1, piece(p)],
                send_sem.at[k - 1, p],
                recv_sem.at[k - 1, p],
                same[k],
            )
        )

    for p in mix:
        fold(3, p)
        to = same[1] if p < half else same[2]
        go(remote(mine.at[3, piece(p)], transit.at[piece(p)], over_send.at[p], over_recv.at[p], to))
    for a, b in zip(low, high):
        for k, p in ((1, a), (2, b)):
            fold(k, p)
            ship(k, p)
    for a, b in zip(low, high):
        for k, p in ((2, a), (1, b)):
            fold(k, p)
            spot = transit.at[piece(p)]
            remote(spot, spot, over_send.at[p], over_recv.at[p], other[0]).wait_recv()
            add_rows(mine.at[k], p * step, step, 32, mine.at[k], transit)
            ship(k, p)
    for p in mix:
        fold(0, p)
    for p in mix:
        for k in (0, 1):
            spot = got.at[k, piece(p)]
            remote(spot, spot, send_sem.at[k, p], recv_sem.at[k, p], other[0]).wait_recv()
        add_rows(o_ref, p * step, step, 32, mine.at[0], got.at[0], got.at[1])
    for copy in started:
        copy.wait_send()


def any_scatter_kernel(n, meet, p_ref, o_ref, mine, theirs, got, load_sem, pair_send, pair_recv, send_sem, recv_sem):
    me = lax.axis_index("expert")
    same, other, _, _ = any_places(n, me)
    rows = p_ref.shape[1]
    order = list(range(1, n // 2)) + [0]
    loads = {}
    for k in order:
        loads[k] = pltpu.make_async_copy(p_ref.at[same[k]], mine.at[k], load_sem.at[k])
        loads[k].start()
    meet(me)
    started = []
    for k in order:
        copy = remote(p_ref.at[other[k]], theirs.at[k], pair_send.at[k], pair_recv.at[k], other[0])
        copy.start()
        started.append(copy)
    for k in order:
        loads[k].wait()
        remote(theirs.at[k], theirs.at[k], pair_send.at[k], pair_recv.at[k], other[0]).wait_recv()
        add_rows(mine.at[k], 0, rows, 32, mine.at[k], theirs.at[k])
        if k:
            copy = remote(mine.at[k], got.at[k], send_sem.at[k], recv_sem.at[k], same[k])
            copy.start()
            started.append(copy)
    for k in range(1, n // 2):
        remote(got.at[k], got.at[k], send_sem.at[k], recv_sem.at[k], other[0]).wait_recv()
    add_rows(o_ref, 0, rows, 32, mine.at[0], *[got.at[k] for k in range(1, n // 2)])
    for copy in started:
        copy.wait_send()


def scatter_sum(x, n, replicas, collective_id, riders=(), parts=4):
    chips = n // 2
    shape = x.shape[1:]
    blocks = pltpu.VMEM((chips,) + shape, bf16)
    if n == 8:
        kernel = functools.partial(quad_scatter_kernel, parts)
        scratch = [blocks, blocks, pltpu.VMEM(shape, bf16), pltpu.VMEM((2,) + shape, bf16)]
        scratch += [DMA((4, parts))] * 3 + [DMA((parts,))] * 2 + [DMA((2, parts))] * 2
    else:
        kernel = functools.partial(any_scatter_kernel, n)
        scratch = [blocks] * 3 + [DMA((chips,))] * 5
    return riding_call(
        n,
        replicas,
        kernel,
        [(x, AWAY_SPEC)],
        [(jax.ShapeDtypeStruct(shape, f32), VMEM_SPEC)],
        scratch,
        list(riders),
        collective_id,
        f"scatter_sum_{collective_id}",
    )


def dot(left, right, left_dim=1, right_dim=0):
    return lax.dot_general(
        left, right, (((left_dim,), (right_dim,)), ((), ())), preferred_element_type=f32
    )


def head_values(lin, gain, cosine, signed_sine):
    inverse = lax.rsqrt(jnp.mean(lin * lin, axis=-1, keepdims=True) + norm_eps)
    normed = lin * inverse * gain
    half = lin.shape[1] // 2
    turned = normed * cosine + pltpu.roll(normed, half, 1) * signed_sine
    return inverse, turned.astype(bf16)


def head_probs(q_rot, k_rot, length, score_scale):
    scores = dot(q_rot, k_rot, 1, 1) * score_scale
    key = lax.broadcasted_iota(jnp.int32, scores.shape, 1)
    masked = jnp.where(key < length, scores, big_negative)
    raised = jnp.exp(masked - jnp.max(masked, axis=-1, keepdims=True))
    return raised / jnp.sum(raised, axis=-1, keepdims=True)


def attend_kernel(
    heads, head_dim, lengths_ref, x_ref, w_ref, wo_ref, qg_ref, kg_ref, cos_ref, sin_ref, mixed_ref, part_ref
):
    length = lengths_ref[pl.program_id(0)]
    wide = heads * head_dim
    qkv = dot(x_ref[0], w_ref[...])
    for h in range(heads):
        at = h * head_dim
        _, q_rot = head_values(qkv[:, at : at + head_dim], qg_ref[...], cos_ref[...], sin_ref[...])
        _, k_rot = head_values(
            qkv[:, wide + at : wide + at + head_dim], kg_ref[...], cos_ref[...], sin_ref[...]
        )
        v = qkv[:, 2 * wide + at : 2 * wide + at + head_dim].astype(bf16)
        probs = head_probs(q_rot, k_rot, length, 1.0 / math.sqrt(head_dim))
        mixed_ref[0, :, at : at + head_dim] = dot(probs.astype(bf16), v).astype(bf16)
    part_ref[0] = dot(mixed_ref[0], wo_ref[...]).astype(bf16)


def attend(lengths, x, w_qkv, w_out, query_g, key_g, cosine, signed_sine):
    seqs, rows, width = x.shape
    head_dim = query_g.shape[0]
    wide = w_qkv.shape[1] // 3
    whole = lambda s, lens: (0, 0)
    table = pl.BlockSpec((rows, head_dim), whole)
    gain = pl.BlockSpec((1, head_dim), whole)
    return pl.pallas_call(
        functools.partial(attend_kernel, wide // head_dim, head_dim),
        out_shape=[
            jax.ShapeDtypeStruct((seqs, rows, wide), bf16),
            jax.ShapeDtypeStruct((seqs, rows, width), bf16),
        ],
        grid_spec=pltpu.PrefetchScalarGridSpec(
            num_scalar_prefetch=1,
            grid=(seqs,),
            in_specs=[
                pl.BlockSpec((1, rows, width), lambda s, lens: (s, 0, 0)),
                pl.BlockSpec((width, 3 * wide), whole),
                pl.BlockSpec((wide, width), whole),
                gain,
                gain,
                table,
                table,
            ],
            out_specs=[
                pl.BlockSpec((1, rows, wide), lambda s, lens: (s, 0, 0)),
                pl.BlockSpec((1, rows, width), lambda s, lens: (s, 0, 0)),
            ],
        ),
        compiler_params=pltpu.CompilerParams(vmem_limit_bytes=kernel_vmem),
        cost_estimate=small_cost,
        name="attend",
    )(lengths, x, w_qkv, w_out, query_g[None, :], key_g[None, :], cosine, signed_sine)


def attend_back_kernel(
    heads,
    head_dim,
    lengths_ref,
    x_ref,
    g_ref,
    mixed_ref,
    w_ref,
    wo_ref,
    qg_ref,
    kg_ref,
    cos_ref,
    sin_ref,
    part_ref,
    dw_ref,
    dgain_ref,
    dw_acc,
    dwo_acc,
    gain_acc,
    gqkv_ref,
):
    step = pl.program_id(0)
    length = lengths_ref[step]
    wide = heads * head_dim
    scale = 1.0 / math.sqrt(head_dim)
    cosine, signed_sine = cos_ref[...], sin_ref[...]

    @pl.when(step == 0)
    def _():
        dw_acc[...] = jnp.zeros_like(dw_acc)
        dwo_acc[...] = jnp.zeros_like(dwo_acc)
        gain_acc[...] = jnp.zeros_like(gain_acc)

    qkv = dot(x_ref[0], w_ref[...])
    g_mixed = dot(g_ref[0], wo_ref[...], 1, 1).astype(bf16)
    dwo_acc[...] += dot(mixed_ref[0], g_ref[0], 0, 0)
    for h in range(heads):
        at = h * head_dim
        q_lin = qkv[:, at : at + head_dim]
        k_lin = qkv[:, wide + at : wide + at + head_dim]
        v = qkv[:, 2 * wide + at : 2 * wide + at + head_dim].astype(bf16)
        q_inv, q_rot = head_values(q_lin, qg_ref[...], cosine, signed_sine)
        k_inv, k_rot = head_values(k_lin, kg_ref[...], cosine, signed_sine)
        probs = head_probs(q_rot, k_rot, length, scale)
        gm = g_mixed[:, at : at + head_dim]
        g_probs = dot(gm, v, 1, 1)
        g_scores = (probs * (g_probs - jnp.sum(probs * g_probs, axis=-1, keepdims=True))).astype(bf16)
        g_v = dot(probs.astype(bf16), gm, 0, 0)
        for i, (g_rot, lin, inv, gain) in enumerate(
            (
                (dot(g_scores, k_rot) * scale, q_lin, q_inv, qg_ref[...]),
                (dot(g_scores, q_rot, 0, 0) * scale, k_lin, k_inv, kg_ref[...]),
            )
        ):
            w = g_rot * cosine - pltpu.roll(g_rot, head_dim // 2, 1) * signed_sine
            u = w * gain
            g_lin = inv * (u - lin * inv * inv * jnp.mean(u * lin, axis=-1, keepdims=True))
            gain_acc[i : i + 1, :] += jnp.sum(w * lin * inv, axis=0, keepdims=True)
            gqkv_ref[:, i * wide + at : i * wide + at + head_dim] = g_lin.astype(bf16)
        gqkv_ref[:, 2 * wide + at : 2 * wide + at + head_dim] = g_v.astype(bf16)
    gqkv = gqkv_ref[...]
    part_ref[0] = dot(gqkv, w_ref[...], 1, 1).astype(bf16)
    dw_acc[...] += dot(x_ref[0], gqkv, 0, 0)

    @pl.when(step == pl.num_programs(0) - 1)
    def _():
        dw_ref[:, : 3 * wide] = dw_acc[...].astype(bf16)
        for i in range(dwo_acc.shape[1] // wide):
            at = i * wide
            dw_ref[at : at + wide, 3 * wide :] = dwo_acc[:, at : at + wide].astype(bf16)
        dgain_ref[...] = gain_acc[...]


def attend_back(lengths, x, g, mixed, w_qkv, w_out, query_g, key_g, cosine, signed_sine):
    seqs, rows, width = x.shape
    head_dim = query_g.shape[0]
    wide = w_qkv.shape[1] // 3
    whole = lambda s, lens: (0, 0)
    block = lambda s, lens: (s, 0, 0)
    table = pl.BlockSpec((rows, head_dim), whole)
    gain = pl.BlockSpec((1, head_dim), whole)
    return pl.pallas_call(
        functools.partial(attend_back_kernel, wide // head_dim, head_dim),
        out_shape=(
            jax.ShapeDtypeStruct((seqs, rows, width), bf16),
            jax.ShapeDtypeStruct((width, 4 * wide), bf16),
            jax.ShapeDtypeStruct((8, head_dim), f32),
        ),
        grid_spec=pltpu.PrefetchScalarGridSpec(
            num_scalar_prefetch=1,
            grid=(seqs,),
            in_specs=[
                pl.BlockSpec((1, rows, width), block),
                pl.BlockSpec((1, rows, width), block),
                pl.BlockSpec((1, rows, wide), block),
                pl.BlockSpec((width, 3 * wide), whole),
                pl.BlockSpec((wide, width), whole),
                gain,
                gain,
                table,
                table,
            ],
            out_specs=(
                pl.BlockSpec((1, rows, width), block),
                pl.BlockSpec((width, 4 * wide), whole),
                pl.BlockSpec((8, head_dim), whole),
            ),
            scratch_shapes=[
                pltpu.VMEM((width, 3 * wide), f32),
                pltpu.VMEM((wide, width), f32),
                pltpu.VMEM((8, head_dim), f32),
                pltpu.VMEM((rows, 3 * wide), bf16),
            ],
        ),
        compiler_params=pltpu.CompilerParams(vmem_limit_bytes=kernel_vmem),
        cost_estimate=small_cost,
        name="attend_back",
    )(lengths, x, g, mixed, w_qkv, w_out, query_g[None, :], key_g[None, :], cosine, signed_sine)


def slot_matrix(slot_row, capacity):
    return lax.broadcasted_iota(jnp.int32, (capacity, slot_row.shape[1]), 0) == slot_row


def stack(pieces):
    return pieces[0] if len(pieces) == 1 else jnp.concatenate(pieces, axis=0)


def expert_in_kernel(capacity, x_ref, cot_ref, slot_ref, gate_ref, wg_ref, wu_ref, in_ref, gr_ref, act_ref, g_ref, u_ref):
    for j in range(wg_ref.shape[0]):
        rows, grads = [], []
        for s in range(x_ref.shape[0]):
            chosen = slot_matrix(slot_ref[j, s], capacity)
            one_hot = jnp.where(chosen, 1.0, 0.0).astype(bf16)
            weight = jnp.sum(jnp.where(chosen, gate_ref[j, s], 0.0), axis=1, keepdims=True)
            rows.append(dot(one_hot, x_ref[s]))
            grads.append(weight * dot(one_hot, cot_ref[s]))
        taken = stack(rows).astype(bf16)
        in_ref[j] = taken
        gr_ref[j] = stack(grads).astype(bf16)
        gate_in = dot(taken, wg_ref[j])
        up_in = dot(taken, wu_ref[j])
        g_ref[j] = gate_in
        u_ref[j] = up_in
        act_ref[j] = (gate_in * jax.nn.sigmoid(gate_in) * up_in).astype(bf16)


def step_rows(groups):
    return 2 if groups % 2 == 0 else 1


def expert_forward(mlp_all, cot_all, slot_of, gates, w_gate, w_up, capacity, index):
    groups, tok_rows, width = mlp_all.shape
    local, ff = 1, w_gate.shape[2]
    seqs = step_rows(groups)
    slots = seqs * capacity
    tok = pl.BlockSpec((seqs, tok_rows, width), lambda i: (i, 0, 0))
    route = pl.BlockSpec((local, seqs, 1, tok_rows), lambda i: (index, i, 0, 0))
    weight = pl.BlockSpec((local, width, ff), lambda i: (index, 0, 0), pipeline_mode=pl.Buffered(1))
    wide = pl.BlockSpec((local, slots, width), lambda i: (0, i, 0))
    slim = pl.BlockSpec((local, slots, ff), lambda i: (0, i, 0))
    total = groups * capacity
    return pl.pallas_call(
        functools.partial(expert_in_kernel, capacity),
        out_shape=[
            jax.ShapeDtypeStruct((local, total, width), bf16),
            jax.ShapeDtypeStruct((local, total, width), bf16),
            jax.ShapeDtypeStruct((local, total, ff), bf16),
            jax.ShapeDtypeStruct((local, total, ff), f32),
            jax.ShapeDtypeStruct((local, total, ff), f32),
        ],
        grid=(groups // seqs,),
        in_specs=[tok, tok, route, route, weight, weight],
        out_specs=[wide, wide, slim, slim, slim],
        compiler_params=pltpu.CompilerParams(vmem_limit_bytes=kernel_vmem),
        cost_estimate=small_cost,
        name="expert_forward",
    )(mlp_all, cot_all, slot_of[:, :, None, :], gates[:, :, None, :], w_gate, w_up)


def expert_out_kernel(capacity, *refs):
    act_refs = refs[:-6]
    cot_ref, slot_ref, gate_ref, wd_ref, sum_ref, gg_ref = refs[-6:]
    parts = [None] * cot_ref.shape[0]
    for j in range(wd_ref.shape[0]):
        out = dot(act_refs[j][0], wd_ref[j])
        for s in range(cot_ref.shape[0]):
            one_hot = jnp.where(slot_matrix(slot_ref[j, s], capacity), 1.0, 0.0).astype(bf16)
            here = dot(one_hot, out[s * capacity : (s + 1) * capacity].astype(bf16), 0, 0)
            gg_ref[j, s] = jnp.sum(here * cot_ref[s].astype(f32), axis=1, keepdims=True)
            term = gate_ref[j, s] * here
            parts[s] = term if j == 0 else parts[s] + term
    for s in range(cot_ref.shape[0]):
        sum_ref[s] = parts[s].astype(bf16)


def expert_combine(acts, cot_all, slot_of, gates, w_down, capacity):
    groups, tok_rows, width = cot_all.shape
    local, ff, _ = w_down.shape
    seqs = step_rows(groups)
    tok = pl.BlockSpec((seqs, tok_rows, width), lambda i: (i, 0, 0))
    route = pl.BlockSpec((local, seqs, 1, tok_rows), lambda i: (0, i, 0, 0))
    column = pl.BlockSpec((local, seqs, tok_rows, 1), lambda i: (0, i, 0, 0))
    weight = pl.BlockSpec((local, ff, width), lambda i: (0, 0, 0), pipeline_mode=pl.Buffered(1))
    slim = pl.BlockSpec((1, seqs * capacity, ff), lambda i: (0, i, 0))
    return pl.pallas_call(
        functools.partial(expert_out_kernel, capacity),
        out_shape=[
            jax.ShapeDtypeStruct((groups, tok_rows, width), bf16),
            jax.ShapeDtypeStruct((local, groups, tok_rows, 1), f32),
        ],
        grid=(groups // seqs,),
        in_specs=[slim] * local + [tok, route, column, weight],
        out_specs=[tok, column],
        compiler_params=pltpu.CompilerParams(vmem_limit_bytes=kernel_vmem),
        cost_estimate=small_cost,
        name="expert_combine",
    )(*acts, cot_all, slot_of[:, :, None, :], gates[:, :, :, None], w_down)


def expert_back_kernel(capacity, *refs):
    local = (len(refs) - 7) // 3
    gr_refs, g_refs, u_refs = (refs[i * local : (i + 1) * local] for i in range(3))
    slot_ref, wg_ref, wu_ref, wd_ref, gg_ref, gu_ref, part_ref = refs[3 * local :]
    seqs = part_ref.shape[0]
    parts = [None] * seqs
    for j in range(wd_ref.shape[0]):
        grad_act = dot(gr_refs[j][0], wd_ref[j], 1, 1)
        gate_in = g_refs[j][0]
        sigma = jax.nn.sigmoid(gate_in)
        grad_up = (grad_act * (gate_in * sigma)).astype(bf16)
        grad_gate = (grad_act * u_refs[j][0] * sigma * (1.0 + gate_in * (1.0 - sigma))).astype(bf16)
        gg_ref[j] = grad_gate
        gu_ref[j] = grad_up
        rows = dot(grad_gate, wg_ref[j], 1, 1) + dot(grad_up, wu_ref[j], 1, 1)
        for s in range(seqs):
            one_hot = jnp.where(slot_matrix(slot_ref[j, s], capacity), 1.0, 0.0).astype(bf16)
            term = dot(one_hot, rows[s * capacity : (s + 1) * capacity].astype(bf16), 0, 0)
            parts[s] = term if j == 0 else parts[s] + term
    for s in range(seqs):
        part_ref[s] = parts[s].astype(bf16)


def expert_back(grad_recv, gate_in, up_in, slot_of, w_gate, w_up, w_down, groups, tok_rows, capacity):
    local, width, ff = w_gate.shape
    seqs = step_rows(groups)
    slots = seqs * capacity
    total = groups * capacity
    tok = pl.BlockSpec((seqs, tok_rows, width), lambda i: (i, 0, 0))
    route = pl.BlockSpec((local, seqs, 1, tok_rows), lambda i: (0, i, 0, 0))
    once = pl.Buffered(1)
    weight = pl.BlockSpec((local, width, ff), lambda i: (0, 0, 0), pipeline_mode=once)
    down = pl.BlockSpec((local, ff, width), lambda i: (0, 0, 0), pipeline_mode=once)
    wide = pl.BlockSpec((1, slots, width), lambda i: (0, i, 0))
    one = pl.BlockSpec((1, slots, ff), lambda i: (0, i, 0))
    slim = pl.BlockSpec((local, slots, ff), lambda i: (0, i, 0))
    return pl.pallas_call(
        functools.partial(expert_back_kernel, capacity),
        out_shape=[
            jax.ShapeDtypeStruct((local, total, ff), bf16),
            jax.ShapeDtypeStruct((local, total, ff), bf16),
            jax.ShapeDtypeStruct((groups, tok_rows, width), bf16),
        ],
        grid=(groups // seqs,),
        in_specs=[wide] * local + [one] * (2 * local) + [route, weight, weight, down],
        out_specs=[slim, slim, tok],
        compiler_params=pltpu.CompilerParams(vmem_limit_bytes=kernel_vmem),
        cost_estimate=small_cost,
        name="expert_back",
    )(*grad_recv, *gate_in, *up_in, slot_of[:, :, None, :], w_gate, w_up, w_down)


def assemble_kernel(x_ref, *outs):
    wide = x_ref.shape[3] // 4
    for i, out in enumerate(outs):
        for s in range(x_ref.shape[1]):
            out[:, s * wide : (s + 1) * wide] = x_ref[0, s, :, i * wide : (i + 1) * wide].astype(f32)


def assemble(x):
    shares, blocks, rows, columns = x.shape
    width = blocks * columns // 4
    return pl.pallas_call(
        assemble_kernel,
        out_shape=[jax.ShapeDtypeStruct((shares * rows, width), f32)] * 4,
        grid=(shares,),
        in_specs=[pl.BlockSpec((1, blocks, rows, columns), lambda p: (p, 0, 0, 0))],
        out_specs=[pl.BlockSpec((rows, width), lambda p: (p, 0))] * 4,
        compiler_params=pltpu.CompilerParams(vmem_limit_bytes=kernel_vmem),
        cost_estimate=small_cost,
        name="assemble",
    )(x)


def pad_rows(flat, tile):
    rows = -(-flat.shape[0] // (128 * tile)) * tile
    return jnp.pad(flat, (0, rows * 128 - flat.shape[0])).reshape(rows, 128)


def einf(spec, left, right):
    return jnp.einsum(spec, left, right, preferred_element_type=f32)


def body(
    tokens,
    cotangent,
    lengths,
    deal_order,
    routes,
    balance_coef,
    w_query,
    w_key,
    w_value,
    w_out,
    w_router,
    attn_gain,
    mlp_gain,
    query_gain,
    key_gain,
    w_gate,
    w_up,
    w_down,
):
    groups = lax.axis_size("expert")
    replicas = lax.axis_size("dp")
    me = lax.axis_index("expert")
    tok_rows, width = tokens.shape
    block_rows = tok_rows // replicas
    total_slots = float(tok_rows * replicas * groups)
    shard_rows = w_query.shape[0]
    local_experts = w_gate.shape[0]
    experts = local_experts * groups
    top_k = routes.shape[1]
    capacity = tok_rows * top_k * 9 // (8 * experts)

    order_row = lax.dynamic_index_in_dim(deal_order, me, 0, keepdims=False)
    dp_ids = jnp.arange(replicas, dtype=jnp.int32)
    matched = (order_row[:, None] == dp_ids[None, :]).astype(jnp.int32)
    inverse_order = jnp.sum(matched * dp_ids[:, None], axis=0)

    def blocks_to_deal(values):
        return values.reshape(replicas, block_rows, width)[inverse_order]

    small = jnp.concatenate(
        [w_router.reshape(-1), attn_gain, mlp_gain, query_gain, key_gain]
    )
    ints = jnp.concatenate([routes.reshape(-1), jnp.broadcast_to(lengths, (top_k,))])
    small_all, ints_all, seq_tokens, w_qkv = front(
        groups,
        replicas,
        0,
        pad_rows(small, 16),
        pad_rows(ints, 8),
        blocks_to_deal(tokens),
        w_query,
        w_key,
        w_value,
    )
    small_all, ints_all = small_all.reshape(groups, -1), ints_all.reshape(groups, -1)
    w_qkv = w_qkv.reshape(width, -1)
    n_router = shard_rows * experts
    cuts = [0, n_router]
    for gain in (attn_gain, mlp_gain, query_gain, key_gain):
        cuts.append(cuts[-1] + gain.shape[0])
    router_full = small_all[:, :n_router].reshape(width, experts)
    attn_g, mlp_g, query_g, key_g = (
        small_all[:, cuts[i] : cuts[i + 1]].reshape(-1).astype(f32) for i in range(1, 5)
    )
    head_dim = query_g.shape[0]
    local_width = w_query.shape[1] // groups

    routes_all = ints_all[:, : tok_rows * top_k].reshape(groups, tok_rows, top_k)
    lengths_all = ints_all[:, tok_rows * top_k]
    positions = jnp.arange(tok_rows, dtype=jnp.int32)
    live_all = (positions[None, :] < lengths_all[:, None]).astype(f32)
    live_rows = (positions < lengths[0]).astype(f32)

    inputs = seq_tokens.astype(f32)
    normed, inv_first = norm_fwd(inputs, attn_g)
    attn_in = normed.astype(bf16)
    attn_all, seq_cot = gather_rows(
        attn_in, groups, replicas, 1, riders=[Deal(blocks_to_deal(cotangent), groups, replicas)]
    )
    grad_output = seq_cot.astype(f32) * live_rows[:, None]
    cot_all = lax.all_gather(grad_output.astype(bf16), "expert", axis=0, tiled=False)

    cosine, signed_sine = rotary_tables(tok_rows, head_dim)
    mixed, hidden_part = attend(
        lengths_all, attn_all, w_qkv, w_out, query_g, key_g, cosine, signed_sine
    )
    hidden = inputs + scatter_sum(hidden_part, groups, replicas, 8)[0]
    mlp_normed, inv_second = norm_fwd(hidden, mlp_g)
    mlp_in = mlp_normed.astype(bf16)
    logits = einf("td,de->te", mlp_in, router_full)
    my_router = jax.nn.softmax(logits, axis=-1)
    mlp_all, router = gather_rows(
        mlp_in,
        groups,
        replicas,
        2,
        riders=[SmallGather(pad_rows(my_router.reshape(-1), 8), groups, replicas)],
    )
    router = router.reshape(groups, -1)[:, : tok_rows * experts].reshape(groups, tok_rows, experts)
    expert_ids = jnp.arange(experts, dtype=jnp.int32)
    picked = jnp.sum(
        (routes_all[:, :, :, None] == expert_ids).astype(f32), axis=2
    )
    chosen_sum = jnp.sum(picked * router, axis=-1, keepdims=True)
    gates = picked * router / chosen_sum
    counts = jnp.sum(picked * live_all[:, :, None], axis=(0, 1))
    prob_sums = jnp.sum(router * live_all[:, :, None], axis=(0, 1))
    live_count = jnp.sum(live_all)[None]
    stats = pad_rows(jnp.concatenate([counts, prob_sums, live_count]), 8)

    first = me * local_experts
    own_picked = lax.dynamic_slice_in_dim(picked, first, local_experts, 2)
    own_gates = lax.dynamic_slice_in_dim(gates, first, local_experts, 2)
    before = (positions[:, None] > positions[None, :]).astype(bf16)
    rank = einf("tu,suj->jst", before, own_picked.astype(bf16))
    own_picked = own_picked.transpose(2, 0, 1)
    own_gates = own_gates.transpose(2, 0, 1)
    slot_of = jnp.where(own_picked > 0.5, rank.astype(jnp.int32), -1)
    expert_in, grad_recv, act_low, gate_in, up_in, total_down = [], [], [], [], [], []
    for j in range(local_experts):
        taken, recv, act, gate, up = expert_forward(
            mlp_all, cot_all, slot_of, own_gates, w_gate, w_up, capacity, j
        )
        grad_down_w = einf("rf,rd->fd", act[0], recv[0]).astype(bf16)
        act, recv, mlp_all, grad_down_w = lax.optimization_barrier((act, recv, mlp_all, grad_down_w))
        total_down.append(lax.psum_scatter(grad_down_w, "dp", scatter_dimension=0, tiled=True))
        for values, value in zip(
            (expert_in, grad_recv, act_low, gate_in, up_in), (taken, recv, act, gate, up)
        ):
            values.append(value)
    grad_gate_in, grad_up_in, grad_part = expert_back(
        grad_recv, gate_in, up_in, slot_of, w_gate, w_up, w_down, groups, tok_rows, capacity
    )
    expert_in = jnp.concatenate(expert_in, axis=0)
    grad_gate_w = einf("jrd,jrf->jdf", expert_in, grad_gate_in).astype(bf16)
    grad_part, act_low, grad_gate_w = lax.optimization_barrier((grad_part, act_low, grad_gate_w))
    total_gate = lax.psum_scatter(grad_gate_w, "dp", scatter_dimension=1, tiled=True)
    sum_part, own_grad_gates = expert_combine(act_low, cot_all, slot_of, own_gates, w_down, capacity)
    gate_rows = own_grad_gates.transpose(1, 0, 2, 3).reshape(groups, -1, 128)
    grad_mlp_in, gate_back, sums = scatter_sum(
        grad_part,
        groups,
        replicas,
        3,
        riders=[Exchange(gate_rows, groups, replicas), DpSum(stats, groups, replicas)],
    )
    sums = sums.reshape(-1)
    counts, prob_sums = sums[:experts], sums[experts : 2 * experts]
    live_count = sums[2 * experts : 2 * experts + 1]
    fraction = counts / (live_count * top_k)
    balance_loss = balance_coef * (experts * jnp.sum(fraction * prob_sums / total_slots))

    grad_gates = gate_back.reshape(experts, tok_rows).T
    my_picked = lax.dynamic_index_in_dim(picked, me, 0, keepdims=False)
    my_gates = lax.dynamic_index_in_dim(gates, me, 0, keepdims=False)
    my_sum = lax.dynamic_index_in_dim(chosen_sum, me, 0, keepdims=False)
    grad_prob = (
        my_picked * (grad_gates - jnp.sum(grad_gates * my_gates, axis=1, keepdims=True)) / my_sum
        + live_rows[:, None] * (balance_coef * experts / total_slots) * fraction[None, :]
    )
    grad_logits = (
        my_router * (grad_prob - jnp.sum(my_router * grad_prob, axis=-1, keepdims=True))
    ).astype(bf16)
    grad_router_w = einf("td,te->de", mlp_in, grad_logits)
    grad_mlp_in = grad_mlp_in + einf("te,de->td", grad_logits, router_full)

    grad_hidden_norm, grad_mlp_g = norm_back(hidden, inv_second, mlp_g, grad_mlp_in, 0)
    grad_hidden = grad_output + grad_hidden_norm
    grad_hidden_low = grad_hidden.astype(bf16)
    grad_hidden_low, total_down = lax.optimization_barrier((grad_hidden_low, total_down))
    (hidden_all,) = gather_rows(grad_hidden_low, groups, replicas, 4)
    grad_attn_part, grad_attn_w, grad_gains = attend_back(
        lengths_all, attn_all, hidden_all, mixed, w_qkv, w_out, query_g, key_g, cosine, signed_sine
    )
    grad_query_g, grad_key_g = grad_gains[0], grad_gains[1]
    attn_share = lax.psum_scatter(
        grad_attn_w.reshape(groups, shard_rows, 4 * local_width), "dp", scatter_dimension=1, tiled=True
    )
    sum_part, grad_attn_part = lax.optimization_barrier((sum_part, grad_attn_part))
    (expert_sum,) = scatter_sum(sum_part, groups, replicas, 6)
    out_seq = (live_rows[:, None] * (hidden + expert_sum)).astype(bf16)

    def to_deal(values):
        return values.reshape(replicas, block_rows, width)

    grad_up_in, grad_attn_part, out_seq, total_gate = lax.optimization_barrier(
        (grad_up_in, grad_attn_part, out_seq, total_gate)
    )
    grad_up_w = einf("jrd,jrf->jdf", expert_in, grad_up_in).astype(bf16)
    grad_up_w, grad_attn_part = lax.optimization_barrier((grad_up_w, grad_attn_part))
    grad_attn_in, out_home = scatter_sum(
        grad_attn_part, groups, replicas, 5, riders=[Deal(to_deal(out_seq), groups, replicas)]
    )
    grad_attn_in, attn_share = lax.optimization_barrier((grad_attn_in, attn_share))
    grad_input_norm, grad_attn_g = norm_back(inputs, inv_first, attn_g, grad_attn_in, 0)
    grad_seq = (grad_hidden + grad_input_norm).astype(bf16)

    pieces = [grad_router_w.reshape(groups, n_router)] + [
        value.reshape(groups, -1) for value in (grad_attn_g, grad_mlp_g, grad_query_g, grad_key_g)
    ]
    pieces = jnp.concatenate(pieces, axis=1)
    pad = -pieces.shape[1] % 1024
    pieces = jnp.pad(pieces, ((0, 0), (0, pad))).reshape(groups, -1, 128)

    attn_sum, total_up, sum_small, grad_home = close(
        attn_share,
        3 * local_width,
        grad_up_w,
        groups,
        replicas,
        7,
        [SmallSum(pieces, groups, replicas), Deal(to_deal(grad_seq), groups, replicas)],
    )
    grad_input = to_deal(grad_home)[order_row].reshape(tok_rows, width).astype(f32)
    output = to_deal(out_home)[order_row].reshape(tok_rows, width)
    sum_q, sum_k, sum_v, sum_o = assemble(attn_sum)
    sum_small = sum_small.reshape(-1)
    sum_r = sum_small[:n_router].reshape(shard_rows, experts)
    sum_ga, sum_gm, sum_gq, sum_gk = (sum_small[cuts[i] : cuts[i + 1]] for i in range(1, 5))
    total_down = jnp.stack(total_down).astype(f32)
    total_gate = total_gate.astype(f32)
    return (
        output,
        balance_loss,
        grad_input,
        sum_q,
        sum_k,
        sum_v,
        sum_o,
        sum_r,
        sum_ga,
        sum_gm,
        sum_gq,
        sum_gk,
        total_gate,
        total_up,
        total_down,
    )


def solution(mesh):
    rows = P(("dp", "expert"), None)
    weight = P("expert", None)
    gain = P("expert")
    cube = P("expert", None, None)
    cube_out = P("expert", "dp", None)
    return jax.shard_map(
        body,
        mesh=mesh,
        in_specs=(
            (rows, rows, P(("dp", "expert")), P(), rows, P())
            + (weight,) * 5
            + (gain,) * 4
            + (cube,) * 3
        ),
        out_specs=(
            (rows, P(), rows) + (weight,) * 5 + (gain,) * 4 + (cube_out,) * 3
        ),
        check_vma=False,
    )
```

```python
import functools
import math

import jax
import jax.numpy as jnp
from jax import lax
from jax.experimental import pallas as pl
from jax.experimental.pallas import tpu as pltpu
from jax.sharding import PartitionSpec as P

norm_eps = 1e-06
rope_base = 50000.0
big_negative = -1e30
bf16 = jnp.bfloat16
f32 = jnp.float32
MESH = pl.DeviceIdType.MESH
DMA = pltpu.SemaphoreType.DMA
kernel_vmem = 62 << 20
small_cost = pl.CostEstimate(flops=0, transcendentals=0, bytes_accessed=1024)


def norm_fwd(values, scales):
    inverse = lax.rsqrt(jnp.mean(values * values, axis=-1, keepdims=True) + norm_eps)
    return (values * inverse * scales, inverse)


def norm_back(values, inverse, scales, grad_out, sum_axes):
    scaled = grad_out * scales
    grad_in = inverse * (
        scaled - values * inverse * inverse * jnp.mean(scaled * values, axis=-1, keepdims=True)
    )
    grad_scale = jnp.sum(grad_out * values * inverse, axis=sum_axes)
    return (grad_in, grad_scale)


def rotary_tables(tok_rows, head_dim):
    half_dim = head_dim // 2
    positions = jnp.arange(tok_rows, dtype=jnp.int32).astype(f32)
    frequency = rope_base ** (-jnp.arange(half_dim, dtype=jnp.int32).astype(f32) * 2.0 / head_dim)
    angles = positions[:, None] * frequency[None, :]
    cosine = jnp.concatenate([jnp.cos(angles), jnp.cos(angles)], axis=-1)
    signed_sine = jnp.concatenate([-jnp.sin(angles), jnp.sin(angles)], axis=-1)
    return (cosine, signed_sine)


def peer(index):
    return {"expert": index}


def remote(src, dst, send, recv, to):
    return pltpu.make_async_remote_copy(
        src_ref=src, dst_ref=dst, send_sem=send, recv_sem=recv, device_id=peer(to), device_id_type=MESH
    )


def greet(n, me, replicas=1):
    barrier = pltpu.get_barrier_semaphore()
    for k in range(1, n):
        pl.semaphore_signal(
            barrier, inc=1, device_id=peer(lax.rem(me + k, n)), device_id_type=MESH
        )
    for k in range(1, replicas):
        other = lax.rem(lax.axis_index("dp") + k, replicas)
        pl.semaphore_signal(barrier, inc=1, device_id={"dp": other}, device_id_type=MESH)
    pl.semaphore_wait(barrier, n + replicas - 2)


def quad_places(me):
    core = lax.rem(me, 2)
    chip = me // 2
    x = lax.rem(chip, 2)
    y = chip // 2

    def at(px, py, pc):
        return (py * 2 + px) * 2 + pc

    spots = ((x, y), (1 - x, y), (x, 1 - y), (1 - x, 1 - y))
    return [at(px, py, core) for px, py in spots], [at(px, py, 1 - core) for px, py in spots]


def any_places(n, me):
    core = lax.rem(me, 2)
    chip = me // 2
    chips = n // 2
    chip_of = [lax.rem(chip + k, chips) for k in range(chips)]
    chip_from = [lax.rem(chip - k + chips, chips) for k in range(chips)]
    return (
        [c * 2 + core for c in chip_of],
        [c * 2 + 1 - core for c in chip_of],
        [c * 2 + core for c in chip_from],
        [c * 2 + 1 - core for c in chip_from],
    )


def deal_copies(replicas, src, dst, own_sem, send_sem, recv_sem):
    here = lax.axis_index("dp")
    rows = src.shape[1]
    mine = pl.ds(here * rows, rows)
    own = pltpu.make_async_copy(src.at[here], dst.at[mine], own_sem)
    away = []
    for k in range(1, replicas):
        to = lax.rem(here + k, replicas)
        away.append(
            pltpu.make_async_remote_copy(
                src_ref=src.at[to],
                dst_ref=dst.at[mine],
                send_sem=send_sem.at[k],
                recv_sem=recv_sem.at[k],
                device_id={"dp": to},
                device_id_type=MESH,
            )
        )
    return own, away


def front_kernel(
    n,
    replicas,
    small,
    ints,
    blocks,
    wq,
    wk,
    wv,
    small_all,
    ints_all,
    seq,
    w_all,
    small_send,
    small_recv,
    own_sem,
    deal_send,
    deal_recv,
    w_own,
    w_send,
    w_recv,
):
    me = lax.axis_index("expert")
    wide = wq.shape[1] // n
    small_all[me] = small[...]
    ints_all[me] = ints[...]
    own, away = deal_copies(replicas, blocks, seq, own_sem, deal_send, deal_recv)
    own.start()

    def columns(weight, index):
        return weight.at[:, pl.ds(pl.multiple_of(index * wide, wide), wide)]

    kept = []
    for i, weight in enumerate((wq, wk, wv)):
        copy = pltpu.make_async_copy(
            columns(weight, me), w_all.at[me, :, pl.ds(i * wide, wide)], w_own.at[i]
        )
        copy.start()
        kept.append(copy)
    greet(n, me, replicas)
    copies = []

    def go(copy):
        copy.start()
        copies.append(copy)

    for k in range(1, n):
        to = lax.rem(me + k, n)
        go(remote(small, small_all.at[me], small_send.at[0, k], small_recv.at[0, k], to))
        go(remote(ints, ints_all.at[me], small_send.at[1, k], small_recv.at[1, k], to))
    for copy in away:
        go(copy)
    for k in range(1, n):
        to = lax.rem(me + k, n)
        for i, weight in enumerate((wq, wk, wv)):
            go(
                remote(
                    columns(weight, to),
                    w_all.at[me, :, pl.ds(i * wide, wide)],
                    w_send.at[i, k],
                    w_recv.at[i, k],
                    to,
                )
            )
    for copy in copies:
        copy.wait()
    own.wait()
    for copy in kept:
        copy.wait()


def front(n, replicas, collective_id, small, ints, blocks, wq, wk, wv):
    vmem = pl.BlockSpec(memory_space=pltpu.VMEM)
    away = pl.BlockSpec(memory_space=pl.ANY)
    rows, width = wq.shape
    return pl.pallas_call(
        functools.partial(front_kernel, n, replicas),
        out_shape=[
            jax.ShapeDtypeStruct((n,) + small.shape, small.dtype),
            jax.ShapeDtypeStruct((n,) + ints.shape, ints.dtype),
            jax.ShapeDtypeStruct((replicas * blocks.shape[1], width), bf16),
            jax.ShapeDtypeStruct((n, rows, 3 * (width // n)), bf16),
        ],
        in_specs=[vmem, vmem, away, away, away, away],
        out_specs=[vmem, vmem, away, away],
        scratch_shapes=[
            DMA((2, n)),
            DMA((2, n)),
            DMA,
            DMA((replicas,)),
            DMA((replicas,)),
            DMA((3,)),
            DMA((3, n)),
            DMA((3, n)),
        ],
        compiler_params=pltpu.CompilerParams(
            collective_id=collective_id, has_side_effects=True, vmem_limit_bytes=kernel_vmem
        ),
        cost_estimate=small_cost,
        name="front",
    )(small, ints, blocks, wq, wk, wv)


VMEM_SPEC = pl.BlockSpec(memory_space=pltpu.VMEM)
AWAY_SPEC = pl.BlockSpec(memory_space=pl.ANY)


def along_dp(src, dst, send, recv, to):
    return pltpu.make_async_remote_copy(
        src_ref=src, dst_ref=dst, send_sem=send, recv_sem=recv, device_id={"dp": to}, device_id_type=MESH
    )


class Exchange:
    over_dp = False

    def __init__(self, x, n, replicas, columns=None):
        self.n = n
        self.columns = columns or x.shape[2]
        self.ins = [(x, VMEM_SPEC)]
        self.outs = [(jax.ShapeDtypeStruct(x.shape, x.dtype), VMEM_SPEC)]
        self.scratch = [DMA((n,)), DMA((n,))]

    def start(self, me, src, out, send, recv):
        cols = pl.ds(0, self.columns)
        self.copies = []
        for k in range(1, self.n):
            to = lax.rem(me + k, self.n)
            self.copies.append(
                remote(src.at[to, :, cols], out.at[me, :, cols], send.at[k], recv.at[k], to)
            )
            self.copies[-1].start()
        out[me, :, : self.columns] = src[me, :, : self.columns]
        if self.columns < src.shape[2]:
            out[:, :, self.columns :] = src[:, :, self.columns :]

    def finish(self, me, *refs):
        for copy in self.copies:
            copy.wait()


class DpSum:
    over_dp = True

    def __init__(self, x, n, replicas):
        self.replicas = replicas
        self.ins = [(x, VMEM_SPEC)]
        self.outs = [(jax.ShapeDtypeStruct(x.shape, x.dtype), VMEM_SPEC)]
        self.scratch = [pltpu.VMEM((replicas,) + x.shape, x.dtype), DMA((replicas,)), DMA((replicas,))]

    def start(self, me, src, out, got, send, recv):
        here = lax.axis_index("dp")
        got[here] = src[...]
        self.copies = []
        for k in range(1, self.replicas):
            to = lax.rem(here + k, self.replicas)
            self.copies.append(along_dp(src, got.at[here], send.at[k], recv.at[k], to))
            self.copies[-1].start()

    def finish(self, me, src, out, got, send, recv):
        for copy in self.copies:
            copy.wait()
        value = got[0]
        for k in range(1, self.replicas):
            value = value + got[k]
        out[...] = value


class SmallSum:
    over_dp = True

    def __init__(self, x, n, replicas):
        self.n, self.replicas = n, replicas
        shape = x.shape[1:]
        self.ins = [(x, VMEM_SPEC)]
        self.outs = [(jax.ShapeDtypeStruct(shape, f32), VMEM_SPEC)]
        self.scratch = [pltpu.VMEM(x.shape, f32), pltpu.VMEM((replicas,) + shape, f32)]
        self.scratch += [DMA((n,)), DMA((n,)), DMA((replicas,)), DMA((replicas,))]

    def start(self, me, src, out, got, total, send, recv, over_send, over_recv):
        got[me] = src[me]
        self.copies = []
        for k in range(1, self.n):
            to = lax.rem(me + k, self.n)
            self.copies.append(remote(src.at[to], got.at[me], send.at[k], recv.at[k], to))
            self.copies[-1].start()

    def finish(self, me, src, out, got, total, send, recv, over_send, over_recv):
        here = lax.axis_index("dp")
        for copy in self.copies:
            copy.wait()
        value = got[0]
        for k in range(1, self.n):
            value = value + got[k]
        total[here] = value
        copies = []
        for k in range(1, self.replicas):
            to = lax.rem(here + k, self.replicas)
            copies.append(along_dp(total.at[here], total.at[here], over_send.at[k], over_recv.at[k], to))
            copies[-1].start()
        for copy in copies:
            copy.wait()
        value = total[0]
        for k in range(1, self.replicas):
            value = value + total[k]
        out[...] = value


class Deal:
    over_dp = True

    def __init__(self, blocks, n, replicas):
        self.replicas = replicas
        _, rows, width = blocks.shape
        self.ins = [(blocks, AWAY_SPEC)]
        self.outs = [(jax.ShapeDtypeStruct((replicas * rows, width), blocks.dtype), AWAY_SPEC)]
        self.scratch = [DMA, DMA((replicas,)), DMA((replicas,))]

    def start(self, me, src, out, own, send, recv):
        kept, away = deal_copies(self.replicas, src, out, own, send, recv)
        kept.start()
        for copy in away:
            copy.start()
        self.copies = away + [kept]

    def finish(self, me, *refs):
        for copy in self.copies:
            copy.wait()


class DpGather:
    over_dp = True

    def __init__(self, x, n, replicas, parts=4):
        self.replicas, self.parts = replicas, parts
        self.size = x.shape[0] // parts
        self.ins = [(x, AWAY_SPEC)]
        self.outs = [(jax.ShapeDtypeStruct((replicas,) + x.shape, x.dtype), AWAY_SPEC)]
        self.scratch = [DMA, DMA((2, replicas, parts)), DMA((2, replicas, parts))]

    def piece(self, p):
        return pl.ds(p * self.size, self.size)

    def hop(self, src, out, send, recv, way, k, p):
        here = lax.axis_index("dp")
        step = 1 - 2 * way
        block = out.at[here - step * k, self.piece(p)]
        origin = block if k else src.at[self.piece(p)]
        return along_dp(origin, block, send.at[way, k, p], recv.at[way, k, p], here + step)

    def sends(self, way, k):
        here = lax.axis_index("dp")
        last = self.replicas - 1
        if way == 0:
            return (here >= k) & (here < last), here >= k + 1
        return (here + k <= last) & (here > 0), here + k + 1 <= last

    def start(self, me, src, out, own, send, recv):
        self.copy = pltpu.make_async_copy(src, out.at[lax.axis_index("dp")], own)
        self.copy.start()
        for way in range(2):

            @pl.when(self.sends(way, 0)[0])
            def _():
                for p in range(self.parts):
                    self.hop(src, out, send, recv, way, 0, p).start()

    def steps(self, src, out, own, send, recv):
        here = lax.axis_index("dp")
        for k in range(self.replicas - 1):
            for p in range(self.parts):
                for way in range(2):

                    @pl.when(self.sends(way, k)[1])
                    def _():
                        block = out.at[here - (1 - 2 * way) * (k + 1), self.piece(p)]
                        along_dp(
                            block, block, send.at[way, k, p], recv.at[way, k, p], here
                        ).wait_recv()

                    if k + 1 < self.replicas - 1:

                        @pl.when(self.sends(way, k + 1)[0])
                        def _():
                            self.hop(src, out, send, recv, way, k + 1, p).start()

                yield

        for k in range(self.replicas - 1):
            for way in range(2):

                @pl.when(self.sends(way, k)[0])
                def _():
                    for p in range(self.parts):
                        self.hop(src, out, send, recv, way, k, p).wait_send()

        self.copy.wait()


class LineSum:
    def __init__(self, values, n, replicas, parts=4):
        self.replicas, self.parts = replicas, parts
        self.blocks = len(values)
        rows, columns = values[0].shape
        self.rows = rows // replicas
        self.size = self.rows // parts
        held = pltpu.VMEM((replicas, self.blocks, self.rows, columns), bf16)
        self.ins = [(x, AWAY_SPEC) for x in values]
        self.outs = [(jax.ShapeDtypeStruct((self.blocks, self.rows, columns), f32), VMEM_SPEC)]
        sems = DMA((2, replicas, parts))
        self.scratch = [held, held, held, DMA((self.blocks, replicas, parts)), sems, sems]

    def loads(self, values, own, sem, c, p):
        rows = pl.ds(pl.multiple_of(c * self.rows + p * self.size, self.size), self.size)
        return [
            pltpu.make_async_copy(
                x.at[rows], own.at[c, b, pl.ds(p * self.size, self.size)], sem.at[b, c, p]
            )
            for b, x in enumerate(values)
        ]

    def hop(self, own, got, send, recv, way, c, p):
        here = lax.axis_index("dp")
        rows = pl.ds(p * self.size, self.size)
        return along_dp(
            own.at[c, :, rows],
            got.at[c, :, rows],
            send.at[way, c, p],
            recv.at[way, c, p],
            here + 1 - 2 * way,
        )

    def add(self, total, got, c, p, widen=None):
        chunk = min(self.size, 32)
        for b in range(self.blocks):

            @pl.loop(0, self.size // chunk)
            def _(i):
                rows = pl.ds(p * self.size + i * chunk, chunk)
                if widen is None:
                    value = total[c, b, rows].astype(f32) + got[c, b, rows].astype(f32)
                    total[c, b, rows] = value.astype(bf16)
                elif got is None:
                    widen[b, rows] = total[c, b, rows].astype(f32)
                else:
                    widen[b, rows] = widen[b, rows] + got[c, b, rows].astype(f32)

    def start(self, values, own, sem):
        for t in range(self.replicas):
            for p in range(self.parts):
                for copy in self.loads(values, own, sem, t, p):
                    copy.start()

    def steps(self, values, out, own, up, down, sem, send, recv):
        here = lax.axis_index("dp")
        last = self.replicas - 1
        for t in range(last):
            for p in range(self.parts):
                for way, c, got in ((0, last - t, up), (1, t, down)):
                    bound = here < c if way == 0 else here > c
                    inner = here > 0 if way == 0 else here < last

                    @pl.when(bound)
                    def _():
                        for copy in self.loads(values, own, sem, c, p):
                            copy.wait()

                        @pl.when(inner)
                        def _():
                            self.hop(own, got, send, recv, way, c, p).wait_recv()
                            self.add(own, got, c, p)

                        self.hop(own, got, send, recv, way, c, p).start()

                yield
        for p in range(self.parts):
            for copy in self.loads(values, own, sem, here, p):
                copy.wait()
            self.add(own, None, here, p, out)
            for way, got, inner in ((0, up, here > 0), (1, down, here < last)):

                @pl.when(inner)
                def _():
                    self.hop(own, got, send, recv, way, here, p).wait_recv()
                    self.add(own, got, here, p, out)

        for t in range(last):
            for p in range(self.parts):
                for way, c, got in ((0, last - t, up), (1, t, down)):

                    @pl.when(here < c if way == 0 else here > c)
                    def _():
                        self.hop(own, got, send, recv, way, c, p).wait_send()


def close_kernel(exchange, gather, line, meet, share, *refs):
    values, (full, out, rows), refs = refs[: line.blocks], refs[line.blocks :][:3], refs[line.blocks + 3 :]
    swap_refs, refs = refs[:2], refs[2:]
    gather_refs, line_refs = refs[: len(gather.scratch)], refs[len(gather.scratch) :]
    me = lax.axis_index("expert")
    line.start(values, line_refs[0], line_refs[3])
    meet(me)
    exchange.start(me, share, rows, *swap_refs)
    running = [line.steps(values, out, *line_refs)]
    next(running[0])
    exchange.finish(me)
    gather.start(me, rows, full, *gather_refs)
    running.append(gather.steps(rows, full, *gather_refs))
    while running:
        running = [r for r in running if next(r, True) is None]


def close(attn_share, columns, grad_up_w, n, replicas, collective_id, riders):
    exchange = Exchange(attn_share, n, replicas, columns)
    gather = DpGather(attn_share, n, replicas)
    line = LineSum(grad_up_w, n, replicas)
    return riding_call(
        n,
        replicas,
        functools.partial(close_kernel, exchange, gather, line),
        exchange.ins + line.ins,
        gather.outs + line.outs,
        [pltpu.VMEM(attn_share.shape, bf16)] + exchange.scratch + gather.scratch + line.scratch,
        riders,
        collective_id,
        "close",
    )


class SmallGather:
    over_dp = False

    def __init__(self, x, n, replicas):
        self.n = n
        self.ins = [(x, VMEM_SPEC)]
        self.outs = [(jax.ShapeDtypeStruct((n,) + x.shape, x.dtype), VMEM_SPEC)]
        self.scratch = [DMA((n,)), DMA((n,))]

    def start(self, me, src, out, send, recv):
        out[me] = src[...]
        self.copies = []
        for k in range(1, self.n):
            to = lax.rem(me + k, self.n)
            self.copies.append(remote(src, out.at[me], send.at[k], recv.at[k], to))
            self.copies[-1].start()

    def finish(self, me, *refs):
        for copy in self.copies:
            copy.wait()


def riding_kernel(n, replicas, main, counts, riders, *refs):
    n_in, n_out, n_scratch = counts
    at = [0]

    def take(count):
        at[0] += count
        return refs[at[0] - count : at[0]]

    main_in = take(n_in)
    rider_in = [take(len(r.ins)) for r in riders]
    main_out = take(n_out)
    rider_out = [take(len(r.outs)) for r in riders]
    main_scratch = take(n_scratch)
    rider_refs = [i + o + take(len(r.scratch)) for r, i, o in zip(riders, rider_in, rider_out)]

    def meet(me):
        greet(n, me, replicas if any(r.over_dp for r in riders) else 1)
        for rider, own in zip(riders, rider_refs):
            rider.start(me, *own)

    main(meet, *main_in, *main_out, *main_scratch)
    me = lax.axis_index("expert")
    for rider, own in zip(riders, rider_refs):
        rider.finish(me, *own)


def riding_call(n, replicas, main, ins, outs, scratch, riders, collective_id, name):
    pairs_in = ins + [pair for r in riders for pair in r.ins]
    pairs_out = outs + [pair for r in riders for pair in r.outs]
    counts = (len(ins), len(outs), len(scratch))
    return pl.pallas_call(
        functools.partial(riding_kernel, n, replicas, main, counts, riders),
        out_shape=[shape for shape, _ in pairs_out],
        in_specs=[spec for _, spec in pairs_in],
        out_specs=[spec for _, spec in pairs_out],
        scratch_shapes=scratch + [shape for r in riders for shape in r.scratch],
        compiler_params=pltpu.CompilerParams(
            collective_id=collective_id, has_side_effects=True, vmem_limit_bytes=kernel_vmem
        ),
        cost_estimate=small_cost,
        name=name,
    )(*[value for value, _ in pairs_in])


def ride_only(meet, *refs):
    meet(lax.axis_index("expert"))


def quad_gather_kernel(parts, meet, x_ref, o_ref, own_sem, send_sem, recv_sem, pass_sem, pair_send, pair_recv):
    me = lax.axis_index("expert")
    same, other = quad_places(me)
    step = x_ref.shape[0] // parts
    half = parts // 2
    own = pltpu.make_async_copy(x_ref, o_ref.at[me], own_sem)
    own.start()
    meet(me)
    started = []

    def go(copy):
        copy.start()
        started.append(copy)

    def piece(p):
        return pl.ds(p * step, step)

    low, high = list(range(half)), list(range(half, parts))
    turns = [(k, seq[i]) for i in range(parts) for k, seq in ((1, high + low), (2, low + high))]
    for k, p in turns:
        go(remote(x_ref.at[piece(p)], o_ref.at[me, piece(p)], send_sem.at[k, p], recv_sem.at[k, p], same[k]))
    for p in range(parts):
        go(remote(x_ref.at[piece(p)], o_ref.at[me, piece(p)], pair_send.at[0, p], pair_recv.at[0, p], other[0]))

    def arrive(k, p):
        block = o_ref.at[same[k], piece(p)]
        remote(block, block, send_sem.at[k, p], recv_sem.at[k, p], other[0]).wait_recv()
        return block

    for k, p in turns:
        block = arrive(k, p)
        if (p >= half) == (k == 1):
            go(remote(block, block, pass_sem.at[p], recv_sem.at[3, p], same[3 - k]))
        go(remote(block, block, pair_send.at[k, p], pair_recv.at[k, p], other[0]))
    for pair in zip(low, high):
        for p in pair:
            block = arrive(3, p)
            go(remote(block, block, pair_send.at[3, p], pair_recv.at[3, p], other[0]))
    for k in range(4):
        for p in range(parts):
            block = o_ref.at[other[k], piece(p)]
            remote(block, block, pair_send.at[k, p], pair_recv.at[k, p], other[0]).wait_recv()
    for copy in started:
        copy.wait_send()
    own.wait()


def any_gather_kernel(n, meet, x_ref, o_ref, own_sem, send_sem, recv_sem, pair_send, pair_recv):
    me = lax.axis_index("expert")
    same, other, same_from, other_from = any_places(n, me)
    own = pltpu.make_async_copy(x_ref, o_ref.at[me], own_sem)
    own.start()
    meet(me)
    started = []
    for k in range(n // 2):
        if k:
            copy = remote(x_ref, o_ref.at[me], send_sem.at[k], recv_sem.at[k], same[k])
        else:
            copy = remote(x_ref, o_ref.at[me], pair_send.at[0], pair_recv.at[0], other[0])
        copy.start()
        started.append(copy)
    for k in range(1, n // 2):
        block = o_ref.at[same_from[k]]
        remote(block, block, send_sem.at[k], recv_sem.at[k], other[0]).wait_recv()
        copy = remote(block, block, pair_send.at[k], pair_recv.at[k], other[0])
        copy.start()
        started.append(copy)
    for k in range(n // 2):
        block = o_ref.at[other_from[k]]
        remote(block, block, pair_send.at[k], pair_recv.at[k], other[0]).wait_recv()
    for copy in started:
        copy.wait_send()
    own.wait()


def gather_plan(n, parts):
    chips = n // 2
    if n == 8:
        sems = [DMA, DMA((4, parts)), DMA((4, parts)), DMA((parts,)), DMA((4, parts)), DMA((4, parts))]
        return functools.partial(quad_gather_kernel, parts), sems
    sems = [DMA, DMA((chips,)), DMA((chips,)), DMA((chips,)), DMA((chips,))]
    return functools.partial(any_gather_kernel, n), sems


def gather_rows(x, n, replicas, collective_id, riders=(), parts=4):
    kernel, sems = gather_plan(n, parts)
    out = jax.ShapeDtypeStruct((n,) + x.shape, x.dtype)
    return riding_call(
        n,
        replicas,
        kernel,
        [(x, AWAY_SPEC)],
        [(out, AWAY_SPEC)],
        sems,
        list(riders),
        collective_id,
        f"gather_rows_{collective_id}",
    )


def add_rows(total, first, rows, chunk, *terms):
    @pl.loop(0, rows // chunk)
    def _(i):
        s = pl.ds(first + i * chunk, chunk)
        value = terms[0][s].astype(f32)
        for term in terms[1:]:
            value = value + term[s].astype(f32)
        total[s] = value.astype(total.dtype)


def quad_scatter_kernel(
    parts, meet, p_ref, o_ref, mine, theirs, transit, got, load_sem, pair_send, pair_recv, over_send, over_recv, send_sem, recv_sem
):
    me = lax.axis_index("expert")
    same, other = quad_places(me)
    step = p_ref.shape[1] // parts
    half = parts // 2
    low, high = list(range(half)), list(range(half, parts))
    mix = [p for pair in zip(low, high) for p in pair]
    order = (3, 1, 2, 0)

    def piece(p):
        return pl.ds(p * step, step)

    loads = {}
    for k in order:
        for p in mix:
            loads[k, p] = pltpu.make_async_copy(
                p_ref.at[same[k], piece(p)], mine.at[k, piece(p)], load_sem.at[k, p]
            )
            loads[k, p].start()
    meet(me)
    started = []

    def go(copy):
        copy.start()
        started.append(copy)

    for k in order:
        for p in mix:
            go(
                remote(
                    p_ref.at[other[k], piece(p)],
                    theirs.at[k, piece(p)],
                    pair_send.at[k, p],
                    pair_recv.at[k, p],
                    other[0],
                )
            )

    def fold(k, p):
        loads[k, p].wait()
        spot = theirs.at[k, piece(p)]
        remote(spot, spot, pair_send.at[k, p], pair_recv.at[k, p], other[0]).wait_recv()
        add_rows(mine.at[k], p * step, step, 32, mine.at[k], theirs.at[k])

    def ship(k, p):
        go(
            remote(
                mine.at[k, piece(p)],
                got.at[k - 1, piece(p)],
                send_sem.at[k - 1, p],
                recv_sem.at[k - 1, p],
                same[k],
            )
        )

    for p in mix:
        fold(3, p)
        to = same[1] if p < half else same[2]
        go(remote(mine.at[3, piece(p)], transit.at[piece(p)], over_send.at[p], over_recv.at[p], to))
    for a, b in zip(low, high):
        for k, p in ((1, a), (2, b)):
            fold(k, p)
            ship(k, p)
    for a, b in zip(low, high):
        for k, p in ((2, a), (1, b)):
            fold(k, p)
            spot = transit.at[piece(p)]
            remote(spot, spot, over_send.at[p], over_recv.at[p], other[0]).wait_recv()
            add_rows(mine.at[k], p * step, step, 32, mine.at[k], transit)
            ship(k, p)
    for p in mix:
        fold(0, p)
    for p in mix:
        for k in (0, 1):
            spot = got.at[k, piece(p)]
            remote(spot, spot, send_sem.at[k, p], recv_sem.at[k, p], other[0]).wait_recv()
        add_rows(o_ref, p * step, step, 32, mine.at[0], got.at[0], got.at[1])
    for copy in started:
        copy.wait_send()


def any_scatter_kernel(n, meet, p_ref, o_ref, mine, theirs, got, load_sem, pair_send, pair_recv, send_sem, recv_sem):
    me = lax.axis_index("expert")
    same, other, _, _ = any_places(n, me)
    rows = p_ref.shape[1]
    order = list(range(1, n // 2)) + [0]
    loads = {}
    for k in order:
        loads[k] = pltpu.make_async_copy(p_ref.at[same[k]], mine.at[k], load_sem.at[k])
        loads[k].start()
    meet(me)
    started = []
    for k in order:
        copy = remote(p_ref.at[other[k]], theirs.at[k], pair_send.at[k], pair_recv.at[k], other[0])
        copy.start()
        started.append(copy)
    for k in order:
        loads[k].wait()
        remote(theirs.at[k], theirs.at[k], pair_send.at[k], pair_recv.at[k], other[0]).wait_recv()
        add_rows(mine.at[k], 0, rows, 32, mine.at[k], theirs.at[k])
        if k:
            copy = remote(mine.at[k], got.at[k], send_sem.at[k], recv_sem.at[k], same[k])
            copy.start()
            started.append(copy)
    for k in range(1, n // 2):
        remote(got.at[k], got.at[k], send_sem.at[k], recv_sem.at[k], other[0]).wait_recv()
    add_rows(o_ref, 0, rows, 32, mine.at[0], *[got.at[k] for k in range(1, n // 2)])
    for copy in started:
        copy.wait_send()


def scatter_sum(x, n, replicas, collective_id, riders=(), parts=4):
    chips = n // 2
    shape = x.shape[1:]
    blocks = pltpu.VMEM((chips,) + shape, bf16)
    if n == 8:
        kernel = functools.partial(quad_scatter_kernel, parts)
        scratch = [blocks, blocks, pltpu.VMEM(shape, bf16), pltpu.VMEM((2,) + shape, bf16)]
        scratch += [DMA((4, parts))] * 3 + [DMA((parts,))] * 2 + [DMA((2, parts))] * 2
    else:
        kernel = functools.partial(any_scatter_kernel, n)
        scratch = [blocks] * 3 + [DMA((chips,))] * 5
    return riding_call(
        n,
        replicas,
        kernel,
        [(x, AWAY_SPEC)],
        [(jax.ShapeDtypeStruct(shape, f32), VMEM_SPEC)],
        scratch,
        list(riders),
        collective_id,
        f"scatter_sum_{collective_id}",
    )


def dot(left, right, left_dim=1, right_dim=0):
    return lax.dot_general(
        left, right, (((left_dim,), (right_dim,)), ((), ())), preferred_element_type=f32
    )


def head_values(lin, gain, cosine, signed_sine):
    inverse = lax.rsqrt(jnp.mean(lin * lin, axis=-1, keepdims=True) + norm_eps)
    normed = lin * inverse * gain
    half = lin.shape[1] // 2
    turned = normed * cosine + pltpu.roll(normed, half, 1) * signed_sine
    return inverse, turned.astype(bf16)


def head_probs(q_rot, k_rot, length, score_scale):
    scores = dot(q_rot, k_rot, 1, 1) * score_scale
    key = lax.broadcasted_iota(jnp.int32, scores.shape, 1)
    masked = jnp.where(key < length, scores, big_negative)
    raised = jnp.exp(masked - jnp.max(masked, axis=-1, keepdims=True))
    return raised / jnp.sum(raised, axis=-1, keepdims=True)


def attend_kernel(
    heads, head_dim, lengths_ref, x_ref, w_ref, wo_ref, qg_ref, kg_ref, cos_ref, sin_ref, mixed_ref, part_ref
):
    length = lengths_ref[pl.program_id(0)]
    wide = heads * head_dim
    qkv = dot(x_ref[0], w_ref[...])
    for h in range(heads):
        at = h * head_dim
        _, q_rot = head_values(qkv[:, at : at + head_dim], qg_ref[...], cos_ref[...], sin_ref[...])
        _, k_rot = head_values(
            qkv[:, wide + at : wide + at + head_dim], kg_ref[...], cos_ref[...], sin_ref[...]
        )
        v = qkv[:, 2 * wide + at : 2 * wide + at + head_dim].astype(bf16)
        probs = head_probs(q_rot, k_rot, length, 1.0 / math.sqrt(head_dim))
        mixed_ref[0, :, at : at + head_dim] = dot(probs.astype(bf16), v).astype(bf16)
    part_ref[0] = dot(mixed_ref[0], wo_ref[...]).astype(bf16)


def attend(lengths, x, w_qkv, w_out, query_g, key_g, cosine, signed_sine):
    seqs, rows, width = x.shape
    head_dim = query_g.shape[0]
    wide = w_qkv.shape[1] // 3
    whole = lambda s, lens: (0, 0)
    table = pl.BlockSpec((rows, head_dim), whole)
    gain = pl.BlockSpec((1, head_dim), whole)
    return pl.pallas_call(
        functools.partial(attend_kernel, wide // head_dim, head_dim),
        out_shape=[
            jax.ShapeDtypeStruct((seqs, rows, wide), bf16),
            jax.ShapeDtypeStruct((seqs, rows, width), bf16),
        ],
        grid_spec=pltpu.PrefetchScalarGridSpec(
            num_scalar_prefetch=1,
            grid=(seqs,),
            in_specs=[
                pl.BlockSpec((1, rows, width), lambda s, lens: (s, 0, 0)),
                pl.BlockSpec((width, 3 * wide), whole),
                pl.BlockSpec((wide, width), whole),
                gain,
                gain,
                table,
                table,
            ],
            out_specs=[
                pl.BlockSpec((1, rows, wide), lambda s, lens: (s, 0, 0)),
                pl.BlockSpec((1, rows, width), lambda s, lens: (s, 0, 0)),
            ],
        ),
        compiler_params=pltpu.CompilerParams(vmem_limit_bytes=kernel_vmem),
        cost_estimate=small_cost,
        name="attend",
    )(lengths, x, w_qkv, w_out, query_g[None, :], key_g[None, :], cosine, signed_sine)


def attend_back_kernel(
    heads,
    head_dim,
    lengths_ref,
    x_ref,
    g_ref,
    mixed_ref,
    w_ref,
    wo_ref,
    qg_ref,
    kg_ref,
    cos_ref,
    sin_ref,
    part_ref,
    dw_ref,
    dgain_ref,
    dw_acc,
    dwo_acc,
    gain_acc,
    gqkv_ref,
):
    step = pl.program_id(0)
    length = lengths_ref[step]
    wide = heads * head_dim
    scale = 1.0 / math.sqrt(head_dim)
    cosine, signed_sine = cos_ref[...], sin_ref[...]

    @pl.when(step == 0)
    def _():
        dw_acc[...] = jnp.zeros_like(dw_acc)
        dwo_acc[...] = jnp.zeros_like(dwo_acc)
        gain_acc[...] = jnp.zeros_like(gain_acc)

    qkv = dot(x_ref[0], w_ref[...])
    g_mixed = dot(g_ref[0], wo_ref[...], 1, 1).astype(bf16)
    dwo_acc[...] += dot(mixed_ref[0], g_ref[0], 0, 0)
    for h in range(heads):
        at = h * head_dim
        q_lin = qkv[:, at : at + head_dim]
        k_lin = qkv[:, wide + at : wide + at + head_dim]
        v = qkv[:, 2 * wide + at : 2 * wide + at + head_dim].astype(bf16)
        q_inv, q_rot = head_values(q_lin, qg_ref[...], cosine, signed_sine)
        k_inv, k_rot = head_values(k_lin, kg_ref[...], cosine, signed_sine)
        probs = head_probs(q_rot, k_rot, length, scale)
        gm = g_mixed[:, at : at + head_dim]
        g_probs = dot(gm, v, 1, 1)
        g_scores = (probs * (g_probs - jnp.sum(probs * g_probs, axis=-1, keepdims=True))).astype(bf16)
        g_v = dot(probs.astype(bf16), gm, 0, 0)
        for i, (g_rot, lin, inv, gain) in enumerate(
            (
                (dot(g_scores, k_rot) * scale, q_lin, q_inv, qg_ref[...]),
                (dot(g_scores, q_rot, 0, 0) * scale, k_lin, k_inv, kg_ref[...]),
            )
        ):
            w = g_rot * cosine - pltpu.roll(g_rot, head_dim // 2, 1) * signed_sine
            u = w * gain
            g_lin = inv * (u - lin * inv * inv * jnp.mean(u * lin, axis=-1, keepdims=True))
            gain_acc[i : i + 1, :] += jnp.sum(w * lin * inv, axis=0, keepdims=True)
            gqkv_ref[:, i * wide + at : i * wide + at + head_dim] = g_lin.astype(bf16)
        gqkv_ref[:, 2 * wide + at : 2 * wide + at + head_dim] = g_v.astype(bf16)
    gqkv = gqkv_ref[...]
    part_ref[0] = dot(gqkv, w_ref[...], 1, 1).astype(bf16)
    dw_acc[...] += dot(x_ref[0], gqkv, 0, 0)

    @pl.when(step == pl.num_programs(0) - 1)
    def _():
        dw_ref[:, : 3 * wide] = dw_acc[...].astype(bf16)
        for i in range(dwo_acc.shape[1] // wide):
            at = i * wide
            dw_ref[at : at + wide, 3 * wide :] = dwo_acc[:, at : at + wide].astype(bf16)
        dgain_ref[...] = gain_acc[...]


def attend_back(lengths, x, g, mixed, w_qkv, w_out, query_g, key_g, cosine, signed_sine):
    seqs, rows, width = x.shape
    head_dim = query_g.shape[0]
    wide = w_qkv.shape[1] // 3
    whole = lambda s, lens: (0, 0)
    block = lambda s, lens: (s, 0, 0)
    table = pl.BlockSpec((rows, head_dim), whole)
    gain = pl.BlockSpec((1, head_dim), whole)
    return pl.pallas_call(
        functools.partial(attend_back_kernel, wide // head_dim, head_dim),
        out_shape=(
            jax.ShapeDtypeStruct((seqs, rows, width), bf16),
            jax.ShapeDtypeStruct((width, 4 * wide), bf16),
            jax.ShapeDtypeStruct((8, head_dim), f32),
        ),
        grid_spec=pltpu.PrefetchScalarGridSpec(
            num_scalar_prefetch=1,
            grid=(seqs,),
            in_specs=[
                pl.BlockSpec((1, rows, width), block),
                pl.BlockSpec((1, rows, width), block),
                pl.BlockSpec((1, rows, wide), block),
                pl.BlockSpec((width, 3 * wide), whole),
                pl.BlockSpec((wide, width), whole),
                gain,
                gain,
                table,
                table,
            ],
            out_specs=(
                pl.BlockSpec((1, rows, width), block),
                pl.BlockSpec((width, 4 * wide), whole),
                pl.BlockSpec((8, head_dim), whole),
            ),
            scratch_shapes=[
                pltpu.VMEM((width, 3 * wide), f32),
                pltpu.VMEM((wide, width), f32),
                pltpu.VMEM((8, head_dim), f32),
                pltpu.VMEM((rows, 3 * wide), bf16),
            ],
        ),
        compiler_params=pltpu.CompilerParams(vmem_limit_bytes=kernel_vmem),
        cost_estimate=small_cost,
        name="attend_back",
    )(lengths, x, g, mixed, w_qkv, w_out, query_g[None, :], key_g[None, :], cosine, signed_sine)


def slot_matrix(slot_row, capacity):
    return lax.broadcasted_iota(jnp.int32, (capacity, slot_row.shape[1]), 0) == slot_row


def stack(pieces):
    return pieces[0] if len(pieces) == 1 else jnp.concatenate(pieces, axis=0)


def expert_in_kernel(capacity, x_ref, cot_ref, slot_ref, gate_ref, wg_ref, wu_ref, in_ref, gr_ref, act_ref, g_ref, u_ref):
    for j in range(wg_ref.shape[0]):
        rows, grads = [], []
        for s in range(x_ref.shape[0]):
            chosen = slot_matrix(slot_ref[j, s], capacity)
            one_hot = jnp.where(chosen, 1.0, 0.0).astype(bf16)
            weight = jnp.sum(jnp.where(chosen, gate_ref[j, s], 0.0), axis=1, keepdims=True)
            rows.append(dot(one_hot, x_ref[s]))
            grads.append(weight * dot(one_hot, cot_ref[s]))
        taken = stack(rows).astype(bf16)
        in_ref[j] = taken
        gr_ref[j] = stack(grads).astype(bf16)
        gate_in = dot(taken, wg_ref[j])
        up_in = dot(taken, wu_ref[j])
        g_ref[j] = gate_in
        u_ref[j] = up_in
        act_ref[j] = (gate_in * jax.nn.sigmoid(gate_in) * up_in).astype(bf16)


def step_rows(groups):
    return 2 if groups % 2 == 0 else 1


def expert_forward(mlp_all, cot_all, slot_of, gates, w_gate, w_up, capacity, index):
    groups, tok_rows, width = mlp_all.shape
    local, ff = 1, w_gate.shape[2]
    seqs = step_rows(groups)
    slots = seqs * capacity
    tok = pl.BlockSpec((seqs, tok_rows, width), lambda i: (i, 0, 0))
    route = pl.BlockSpec((local, seqs, 1, tok_rows), lambda i: (index, i, 0, 0))
    weight = pl.BlockSpec((local, width, ff), lambda i: (index, 0, 0), pipeline_mode=pl.Buffered(1))
    wide = pl.BlockSpec((local, slots, width), lambda i: (0, i, 0))
    slim = pl.BlockSpec((local, slots, ff), lambda i: (0, i, 0))
    total = groups * capacity
    return pl.pallas_call(
        functools.partial(expert_in_kernel, capacity),
        out_shape=[
            jax.ShapeDtypeStruct((local, total, width), bf16),
            jax.ShapeDtypeStruct((local, total, width), bf16),
            jax.ShapeDtypeStruct((local, total, ff), bf16),
            jax.ShapeDtypeStruct((local, total, ff), f32),
            jax.ShapeDtypeStruct((local, total, ff), f32),
        ],
        grid=(groups // seqs,),
        in_specs=[tok, tok, route, route, weight, weight],
        out_specs=[wide, wide, slim, slim, slim],
        compiler_params=pltpu.CompilerParams(vmem_limit_bytes=kernel_vmem),
        cost_estimate=small_cost,
        name="expert_forward",
    )(mlp_all, cot_all, slot_of[:, :, None, :], gates[:, :, None, :], w_gate, w_up)


def expert_out_kernel(capacity, *refs):
    act_refs = refs[:-6]
    cot_ref, slot_ref, gate_ref, wd_ref, sum_ref, gg_ref = refs[-6:]
    parts = [None] * cot_ref.shape[0]
    for j in range(wd_ref.shape[0]):
        out = dot(act_refs[j][0], wd_ref[j])
        for s in range(cot_ref.shape[0]):
            one_hot = jnp.where(slot_matrix(slot_ref[j, s], capacity), 1.0, 0.0).astype(bf16)
            here = dot(one_hot, out[s * capacity : (s + 1) * capacity].astype(bf16), 0, 0)
            gg_ref[j, s] = jnp.sum(here * cot_ref[s].astype(f32), axis=1, keepdims=True)
            term = gate_ref[j, s] * here
            parts[s] = term if j == 0 else parts[s] + term
    for s in range(cot_ref.shape[0]):
        sum_ref[s] = parts[s].astype(bf16)


def expert_combine(acts, cot_all, slot_of, gates, w_down, capacity):
    groups, tok_rows, width = cot_all.shape
    local, ff, _ = w_down.shape
    seqs = step_rows(groups)
    tok = pl.BlockSpec((seqs, tok_rows, width), lambda i: (i, 0, 0))
    route = pl.BlockSpec((local, seqs, 1, tok_rows), lambda i: (0, i, 0, 0))
    column = pl.BlockSpec((local, seqs, tok_rows, 1), lambda i: (0, i, 0, 0))
    weight = pl.BlockSpec((local, ff, width), lambda i: (0, 0, 0), pipeline_mode=pl.Buffered(1))
    slim = pl.BlockSpec((1, seqs * capacity, ff), lambda i: (0, i, 0))
    return pl.pallas_call(
        functools.partial(expert_out_kernel, capacity),
        out_shape=[
            jax.ShapeDtypeStruct((groups, tok_rows, width), bf16),
            jax.ShapeDtypeStruct((local, groups, tok_rows, 1), f32),
        ],
        grid=(groups // seqs,),
        in_specs=[slim] * local + [tok, route, column, weight],
        out_specs=[tok, column],
        compiler_params=pltpu.CompilerParams(vmem_limit_bytes=kernel_vmem),
        cost_estimate=small_cost,
        name="expert_combine",
    )(*acts, cot_all, slot_of[:, :, None, :], gates[:, :, :, None], w_down)


def expert_back_kernel(capacity, *refs):
    local = (len(refs) - 7) // 3
    gr_refs, g_refs, u_refs = (refs[i * local : (i + 1) * local] for i in range(3))
    slot_ref, wg_ref, wu_ref, wd_ref, gg_ref, gu_ref, part_ref = refs[3 * local :]
    seqs = part_ref.shape[0]
    parts = [None] * seqs
    for j in range(wd_ref.shape[0]):
        grad_act = dot(gr_refs[j][0], wd_ref[j], 1, 1)
        gate_in = g_refs[j][0]
        sigma = jax.nn.sigmoid(gate_in)
        grad_up = (grad_act * (gate_in * sigma)).astype(bf16)
        grad_gate = (grad_act * u_refs[j][0] * sigma * (1.0 + gate_in * (1.0 - sigma))).astype(bf16)
        gg_ref[j] = grad_gate
        gu_ref[j] = grad_up
        rows = dot(grad_gate, wg_ref[j], 1, 1) + dot(grad_up, wu_ref[j], 1, 1)
        for s in range(seqs):
            one_hot = jnp.where(slot_matrix(slot_ref[j, s], capacity), 1.0, 0.0).astype(bf16)
            term = dot(one_hot, rows[s * capacity : (s + 1) * capacity].astype(bf16), 0, 0)
            parts[s] = term if j == 0 else parts[s] + term
    for s in range(seqs):
        part_ref[s] = parts[s].astype(bf16)


def expert_back(grad_recv, gate_in, up_in, slot_of, w_gate, w_up, w_down, groups, tok_rows, capacity):
    local, width, ff = w_gate.shape
    seqs = step_rows(groups)
    slots = seqs * capacity
    total = groups * capacity
    tok = pl.BlockSpec((seqs, tok_rows, width), lambda i: (i, 0, 0))
    route = pl.BlockSpec((local, seqs, 1, tok_rows), lambda i: (0, i, 0, 0))
    once = pl.Buffered(1)
    weight = pl.BlockSpec((local, width, ff), lambda i: (0, 0, 0), pipeline_mode=once)
    down = pl.BlockSpec((local, ff, width), lambda i: (0, 0, 0), pipeline_mode=once)
    wide = pl.BlockSpec((1, slots, width), lambda i: (0, i, 0))
    one = pl.BlockSpec((1, slots, ff), lambda i: (0, i, 0))
    slim = pl.BlockSpec((local, slots, ff), lambda i: (0, i, 0))
    return pl.pallas_call(
        functools.partial(expert_back_kernel, capacity),
        out_shape=[
            jax.ShapeDtypeStruct((local, total, ff), bf16),
            jax.ShapeDtypeStruct((local, total, ff), bf16),
            jax.ShapeDtypeStruct((groups, tok_rows, width), bf16),
        ],
        grid=(groups // seqs,),
        in_specs=[wide] * local + [one] * (2 * local) + [route, weight, weight, down],
        out_specs=[slim, slim, tok],
        compiler_params=pltpu.CompilerParams(vmem_limit_bytes=kernel_vmem),
        cost_estimate=small_cost,
        name="expert_back",
    )(*grad_recv, *gate_in, *up_in, slot_of[:, :, None, :], w_gate, w_up, w_down)


def assemble_kernel(
    order_ref, x_ref, grad_ref, out_ref, last_ref, q_ref, k_ref, v_ref, o_ref, grad_input_ref, output_ref, up_ref
):
    wide = x_ref.shape[3] // 4
    for i, to in enumerate((q_ref, k_ref, v_ref, o_ref)):
        for s in range(x_ref.shape[1]):
            to[:, s * wide : (s + 1) * wide] = x_ref[0, s, :, i * wide : (i + 1) * wide].astype(f32)
    grad_input_ref[...] = grad_ref[0].astype(f32)
    output_ref[...] = out_ref[0]
    up_ref[...] = last_ref[...]


def assemble(order_row, x, grad_home, out_home, last):
    shares, blocks, rows, columns = x.shape
    _, dealt, width = grad_home.shape
    local, up_rows, ff = last.shape
    weight = jax.ShapeDtypeStruct((shares * rows, width), f32)
    at = lambda p, order: (p, 0)
    home = pl.BlockSpec((1, dealt, width), lambda p, order: (order[p], 0, 0))
    part = up_rows // shares
    return pl.pallas_call(
        assemble_kernel,
        out_shape=[weight] * 4
        + [
            jax.ShapeDtypeStruct((shares * dealt, width), f32),
            jax.ShapeDtypeStruct((shares * dealt, width), bf16),
            jax.ShapeDtypeStruct((local, up_rows, ff), f32),
        ],
        grid_spec=pltpu.PrefetchScalarGridSpec(
            num_scalar_prefetch=1,
            grid=(shares,),
            in_specs=[pl.BlockSpec((1, blocks, rows, columns), lambda p, order: (p, 0, 0, 0)), home, home]
            + [pl.BlockSpec((local, part, ff), lambda p, order: (0, p, 0))],
            out_specs=[pl.BlockSpec((rows, width), at)] * 4
            + [pl.BlockSpec((dealt, width), at)] * 2
            + [pl.BlockSpec((local, part, ff), lambda p, order: (0, p, 0))],
        ),
        compiler_params=pltpu.CompilerParams(vmem_limit_bytes=kernel_vmem),
        cost_estimate=small_cost,
        name="assemble",
    )(order_row, x, grad_home, out_home, last)


def pad_rows(flat, tile):
    rows = -(-flat.shape[0] // (128 * tile)) * tile
    return jnp.pad(flat, (0, rows * 128 - flat.shape[0])).reshape(rows, 128)


def einf(spec, left, right):
    return jnp.einsum(spec, left, right, preferred_element_type=f32)


def body(
    tokens,
    cotangent,
    lengths,
    deal_order,
    routes,
    balance_coef,
    w_query,
    w_key,
    w_value,
    w_out,
    w_router,
    attn_gain,
    mlp_gain,
    query_gain,
    key_gain,
    w_gate,
    w_up,
    w_down,
):
    groups = lax.axis_size("expert")
    replicas = lax.axis_size("dp")
    me = lax.axis_index("expert")
    tok_rows, width = tokens.shape
    block_rows = tok_rows // replicas
    total_slots = float(tok_rows * replicas * groups)
    shard_rows = w_query.shape[0]
    local_experts = w_gate.shape[0]
    experts = local_experts * groups
    top_k = routes.shape[1]
    capacity = tok_rows * top_k * 9 // (8 * experts)

    order_row = lax.dynamic_index_in_dim(deal_order, me, 0, keepdims=False)
    dp_ids = jnp.arange(replicas, dtype=jnp.int32)
    matched = (order_row[:, None] == dp_ids[None, :]).astype(jnp.int32)
    inverse_order = jnp.sum(matched * dp_ids[:, None], axis=0)

    def blocks_to_deal(values):
        return values.reshape(replicas, block_rows, width)[inverse_order]

    small = jnp.concatenate(
        [w_router.reshape(-1), attn_gain, mlp_gain, query_gain, key_gain]
    )
    ints = jnp.concatenate([routes.reshape(-1), jnp.broadcast_to(lengths, (top_k,))])
    small_all, ints_all, seq_tokens, w_qkv = front(
        groups,
        replicas,
        0,
        pad_rows(small, 16),
        pad_rows(ints, 8),
        blocks_to_deal(tokens),
        w_query,
        w_key,
        w_value,
    )
    small_all, ints_all = small_all.reshape(groups, -1), ints_all.reshape(groups, -1)
    w_qkv = w_qkv.reshape(width, -1)
    n_router = shard_rows * experts
    cuts = [0, n_router]
    for gain in (attn_gain, mlp_gain, query_gain, key_gain):
        cuts.append(cuts[-1] + gain.shape[0])
    router_full = small_all[:, :n_router].reshape(width, experts)
    attn_g, mlp_g, query_g, key_g = (
        small_all[:, cuts[i] : cuts[i + 1]].reshape(-1).astype(f32) for i in range(1, 5)
    )
    head_dim = query_g.shape[0]
    local_width = w_query.shape[1] // groups

    routes_all = ints_all[:, : tok_rows * top_k].reshape(groups, tok_rows, top_k)
    lengths_all = ints_all[:, tok_rows * top_k]
    positions = jnp.arange(tok_rows, dtype=jnp.int32)
    live_all = (positions[None, :] < lengths_all[:, None]).astype(f32)
    live_rows = (positions < lengths[0]).astype(f32)

    inputs = seq_tokens.astype(f32)
    normed, inv_first = norm_fwd(inputs, attn_g)
    attn_in = normed.astype(bf16)
    attn_all, seq_cot = gather_rows(
        attn_in, groups, replicas, 1, riders=[Deal(blocks_to_deal(cotangent), groups, replicas)]
    )
    grad_output = seq_cot.astype(f32) * live_rows[:, None]
    cot_all = lax.all_gather(grad_output.astype(bf16), "expert", axis=0, tiled=False)

    cosine, signed_sine = rotary_tables(tok_rows, head_dim)
    mixed, hidden_part = attend(
        lengths_all, attn_all, w_qkv, w_out, query_g, key_g, cosine, signed_sine
    )
    hidden = inputs + scatter_sum(hidden_part, groups, replicas, 8)[0]
    mlp_normed, inv_second = norm_fwd(hidden, mlp_g)
    mlp_in = mlp_normed.astype(bf16)
    logits = einf("td,de->te", mlp_in, router_full)
    my_router = jax.nn.softmax(logits, axis=-1)
    mlp_all, router = gather_rows(
        mlp_in,
        groups,
        replicas,
        2,
        riders=[SmallGather(pad_rows(my_router.reshape(-1), 8), groups, replicas)],
    )
    router = router.reshape(groups, -1)[:, : tok_rows * experts].reshape(groups, tok_rows, experts)
    expert_ids = jnp.arange(experts, dtype=jnp.int32)
    picked = jnp.sum(
        (routes_all[:, :, :, None] == expert_ids).astype(f32), axis=2
    )
    chosen_sum = jnp.sum(picked * router, axis=-1, keepdims=True)
    gates = picked * router / chosen_sum
    counts = jnp.sum(picked * live_all[:, :, None], axis=(0, 1))
    prob_sums = jnp.sum(router * live_all[:, :, None], axis=(0, 1))
    live_count = jnp.sum(live_all)[None]
    stats = pad_rows(jnp.concatenate([counts, prob_sums, live_count]), 8)

    first = me * local_experts
    own_picked = lax.dynamic_slice_in_dim(picked, first, local_experts, 2)
    own_gates = lax.dynamic_slice_in_dim(gates, first, local_experts, 2)
    before = (positions[:, None] > positions[None, :]).astype(bf16)
    rank = einf("tu,suj->jst", before, own_picked.astype(bf16))
    own_picked = own_picked.transpose(2, 0, 1)
    own_gates = own_gates.transpose(2, 0, 1)
    slot_of = jnp.where(own_picked > 0.5, rank.astype(jnp.int32), -1)
    expert_in, grad_recv, act_low, gate_in, up_in, total_down = [], [], [], [], [], []
    for j in range(local_experts):
        taken, recv, act, gate, up = expert_forward(
            mlp_all, cot_all, slot_of, own_gates, w_gate, w_up, capacity, j
        )
        grad_down_w = einf("rf,rd->fd", act[0], recv[0]).astype(bf16)
        act, recv, mlp_all, grad_down_w = lax.optimization_barrier((act, recv, mlp_all, grad_down_w))
        total_down.append(lax.psum_scatter(grad_down_w, "dp", scatter_dimension=0, tiled=True))
        for values, value in zip(
            (expert_in, grad_recv, act_low, gate_in, up_in), (taken, recv, act, gate, up)
        ):
            values.append(value)
    grad_gate_in, grad_up_in, grad_part = expert_back(
        grad_recv, gate_in, up_in, slot_of, w_gate, w_up, w_down, groups, tok_rows, capacity
    )
    grad_gate_w = jnp.stack(
        [einf("rd,rf->df", expert_in[j][0], grad_gate_in[j]).astype(bf16) for j in range(local_experts)]
    )
    grad_part, act_low, grad_gate_w = lax.optimization_barrier((grad_part, act_low, grad_gate_w))
    total_gate = lax.psum_scatter(grad_gate_w, "dp", scatter_dimension=1, tiled=True)
    sum_part, own_grad_gates = expert_combine(act_low, cot_all, slot_of, own_gates, w_down, capacity)
    gate_rows = own_grad_gates.transpose(1, 0, 2, 3).reshape(groups, -1, 128)
    grad_mlp_in, gate_back, sums = scatter_sum(
        grad_part,
        groups,
        replicas,
        3,
        riders=[Exchange(gate_rows, groups, replicas), DpSum(stats, groups, replicas)],
    )
    sums = sums.reshape(-1)
    counts, prob_sums = sums[:experts], sums[experts : 2 * experts]
    live_count = sums[2 * experts : 2 * experts + 1]
    fraction = counts / (live_count * top_k)
    balance_loss = balance_coef * (experts * jnp.sum(fraction * prob_sums / total_slots))

    grad_gates = gate_back.reshape(experts, tok_rows).T
    my_picked = lax.dynamic_index_in_dim(picked, me, 0, keepdims=False)
    my_gates = lax.dynamic_index_in_dim(gates, me, 0, keepdims=False)
    my_sum = lax.dynamic_index_in_dim(chosen_sum, me, 0, keepdims=False)
    grad_prob = (
        my_picked * (grad_gates - jnp.sum(grad_gates * my_gates, axis=1, keepdims=True)) / my_sum
        + live_rows[:, None] * (balance_coef * experts / total_slots) * fraction[None, :]
    )
    grad_logits = (
        my_router * (grad_prob - jnp.sum(my_router * grad_prob, axis=-1, keepdims=True))
    ).astype(bf16)
    grad_router_w = einf("td,te->de", mlp_in, grad_logits)
    grad_mlp_in = grad_mlp_in + einf("te,de->td", grad_logits, router_full)

    grad_hidden_norm, grad_mlp_g = norm_back(hidden, inv_second, mlp_g, grad_mlp_in, 0)
    grad_hidden = grad_output + grad_hidden_norm
    grad_hidden_low = grad_hidden.astype(bf16)
    grad_hidden_low, total_down = lax.optimization_barrier((grad_hidden_low, total_down))
    (hidden_all,) = gather_rows(grad_hidden_low, groups, replicas, 4)
    grad_attn_part, grad_attn_w, grad_gains = attend_back(
        lengths_all, attn_all, hidden_all, mixed, w_qkv, w_out, query_g, key_g, cosine, signed_sine
    )
    grad_query_g, grad_key_g = grad_gains[0], grad_gains[1]
    attn_share = lax.psum_scatter(
        grad_attn_w.reshape(groups, shard_rows, 4 * local_width), "dp", scatter_dimension=1, tiled=True
    )
    sum_part, grad_attn_part = lax.optimization_barrier((sum_part, grad_attn_part))
    (expert_sum,) = scatter_sum(sum_part, groups, replicas, 6)
    out_seq = (live_rows[:, None] * (hidden + expert_sum)).astype(bf16)

    def to_deal(values):
        return values.reshape(replicas, block_rows, width)

    grad_up_in, out_seq, total_gate = lax.optimization_barrier((grad_up_in, out_seq, total_gate))
    total_gate = total_gate.astype(f32)
    total_gate, grad_attn_part = lax.optimization_barrier((total_gate, grad_attn_part))
    grad_up_w = [
        einf("rd,rf->df", expert_in[j][0], grad_up_in[j]).astype(bf16) for j in range(local_experts)
    ]
    grad_up_w, grad_attn_part = lax.optimization_barrier((grad_up_w, grad_attn_part))
    grad_attn_in, out_home = scatter_sum(
        grad_attn_part, groups, replicas, 5, riders=[Deal(to_deal(out_seq), groups, replicas)]
    )
    grad_input_norm, grad_attn_g = norm_back(inputs, inv_first, attn_g, grad_attn_in, 0)
    grad_seq = (grad_hidden + grad_input_norm).astype(bf16)

    pieces = [grad_router_w.reshape(groups, n_router)] + [
        value.reshape(groups, -1) for value in (grad_attn_g, grad_mlp_g, grad_query_g, grad_key_g)
    ]
    pieces = jnp.concatenate(pieces, axis=1)
    pad = -pieces.shape[1] % 1024
    pieces = jnp.pad(pieces, ((0, 0), (0, pad))).reshape(groups, -1, 128)

    pieces, grad_seq, attn_share = lax.optimization_barrier((pieces, grad_seq, attn_share))
    attn_sum, total_up, sum_small, grad_home = close(
        attn_share,
        3 * local_width,
        grad_up_w,
        groups,
        replicas,
        7,
        [SmallSum(pieces, groups, replicas), Deal(to_deal(grad_seq), groups, replicas)],
    )
    sum_q, sum_k, sum_v, sum_o, grad_input, output, total_up = assemble(
        order_row, attn_sum, to_deal(grad_home), to_deal(out_home), total_up
    )
    sum_small = sum_small.reshape(-1)
    sum_r = sum_small[:n_router].reshape(shard_rows, experts)
    sum_ga, sum_gm, sum_gq, sum_gk = (sum_small[cuts[i] : cuts[i + 1]] for i in range(1, 5))
    total_down = jnp.stack(total_down).astype(f32)
    return (
        output,
        balance_loss,
        grad_input,
        sum_q,
        sum_k,
        sum_v,
        sum_o,
        sum_r,
        sum_ga,
        sum_gm,
        sum_gq,
        sum_gk,
        total_gate,
        total_up,
        total_down,
    )


def solution(mesh):
    rows = P(("dp", "expert"), None)
    weight = P("expert", None)
    gain = P("expert")
    cube = P("expert", None, None)
    cube_out = P("expert", "dp", None)
    return jax.shard_map(
        body,
        mesh=mesh,
        in_specs=(
            (rows, rows, P(("dp", "expert")), P(), rows, P())
            + (weight,) * 5
            + (gain,) * 4
            + (cube,) * 3
        ),
        out_specs=(
            (rows, P(), rows) + (weight,) * 5 + (gain,) * 4 + (cube_out,) * 3
        ),
        check_vma=False,
    )
```

```python
import functools
import math

import jax
import jax.numpy as jnp
from jax import lax
from jax.experimental import pallas as pl
from jax.experimental.pallas import tpu as pltpu
from jax.sharding import PartitionSpec as P

norm_eps = 1e-06
rope_base = 50000.0
big_negative = -1e30
bf16 = jnp.bfloat16
f32 = jnp.float32
MESH = pl.DeviceIdType.MESH
DMA = pltpu.SemaphoreType.DMA
kernel_vmem = 62 << 20
small_cost = pl.CostEstimate(flops=0, transcendentals=0, bytes_accessed=1024)


def norm_fwd(values, scales):
    inverse = lax.rsqrt(jnp.mean(values * values, axis=-1, keepdims=True) + norm_eps)
    return (values * inverse * scales, inverse)


def norm_back(values, inverse, scales, grad_out, sum_axes):
    scaled = grad_out * scales
    grad_in = inverse * (
        scaled - values * inverse * inverse * jnp.mean(scaled * values, axis=-1, keepdims=True)
    )
    grad_scale = jnp.sum(grad_out * values * inverse, axis=sum_axes)
    return (grad_in, grad_scale)


def rotary_tables(tok_rows, head_dim):
    half_dim = head_dim // 2
    positions = jnp.arange(tok_rows, dtype=jnp.int32).astype(f32)
    frequency = rope_base ** (-jnp.arange(half_dim, dtype=jnp.int32).astype(f32) * 2.0 / head_dim)
    angles = positions[:, None] * frequency[None, :]
    cosine = jnp.concatenate([jnp.cos(angles), jnp.cos(angles)], axis=-1)
    signed_sine = jnp.concatenate([-jnp.sin(angles), jnp.sin(angles)], axis=-1)
    return (cosine, signed_sine)


def peer(index):
    return {"expert": index}


def remote(src, dst, send, recv, to):
    return pltpu.make_async_remote_copy(
        src_ref=src, dst_ref=dst, send_sem=send, recv_sem=recv, device_id=peer(to), device_id_type=MESH
    )


def greet(n, me, replicas=1):
    barrier = pltpu.get_barrier_semaphore()
    for k in range(1, n):
        pl.semaphore_signal(
            barrier, inc=1, device_id=peer(lax.rem(me + k, n)), device_id_type=MESH
        )
    for k in range(1, replicas):
        other = lax.rem(lax.axis_index("dp") + k, replicas)
        pl.semaphore_signal(barrier, inc=1, device_id={"dp": other}, device_id_type=MESH)
    pl.semaphore_wait(barrier, n + replicas - 2)


def quad_places(me):
    core = lax.rem(me, 2)
    chip = me // 2
    x = lax.rem(chip, 2)
    y = chip // 2

    def at(px, py, pc):
        return (py * 2 + px) * 2 + pc

    spots = ((x, y), (1 - x, y), (x, 1 - y), (1 - x, 1 - y))
    return [at(px, py, core) for px, py in spots], [at(px, py, 1 - core) for px, py in spots]


def any_places(n, me):
    core = lax.rem(me, 2)
    chip = me // 2
    chips = n // 2
    chip_of = [lax.rem(chip + k, chips) for k in range(chips)]
    chip_from = [lax.rem(chip - k + chips, chips) for k in range(chips)]
    return (
        [c * 2 + core for c in chip_of],
        [c * 2 + 1 - core for c in chip_of],
        [c * 2 + core for c in chip_from],
        [c * 2 + 1 - core for c in chip_from],
    )


def deal_copies(replicas, src, dst, own_sem, send_sem, recv_sem):
    here = lax.axis_index("dp")
    rows = src.shape[1]
    mine = pl.ds(here * rows, rows)
    own = pltpu.make_async_copy(src.at[here], dst.at[mine], own_sem)
    away = []
    for k in range(1, replicas):
        to = lax.rem(here + k, replicas)
        away.append(
            pltpu.make_async_remote_copy(
                src_ref=src.at[to],
                dst_ref=dst.at[mine],
                send_sem=send_sem.at[k],
                recv_sem=recv_sem.at[k],
                device_id={"dp": to},
                device_id_type=MESH,
            )
        )
    return own, away


def front_kernel(
    n,
    replicas,
    small,
    ints,
    blocks,
    wq,
    wk,
    wv,
    small_all,
    ints_all,
    seq,
    w_all,
    small_send,
    small_recv,
    own_sem,
    deal_send,
    deal_recv,
    w_own,
    w_send,
    w_recv,
):
    me = lax.axis_index("expert")
    wide = wq.shape[1] // n
    small_all[me] = small[...]
    ints_all[me] = ints[...]
    own, away = deal_copies(replicas, blocks, seq, own_sem, deal_send, deal_recv)
    own.start()

    def columns(weight, index):
        return weight.at[:, pl.ds(pl.multiple_of(index * wide, wide), wide)]

    kept = []
    for i, weight in enumerate((wq, wk, wv)):
        copy = pltpu.make_async_copy(
            columns(weight, me), w_all.at[me, :, pl.ds(i * wide, wide)], w_own.at[i]
        )
        copy.start()
        kept.append(copy)
    greet(n, me, replicas)
    copies = []

    def go(copy):
        copy.start()
        copies.append(copy)

    for k in range(1, n):
        to = lax.rem(me + k, n)
        go(remote(small, small_all.at[me], small_send.at[0, k], small_recv.at[0, k], to))
        go(remote(ints, ints_all.at[me], small_send.at[1, k], small_recv.at[1, k], to))
    for copy in away:
        go(copy)
    for k in range(1, n):
        to = lax.rem(me + k, n)
        for i, weight in enumerate((wq, wk, wv)):
            go(
                remote(
                    columns(weight, to),
                    w_all.at[me, :, pl.ds(i * wide, wide)],
                    w_send.at[i, k],
                    w_recv.at[i, k],
                    to,
                )
            )
    for copy in copies:
        copy.wait()
    own.wait()
    for copy in kept:
        copy.wait()


def front(n, replicas, collective_id, small, ints, blocks, wq, wk, wv):
    vmem = pl.BlockSpec(memory_space=pltpu.VMEM)
    away = pl.BlockSpec(memory_space=pl.ANY)
    rows, width = wq.shape
    return pl.pallas_call(
        functools.partial(front_kernel, n, replicas),
        out_shape=[
            jax.ShapeDtypeStruct((n,) + small.shape, small.dtype),
            jax.ShapeDtypeStruct((n,) + ints.shape, ints.dtype),
            jax.ShapeDtypeStruct((replicas * blocks.shape[1], width), bf16),
            jax.ShapeDtypeStruct((n, rows, 3 * (width // n)), bf16),
        ],
        in_specs=[vmem, vmem, away, away, away, away],
        out_specs=[vmem, vmem, away, away],
        scratch_shapes=[
            DMA((2, n)),
            DMA((2, n)),
            DMA,
            DMA((replicas,)),
            DMA((replicas,)),
            DMA((3,)),
            DMA((3, n)),
            DMA((3, n)),
        ],
        compiler_params=pltpu.CompilerParams(
            collective_id=collective_id, has_side_effects=True, vmem_limit_bytes=kernel_vmem
        ),
        cost_estimate=small_cost,
        name="front",
    )(small, ints, blocks, wq, wk, wv)


VMEM_SPEC = pl.BlockSpec(memory_space=pltpu.VMEM)
AWAY_SPEC = pl.BlockSpec(memory_space=pl.ANY)


def along_dp(src, dst, send, recv, to):
    return pltpu.make_async_remote_copy(
        src_ref=src, dst_ref=dst, send_sem=send, recv_sem=recv, device_id={"dp": to}, device_id_type=MESH
    )


class Exchange:
    over_dp = False

    def __init__(self, x, n, replicas, columns=None):
        self.n = n
        self.columns = columns or x.shape[2]
        self.ins = [(x, VMEM_SPEC)]
        self.outs = [(jax.ShapeDtypeStruct(x.shape, x.dtype), VMEM_SPEC)]
        self.scratch = [DMA((n,)), DMA((n,))]

    def start(self, me, src, out, send, recv):
        cols = pl.ds(0, self.columns)
        self.copies = []
        for k in range(1, self.n):
            to = lax.rem(me + k, self.n)
            self.copies.append(
                remote(src.at[to, :, cols], out.at[me, :, cols], send.at[k], recv.at[k], to)
            )
            self.copies[-1].start()
        out[me, :, : self.columns] = src[me, :, : self.columns]
        if self.columns < src.shape[2]:
            out[:, :, self.columns :] = src[:, :, self.columns :]

    def finish(self, me, *refs):
        for copy in self.copies:
            copy.wait()


class DpSum:
    over_dp = True

    def __init__(self, x, n, replicas):
        self.replicas = replicas
        self.ins = [(x, VMEM_SPEC)]
        self.outs = [(jax.ShapeDtypeStruct(x.shape, x.dtype), VMEM_SPEC)]
        self.scratch = [pltpu.VMEM((replicas,) + x.shape, x.dtype), DMA((replicas,)), DMA((replicas,))]

    def start(self, me, src, out, got, send, recv):
        here = lax.axis_index("dp")
        got[here] = src[...]
        self.copies = []
        for k in range(1, self.replicas):
            to = lax.rem(here + k, self.replicas)
            self.copies.append(along_dp(src, got.at[here], send.at[k], recv.at[k], to))
            self.copies[-1].start()

    def finish(self, me, src, out, got, send, recv):
        for copy in self.copies:
            copy.wait()
        value = got[0]
        for k in range(1, self.replicas):
            value = value + got[k]
        out[...] = value


class SmallSum:
    over_dp = True

    def __init__(self, x, n, replicas):
        self.n, self.replicas = n, replicas
        shape = x.shape[1:]
        self.ins = [(x, VMEM_SPEC)]
        self.outs = [(jax.ShapeDtypeStruct(shape, f32), VMEM_SPEC)]
        self.scratch = [pltpu.VMEM(x.shape, f32), pltpu.VMEM((replicas,) + shape, f32)]
        self.scratch += [DMA((n,)), DMA((n,)), DMA((replicas,)), DMA((replicas,))]

    def start(self, me, src, out, got, total, send, recv, over_send, over_recv):
        got[me] = src[me]
        self.copies = []
        for k in range(1, self.n):
            to = lax.rem(me + k, self.n)
            self.copies.append(remote(src.at[to], got.at[me], send.at[k], recv.at[k], to))
            self.copies[-1].start()

    def finish(self, me, src, out, got, total, send, recv, over_send, over_recv):
        here = lax.axis_index("dp")
        for copy in self.copies:
            copy.wait()
        value = got[0]
        for k in range(1, self.n):
            value = value + got[k]
        total[here] = value
        copies = []
        for k in range(1, self.replicas):
            to = lax.rem(here + k, self.replicas)
            copies.append(along_dp(total.at[here], total.at[here], over_send.at[k], over_recv.at[k], to))
            copies[-1].start()
        for copy in copies:
            copy.wait()
        value = total[0]
        for k in range(1, self.replicas):
            value = value + total[k]
        out[...] = value


class Deal:
    over_dp = True

    def __init__(self, blocks, n, replicas):
        self.replicas = replicas
        _, rows, width = blocks.shape
        self.ins = [(blocks, AWAY_SPEC)]
        self.outs = [(jax.ShapeDtypeStruct((replicas * rows, width), blocks.dtype), AWAY_SPEC)]
        self.scratch = [DMA, DMA((replicas,)), DMA((replicas,))]

    def start(self, me, src, out, own, send, recv):
        kept, away = deal_copies(self.replicas, src, out, own, send, recv)
        kept.start()
        for copy in away:
            copy.start()
        self.copies = away + [kept]

    def finish(self, me, *refs):
        for copy in self.copies:
            copy.wait()


class DpGather:
    over_dp = True

    def __init__(self, x, n, replicas, parts=4):
        self.replicas, self.parts = replicas, parts
        self.size = x.shape[0] // parts
        self.ins = [(x, AWAY_SPEC)]
        self.outs = [(jax.ShapeDtypeStruct((replicas,) + x.shape, x.dtype), AWAY_SPEC)]
        self.scratch = [DMA, DMA((2, replicas, parts)), DMA((2, replicas, parts))]

    def piece(self, p):
        return pl.ds(p * self.size, self.size)

    def hop(self, src, out, send, recv, way, k, p):
        here = lax.axis_index("dp")
        step = 1 - 2 * way
        block = out.at[here - step * k, self.piece(p)]
        origin = block if k else src.at[self.piece(p)]
        return along_dp(origin, block, send.at[way, k, p], recv.at[way, k, p], here + step)

    def sends(self, way, k):
        here = lax.axis_index("dp")
        last = self.replicas - 1
        if way == 0:
            return (here >= k) & (here < last), here >= k + 1
        return (here + k <= last) & (here > 0), here + k + 1 <= last

    def start(self, me, src, out, own, send, recv):
        self.copy = pltpu.make_async_copy(src, out.at[lax.axis_index("dp")], own)
        self.copy.start()
        for way in range(2):

            @pl.when(self.sends(way, 0)[0])
            def _():
                for p in range(self.parts):
                    self.hop(src, out, send, recv, way, 0, p).start()

    def steps(self, src, out, own, send, recv):
        here = lax.axis_index("dp")
        for k in range(self.replicas - 1):
            for p in range(self.parts):
                for way in range(2):

                    @pl.when(self.sends(way, k)[1])
                    def _():
                        block = out.at[here - (1 - 2 * way) * (k + 1), self.piece(p)]
                        along_dp(
                            block, block, send.at[way, k, p], recv.at[way, k, p], here
                        ).wait_recv()

                    if k + 1 < self.replicas - 1:

                        @pl.when(self.sends(way, k + 1)[0])
                        def _():
                            self.hop(src, out, send, recv, way, k + 1, p).start()

                yield

        for k in range(self.replicas - 1):
            for way in range(2):

                @pl.when(self.sends(way, k)[0])
                def _():
                    for p in range(self.parts):
                        self.hop(src, out, send, recv, way, k, p).wait_send()

        self.copy.wait()


class LineSum:
    def __init__(self, values, n, replicas, parts=8):
        self.replicas, self.parts = replicas, parts
        self.blocks = len(values)
        rows, columns = values[0].shape
        self.rows = rows // replicas
        self.size = self.rows // parts
        held = pltpu.VMEM((replicas, self.blocks, self.rows, columns), bf16)
        self.ins = [(x, AWAY_SPEC) for x in values]
        self.outs = [(jax.ShapeDtypeStruct((self.blocks, self.rows, columns), f32), VMEM_SPEC)]
        sems = DMA((2, replicas, parts))
        self.scratch = [held, held, held, DMA((self.blocks, replicas, parts)), sems, sems]

    def loads(self, values, own, sem, c, p):
        rows = pl.ds(pl.multiple_of(c * self.rows + p * self.size, self.size), self.size)
        return [
            pltpu.make_async_copy(
                x.at[rows], own.at[c, b, pl.ds(p * self.size, self.size)], sem.at[b, c, p]
            )
            for b, x in enumerate(values)
        ]

    def hop(self, own, got, send, recv, way, c, p):
        here = lax.axis_index("dp")
        rows = pl.ds(p * self.size, self.size)
        return along_dp(
            own.at[c, :, rows],
            got.at[c, :, rows],
            send.at[way, c, p],
            recv.at[way, c, p],
            here + 1 - 2 * way,
        )

    def add(self, total, got, c, p, widen=None):
        chunk = min(self.size, 32)
        for b in range(self.blocks):

            @pl.loop(0, self.size // chunk)
            def _(i):
                rows = pl.ds(p * self.size + i * chunk, chunk)
                if widen is None:
                    value = total[c, b, rows].astype(f32) + got[c, b, rows].astype(f32)
                    total[c, b, rows] = value.astype(bf16)
                elif got is None:
                    widen[b, rows] = total[c, b, rows].astype(f32)
                else:
                    widen[b, rows] = widen[b, rows] + got[c, b, rows].astype(f32)

    def start(self, values, own, sem):
        for t in range(self.replicas):
            for p in range(self.parts):
                for copy in self.loads(values, own, sem, t, p):
                    copy.start()

    def steps(self, values, out, own, up, down, sem, send, recv):
        here = lax.axis_index("dp")
        last = self.replicas - 1
        for t in range(last):
            for p in range(self.parts):
                for way, c, got in ((0, last - t, up), (1, t, down)):
                    bound = here < c if way == 0 else here > c
                    inner = here > 0 if way == 0 else here < last

                    @pl.when(bound)
                    def _():
                        for copy in self.loads(values, own, sem, c, p):
                            copy.wait()

                        @pl.when(inner)
                        def _():
                            self.hop(own, got, send, recv, way, c, p).wait_recv()
                            self.add(own, got, c, p)

                        self.hop(own, got, send, recv, way, c, p).start()

                yield
        for p in range(self.parts):
            for copy in self.loads(values, own, sem, here, p):
                copy.wait()
            self.add(own, None, here, p, out)
            for way, got, inner in ((0, up, here > 0), (1, down, here < last)):

                @pl.when(inner)
                def _():
                    self.hop(own, got, send, recv, way, here, p).wait_recv()
                    self.add(own, got, here, p, out)

        for t in range(last):
            for p in range(self.parts):
                for way, c, got in ((0, last - t, up), (1, t, down)):

                    @pl.when(here < c if way == 0 else here > c)
                    def _():
                        self.hop(own, got, send, recv, way, c, p).wait_send()


def close_kernel(exchange, gather, line, meet, share, *refs):
    values, (full, out, rows), refs = refs[: line.blocks], refs[line.blocks :][:3], refs[line.blocks + 3 :]
    swap_refs, refs = refs[:2], refs[2:]
    gather_refs, line_refs = refs[: len(gather.scratch)], refs[len(gather.scratch) :]
    me = lax.axis_index("expert")
    line.start(values, line_refs[0], line_refs[3])
    meet(me)
    exchange.start(me, share, rows, *swap_refs)
    running = [line.steps(values, out, *line_refs)]
    next(running[0])
    exchange.finish(me)
    gather.start(me, rows, full, *gather_refs)
    running.append(gather.steps(rows, full, *gather_refs))
    turn = 0
    while running:
        turn += 1
        running = [r for i, r in enumerate(running) if (i and turn % 2) or next(r, True) is None]


def close(attn_share, columns, grad_up_w, n, replicas, collective_id, riders):
    exchange = Exchange(attn_share, n, replicas, columns)
    gather = DpGather(attn_share, n, replicas)
    line = LineSum(grad_up_w, n, replicas)
    return riding_call(
        n,
        replicas,
        functools.partial(close_kernel, exchange, gather, line),
        exchange.ins + line.ins,
        gather.outs + line.outs,
        [pltpu.VMEM(attn_share.shape, bf16)] + exchange.scratch + gather.scratch + line.scratch,
        riders,
        collective_id,
        "close",
    )


class SmallGather:
    over_dp = False

    def __init__(self, x, n, replicas):
        self.n = n
        self.ins = [(x, VMEM_SPEC)]
        self.outs = [(jax.ShapeDtypeStruct((n,) + x.shape, x.dtype), VMEM_SPEC)]
        self.scratch = [DMA((n,)), DMA((n,))]

    def start(self, me, src, out, send, recv):
        out[me] = src[...]
        self.copies = []
        for k in range(1, self.n):
            to = lax.rem(me + k, self.n)
            self.copies.append(remote(src, out.at[me], send.at[k], recv.at[k], to))
            self.copies[-1].start()

    def finish(self, me, *refs):
        for copy in self.copies:
            copy.wait()


def riding_kernel(n, replicas, main, counts, riders, *refs):
    n_in, n_out, n_scratch = counts
    at = [0]

    def take(count):
        at[0] += count
        return refs[at[0] - count : at[0]]

    main_in = take(n_in)
    rider_in = [take(len(r.ins)) for r in riders]
    main_out = take(n_out)
    rider_out = [take(len(r.outs)) for r in riders]
    main_scratch = take(n_scratch)
    rider_refs = [i + o + take(len(r.scratch)) for r, i, o in zip(riders, rider_in, rider_out)]

    def meet(me):
        greet(n, me, replicas if any(r.over_dp for r in riders) else 1)
        for rider, own in zip(riders, rider_refs):
            rider.start(me, *own)

    main(meet, *main_in, *main_out, *main_scratch)
    me = lax.axis_index("expert")
    for rider, own in zip(riders, rider_refs):
        rider.finish(me, *own)


def riding_call(n, replicas, main, ins, outs, scratch, riders, collective_id, name):
    pairs_in = ins + [pair for r in riders for pair in r.ins]
    pairs_out = outs + [pair for r in riders for pair in r.outs]
    counts = (len(ins), len(outs), len(scratch))
    return pl.pallas_call(
        functools.partial(riding_kernel, n, replicas, main, counts, riders),
        out_shape=[shape for shape, _ in pairs_out],
        in_specs=[spec for _, spec in pairs_in],
        out_specs=[spec for _, spec in pairs_out],
        scratch_shapes=scratch + [shape for r in riders for shape in r.scratch],
        compiler_params=pltpu.CompilerParams(
            collective_id=collective_id, has_side_effects=True, vmem_limit_bytes=kernel_vmem
        ),
        cost_estimate=small_cost,
        name=name,
    )(*[value for value, _ in pairs_in])


def ride_only(meet, *refs):
    meet(lax.axis_index("expert"))


def quad_gather_kernel(parts, meet, x_ref, o_ref, own_sem, send_sem, recv_sem, pass_sem, pair_send, pair_recv):
    me = lax.axis_index("expert")
    same, other = quad_places(me)
    step = x_ref.shape[0] // parts
    half = parts // 2
    own = pltpu.make_async_copy(x_ref, o_ref.at[me], own_sem)
    own.start()
    meet(me)
    started = []

    def go(copy):
        copy.start()
        started.append(copy)

    def piece(p):
        return pl.ds(p * step, step)

    low, high = list(range(half)), list(range(half, parts))
    turns = [(k, seq[i]) for i in range(parts) for k, seq in ((1, high + low), (2, low + high))]
    for k, p in turns:
        go(remote(x_ref.at[piece(p)], o_ref.at[me, piece(p)], send_sem.at[k, p], recv_sem.at[k, p], same[k]))
    for p in range(parts):
        go(remote(x_ref.at[piece(p)], o_ref.at[me, piece(p)], pair_send.at[0, p], pair_recv.at[0, p], other[0]))

    def arrive(k, p):
        block = o_ref.at[same[k], piece(p)]
        remote(block, block, send_sem.at[k, p], recv_sem.at[k, p], other[0]).wait_recv()
        return block

    for k, p in turns:
        block = arrive(k, p)
        if (p >= half) == (k == 1):
            go(remote(block, block, pass_sem.at[p], recv_sem.at[3, p], same[3 - k]))
        go(remote(block, block, pair_send.at[k, p], pair_recv.at[k, p], other[0]))
    for pair in zip(low, high):
        for p in pair:
            block = arrive(3, p)
            go(remote(block, block, pair_send.at[3, p], pair_recv.at[3, p], other[0]))
    for k in range(4):
        for p in range(parts):
            block = o_ref.at[other[k], piece(p)]
            remote(block, block, pair_send.at[k, p], pair_recv.at[k, p], other[0]).wait_recv()
    for copy in started:
        copy.wait_send()
    own.wait()


def any_gather_kernel(n, meet, x_ref, o_ref, own_sem, send_sem, recv_sem, pair_send, pair_recv):
    me = lax.axis_index("expert")
    same, other, same_from, other_from = any_places(n, me)
    own = pltpu.make_async_copy(x_ref, o_ref.at[me], own_sem)
    own.start()
    meet(me)
    started = []
    for k in range(n // 2):
        if k:
            copy = remote(x_ref, o_ref.at[me], send_sem.at[k], recv_sem.at[k], same[k])
        else:
            copy = remote(x_ref, o_ref.at[me], pair_send.at[0], pair_recv.at[0], other[0])
        copy.start()
        started.append(copy)
    for k in range(1, n // 2):
        block = o_ref.at[same_from[k]]
        remote(block, block, send_sem.at[k], recv_sem.at[k], other[0]).wait_recv()
        copy = remote(block, block, pair_send.at[k], pair_recv.at[k], other[0])
        copy.start()
        started.append(copy)
    for k in range(n // 2):
        block = o_ref.at[other_from[k]]
        remote(block, block, pair_send.at[k], pair_recv.at[k], other[0]).wait_recv()
    for copy in started:
        copy.wait_send()
    own.wait()


def gather_plan(n, parts):
    chips = n // 2
    if n == 8:
        sems = [DMA, DMA((4, parts)), DMA((4, parts)), DMA((parts,)), DMA((4, parts)), DMA((4, parts))]
        return functools.partial(quad_gather_kernel, parts), sems
    sems = [DMA, DMA((chips,)), DMA((chips,)), DMA((chips,)), DMA((chips,))]
    return functools.partial(any_gather_kernel, n), sems


def gather_rows(x, n, replicas, collective_id, riders=(), parts=4):
    kernel, sems = gather_plan(n, parts)
    out = jax.ShapeDtypeStruct((n,) + x.shape, x.dtype)
    return riding_call(
        n,
        replicas,
        kernel,
        [(x, AWAY_SPEC)],
        [(out, AWAY_SPEC)],
        sems,
        list(riders),
        collective_id,
        f"gather_rows_{collective_id}",
    )


def add_rows(total, first, rows, chunk, *terms):
    @pl.loop(0, rows // chunk)
    def _(i):
        s = pl.ds(first + i * chunk, chunk)
        value = terms[0][s].astype(f32)
        for term in terms[1:]:
            value = value + term[s].astype(f32)
        total[s] = value.astype(total.dtype)


def quad_scatter_kernel(
    parts, meet, p_ref, o_ref, mine, theirs, transit, got, load_sem, pair_send, pair_recv, over_send, over_recv, send_sem, recv_sem
):
    me = lax.axis_index("expert")
    same, other = quad_places(me)
    step = p_ref.shape[1] // parts
    half = parts // 2
    low, high = list(range(half)), list(range(half, parts))
    mix = [p for pair in zip(low, high) for p in pair]
    order = (3, 1, 2, 0)

    def piece(p):
        return pl.ds(p * step, step)

    loads = {}
    for k in order:
        for p in mix:
            loads[k, p] = pltpu.make_async_copy(
                p_ref.at[same[k], piece(p)], mine.at[k, piece(p)], load_sem.at[k, p]
            )
            loads[k, p].start()
    meet(me)
    started = []

    def go(copy):
        copy.start()
        started.append(copy)

    for k in order:
        for p in mix:
            go(
                remote(
                    p_ref.at[other[k], piece(p)],
                    theirs.at[k, piece(p)],
                    pair_send.at[k, p],
                    pair_recv.at[k, p],
                    other[0],
                )
            )

    def fold(k, p):
        loads[k, p].wait()
        spot = theirs.at[k, piece(p)]
        remote(spot, spot, pair_send.at[k, p], pair_recv.at[k, p], other[0]).wait_recv()
        add_rows(mine.at[k], p * step, step, 32, mine.at[k], theirs.at[k])

    def ship(k, p):
        go(
            remote(
                mine.at[k, piece(p)],
                got.at[k - 1, piece(p)],
                send_sem.at[k - 1, p],
                recv_sem.at[k - 1, p],
                same[k],
            )
        )

    for p in mix:
        fold(3, p)
        to = same[1] if p < half else same[2]
        go(remote(mine.at[3, piece(p)], transit.at[piece(p)], over_send.at[p], over_recv.at[p], to))
    for a, b in zip(low, high):
        for k, p in ((1, a), (2, b)):
            fold(k, p)
            ship(k, p)
    for a, b in zip(low, high):
        for k, p in ((2, a), (1, b)):
            fold(k, p)
            spot = transit.at[piece(p)]
            remote(spot, spot, over_send.at[p], over_recv.at[p], other[0]).wait_recv()
            add_rows(mine.at[k], p * step, step, 32, mine.at[k], transit)
            ship(k, p)
    for p in mix:
        fold(0, p)
    for p in mix:
        for k in (0, 1):
            spot = got.at[k, piece(p)]
            remote(spot, spot, send_sem.at[k, p], recv_sem.at[k, p], other[0]).wait_recv()
        add_rows(o_ref, p * step, step, 32, mine.at[0], got.at[0], got.at[1])
    for copy in started:
        copy.wait_send()


def any_scatter_kernel(n, meet, p_ref, o_ref, mine, theirs, got, load_sem, pair_send, pair_recv, send_sem, recv_sem):
    me = lax.axis_index("expert")
    same, other, _, _ = any_places(n, me)
    rows = p_ref.shape[1]
    order = list(range(1, n // 2)) + [0]
    loads = {}
    for k in order:
        loads[k] = pltpu.make_async_copy(p_ref.at[same[k]], mine.at[k], load_sem.at[k])
        loads[k].start()
    meet(me)
    started = []
    for k in order:
        copy = remote(p_ref.at[other[k]], theirs.at[k], pair_send.at[k], pair_recv.at[k], other[0])
        copy.start()
        started.append(copy)
    for k in order:
        loads[k].wait()
        remote(theirs.at[k], theirs.at[k], pair_send.at[k], pair_recv.at[k], other[0]).wait_recv()
        add_rows(mine.at[k], 0, rows, 32, mine.at[k], theirs.at[k])
        if k:
            copy = remote(mine.at[k], got.at[k], send_sem.at[k], recv_sem.at[k], same[k])
            copy.start()
            started.append(copy)
    for k in range(1, n // 2):
        remote(got.at[k], got.at[k], send_sem.at[k], recv_sem.at[k], other[0]).wait_recv()
    add_rows(o_ref, 0, rows, 32, mine.at[0], *[got.at[k] for k in range(1, n // 2)])
    for copy in started:
        copy.wait_send()


def scatter_sum(x, n, replicas, collective_id, riders=(), parts=4):
    chips = n // 2
    shape = x.shape[1:]
    blocks = pltpu.VMEM((chips,) + shape, bf16)
    if n == 8:
        kernel = functools.partial(quad_scatter_kernel, parts)
        scratch = [blocks, blocks, pltpu.VMEM(shape, bf16), pltpu.VMEM((2,) + shape, bf16)]
        scratch += [DMA((4, parts))] * 3 + [DMA((parts,))] * 2 + [DMA((2, parts))] * 2
    else:
        kernel = functools.partial(any_scatter_kernel, n)
        scratch = [blocks] * 3 + [DMA((chips,))] * 5
    return riding_call(
        n,
        replicas,
        kernel,
        [(x, AWAY_SPEC)],
        [(jax.ShapeDtypeStruct(shape, f32), VMEM_SPEC)],
        scratch,
        list(riders),
        collective_id,
        f"scatter_sum_{collective_id}",
    )


def dot(left, right, left_dim=1, right_dim=0):
    return lax.dot_general(
        left, right, (((left_dim,), (right_dim,)), ((), ())), preferred_element_type=f32
    )


def head_values(lin, gain, cosine, signed_sine):
    inverse = lax.rsqrt(jnp.mean(lin * lin, axis=-1, keepdims=True) + norm_eps)
    normed = lin * inverse * gain
    half = lin.shape[1] // 2
    turned = normed * cosine + pltpu.roll(normed, half, 1) * signed_sine
    return inverse, turned.astype(bf16)


def head_probs(q_rot, k_rot, length, score_scale):
    scores = dot(q_rot, k_rot, 1, 1) * score_scale
    key = lax.broadcasted_iota(jnp.int32, scores.shape, 1)
    masked = jnp.where(key < length, scores, big_negative)
    raised = jnp.exp(masked - jnp.max(masked, axis=-1, keepdims=True))
    return raised / jnp.sum(raised, axis=-1, keepdims=True)


def attend_kernel(
    heads, head_dim, lengths_ref, x_ref, w_ref, wo_ref, qg_ref, kg_ref, cos_ref, sin_ref, mixed_ref, part_ref
):
    length = lengths_ref[pl.program_id(0)]
    wide = heads * head_dim
    qkv = dot(x_ref[0], w_ref[...])
    for h in range(heads):
        at = h * head_dim
        _, q_rot = head_values(qkv[:, at : at + head_dim], qg_ref[...], cos_ref[...], sin_ref[...])
        _, k_rot = head_values(
            qkv[:, wide + at : wide + at + head_dim], kg_ref[...], cos_ref[...], sin_ref[...]
        )
        v = qkv[:, 2 * wide + at : 2 * wide + at + head_dim].astype(bf16)
        probs = head_probs(q_rot, k_rot, length, 1.0 / math.sqrt(head_dim))
        mixed_ref[0, :, at : at + head_dim] = dot(probs.astype(bf16), v).astype(bf16)
    part_ref[0] = dot(mixed_ref[0], wo_ref[...]).astype(bf16)


def attend(lengths, x, w_qkv, w_out, query_g, key_g, cosine, signed_sine):
    seqs, rows, width = x.shape
    head_dim = query_g.shape[0]
    wide = w_qkv.shape[1] // 3
    whole = lambda s, lens: (0, 0)
    table = pl.BlockSpec((rows, head_dim), whole)
    gain = pl.BlockSpec((1, head_dim), whole)
    return pl.pallas_call(
        functools.partial(attend_kernel, wide // head_dim, head_dim),
        out_shape=[
            jax.ShapeDtypeStruct((seqs, rows, wide), bf16),
            jax.ShapeDtypeStruct((seqs, rows, width), bf16),
        ],
        grid_spec=pltpu.PrefetchScalarGridSpec(
            num_scalar_prefetch=1,
            grid=(seqs,),
            in_specs=[
                pl.BlockSpec((1, rows, width), lambda s, lens: (s, 0, 0)),
                pl.BlockSpec((width, 3 * wide), whole),
                pl.BlockSpec((wide, width), whole),
                gain,
                gain,
                table,
                table,
            ],
            out_specs=[
                pl.BlockSpec((1, rows, wide), lambda s, lens: (s, 0, 0)),
                pl.BlockSpec((1, rows, width), lambda s, lens: (s, 0, 0)),
            ],
        ),
        compiler_params=pltpu.CompilerParams(vmem_limit_bytes=kernel_vmem),
        cost_estimate=small_cost,
        name="attend",
    )(lengths, x, w_qkv, w_out, query_g[None, :], key_g[None, :], cosine, signed_sine)


def attend_back_kernel(
    heads,
    head_dim,
    lengths_ref,
    x_ref,
    g_ref,
    mixed_ref,
    w_ref,
    wo_ref,
    qg_ref,
    kg_ref,
    cos_ref,
    sin_ref,
    part_ref,
    dw_ref,
    dgain_ref,
    dw_acc,
    dwo_acc,
    gain_acc,
    gqkv_ref,
):
    step = pl.program_id(0)
    length = lengths_ref[step]
    wide = heads * head_dim
    scale = 1.0 / math.sqrt(head_dim)
    cosine, signed_sine = cos_ref[...], sin_ref[...]

    @pl.when(step == 0)
    def _():
        dw_acc[...] = jnp.zeros_like(dw_acc)
        dwo_acc[...] = jnp.zeros_like(dwo_acc)
        gain_acc[...] = jnp.zeros_like(gain_acc)

    qkv = dot(x_ref[0], w_ref[...])
    g_mixed = dot(g_ref[0], wo_ref[...], 1, 1).astype(bf16)
    dwo_acc[...] += dot(mixed_ref[0], g_ref[0], 0, 0)
    for h in range(heads):
        at = h * head_dim
        q_lin = qkv[:, at : at + head_dim]
        k_lin = qkv[:, wide + at : wide + at + head_dim]
        v = qkv[:, 2 * wide + at : 2 * wide + at + head_dim].astype(bf16)
        q_inv, q_rot = head_values(q_lin, qg_ref[...], cosine, signed_sine)
        k_inv, k_rot = head_values(k_lin, kg_ref[...], cosine, signed_sine)
        probs = head_probs(q_rot, k_rot, length, scale)
        gm = g_mixed[:, at : at + head_dim]
        g_probs = dot(gm, v, 1, 1)
        g_scores = (probs * (g_probs - jnp.sum(probs * g_probs, axis=-1, keepdims=True))).astype(bf16)
        g_v = dot(probs.astype(bf16), gm, 0, 0)
        for i, (g_rot, lin, inv, gain) in enumerate(
            (
                (dot(g_scores, k_rot) * scale, q_lin, q_inv, qg_ref[...]),
                (dot(g_scores, q_rot, 0, 0) * scale, k_lin, k_inv, kg_ref[...]),
            )
        ):
            w = g_rot * cosine - pltpu.roll(g_rot, head_dim // 2, 1) * signed_sine
            u = w * gain
            g_lin = inv * (u - lin * inv * inv * jnp.mean(u * lin, axis=-1, keepdims=True))
            gain_acc[i : i + 1, :] += jnp.sum(w * lin * inv, axis=0, keepdims=True)
            gqkv_ref[:, i * wide + at : i * wide + at + head_dim] = g_lin.astype(bf16)
        gqkv_ref[:, 2 * wide + at : 2 * wide + at + head_dim] = g_v.astype(bf16)
    gqkv = gqkv_ref[...]
    part_ref[0] = dot(gqkv, w_ref[...], 1, 1).astype(bf16)
    dw_acc[...] += dot(x_ref[0], gqkv, 0, 0)

    @pl.when(step == pl.num_programs(0) - 1)
    def _():
        dw_ref[:, : 3 * wide] = dw_acc[...].astype(bf16)
        for i in range(dwo_acc.shape[1] // wide):
            at = i * wide
            dw_ref[at : at + wide, 3 * wide :] = dwo_acc[:, at : at + wide].astype(bf16)
        dgain_ref[...] = gain_acc[...]


def attend_back(lengths, x, g, mixed, w_qkv, w_out, query_g, key_g, cosine, signed_sine):
    seqs, rows, width = x.shape
    head_dim = query_g.shape[0]
    wide = w_qkv.shape[1] // 3
    whole = lambda s, lens: (0, 0)
    block = lambda s, lens: (s, 0, 0)
    table = pl.BlockSpec((rows, head_dim), whole)
    gain = pl.BlockSpec((1, head_dim), whole)
    return pl.pallas_call(
        functools.partial(attend_back_kernel, wide // head_dim, head_dim),
        out_shape=(
            jax.ShapeDtypeStruct((seqs, rows, width), bf16),
            jax.ShapeDtypeStruct((width, 4 * wide), bf16),
            jax.ShapeDtypeStruct((8, head_dim), f32),
        ),
        grid_spec=pltpu.PrefetchScalarGridSpec(
            num_scalar_prefetch=1,
            grid=(seqs,),
            in_specs=[
                pl.BlockSpec((1, rows, width), block),
                pl.BlockSpec((1, rows, width), block),
                pl.BlockSpec((1, rows, wide), block),
                pl.BlockSpec((width, 3 * wide), whole),
                pl.BlockSpec((wide, width), whole),
                gain,
                gain,
                table,
                table,
            ],
            out_specs=(
                pl.BlockSpec((1, rows, width), block),
                pl.BlockSpec((width, 4 * wide), whole),
                pl.BlockSpec((8, head_dim), whole),
            ),
            scratch_shapes=[
                pltpu.VMEM((width, 3 * wide), f32),
                pltpu.VMEM((wide, width), f32),
                pltpu.VMEM((8, head_dim), f32),
                pltpu.VMEM((rows, 3 * wide), bf16),
            ],
        ),
        compiler_params=pltpu.CompilerParams(vmem_limit_bytes=kernel_vmem),
        cost_estimate=small_cost,
        name="attend_back",
    )(lengths, x, g, mixed, w_qkv, w_out, query_g[None, :], key_g[None, :], cosine, signed_sine)


def slot_matrix(slot_row, capacity):
    return lax.broadcasted_iota(jnp.int32, (capacity, slot_row.shape[1]), 0) == slot_row


def stack(pieces):
    return pieces[0] if len(pieces) == 1 else jnp.concatenate(pieces, axis=0)


def expert_in_kernel(capacity, x_ref, cot_ref, slot_ref, gate_ref, wg_ref, wu_ref, in_ref, gr_ref, act_ref, g_ref, u_ref):
    for j in range(wg_ref.shape[0]):
        rows, grads = [], []
        for s in range(x_ref.shape[0]):
            chosen = slot_matrix(slot_ref[j, s], capacity)
            one_hot = jnp.where(chosen, 1.0, 0.0).astype(bf16)
            weight = jnp.sum(jnp.where(chosen, gate_ref[j, s], 0.0), axis=1, keepdims=True)
            rows.append(dot(one_hot, x_ref[s]))
            grads.append(weight * dot(one_hot, cot_ref[s]))
        taken = stack(rows).astype(bf16)
        in_ref[j] = taken
        gr_ref[j] = stack(grads).astype(bf16)
        gate_in = dot(taken, wg_ref[j])
        up_in = dot(taken, wu_ref[j])
        g_ref[j] = gate_in
        u_ref[j] = up_in
        act_ref[j] = (gate_in * jax.nn.sigmoid(gate_in) * up_in).astype(bf16)


def step_rows(groups):
    return 2 if groups % 2 == 0 else 1


def expert_forward(mlp_all, cot_all, slot_of, gates, w_gate, w_up, capacity, index):
    groups, tok_rows, width = mlp_all.shape
    local, ff = 1, w_gate.shape[2]
    seqs = step_rows(groups)
    slots = seqs * capacity
    tok = pl.BlockSpec((seqs, tok_rows, width), lambda i: (i, 0, 0))
    route = pl.BlockSpec((local, seqs, 1, tok_rows), lambda i: (index, i, 0, 0))
    weight = pl.BlockSpec((local, width, ff), lambda i: (index, 0, 0), pipeline_mode=pl.Buffered(1))
    wide = pl.BlockSpec((local, slots, width), lambda i: (0, i, 0))
    slim = pl.BlockSpec((local, slots, ff), lambda i: (0, i, 0))
    total = groups * capacity
    return pl.pallas_call(
        functools.partial(expert_in_kernel, capacity),
        out_shape=[
            jax.ShapeDtypeStruct((local, total, width), bf16),
            jax.ShapeDtypeStruct((local, total, width), bf16),
            jax.ShapeDtypeStruct((local, total, ff), bf16),
            jax.ShapeDtypeStruct((local, total, ff), f32),
            jax.ShapeDtypeStruct((local, total, ff), f32),
        ],
        grid=(groups // seqs,),
        in_specs=[tok, tok, route, route, weight, weight],
        out_specs=[wide, wide, slim, slim, slim],
        compiler_params=pltpu.CompilerParams(vmem_limit_bytes=kernel_vmem),
        cost_estimate=small_cost,
        name="expert_forward",
    )(mlp_all, cot_all, slot_of[:, :, None, :], gates[:, :, None, :], w_gate, w_up)


def expert_out_kernel(capacity, *refs):
    act_refs = refs[:-6]
    cot_ref, slot_ref, gate_ref, wd_ref, sum_ref, gg_ref = refs[-6:]
    parts = [None] * cot_ref.shape[0]
    for j in range(wd_ref.shape[0]):
        out = dot(act_refs[j][0], wd_ref[j])
        for s in range(cot_ref.shape[0]):
            one_hot = jnp.where(slot_matrix(slot_ref[j, s], capacity), 1.0, 0.0).astype(bf16)
            here = dot(one_hot, out[s * capacity : (s + 1) * capacity].astype(bf16), 0, 0)
            gg_ref[j, s] = jnp.sum(here * cot_ref[s].astype(f32), axis=1, keepdims=True)
            term = gate_ref[j, s] * here
            parts[s] = term if j == 0 else parts[s] + term
    for s in range(cot_ref.shape[0]):
        sum_ref[s] = parts[s].astype(bf16)


def expert_combine(acts, cot_all, slot_of, gates, w_down, capacity):
    groups, tok_rows, width = cot_all.shape
    local, ff, _ = w_down.shape
    seqs = step_rows(groups)
    tok = pl.BlockSpec((seqs, tok_rows, width), lambda i: (i, 0, 0))
    route = pl.BlockSpec((local, seqs, 1, tok_rows), lambda i: (0, i, 0, 0))
    column = pl.BlockSpec((local, seqs, tok_rows, 1), lambda i: (0, i, 0, 0))
    weight = pl.BlockSpec((local, ff, width), lambda i: (0, 0, 0), pipeline_mode=pl.Buffered(1))
    slim = pl.BlockSpec((1, seqs * capacity, ff), lambda i: (0, i, 0))
    return pl.pallas_call(
        functools.partial(expert_out_kernel, capacity),
        out_shape=[
            jax.ShapeDtypeStruct((groups, tok_rows, width), bf16),
            jax.ShapeDtypeStruct((local, groups, tok_rows, 1), f32),
        ],
        grid=(groups // seqs,),
        in_specs=[slim] * local + [tok, route, column, weight],
        out_specs=[tok, column],
        compiler_params=pltpu.CompilerParams(vmem_limit_bytes=kernel_vmem),
        cost_estimate=small_cost,
        name="expert_combine",
    )(*acts, cot_all, slot_of[:, :, None, :], gates[:, :, :, None], w_down)


def expert_back_kernel(capacity, *refs):
    local = (len(refs) - 7) // 3
    gr_refs, g_refs, u_refs = (refs[i * local : (i + 1) * local] for i in range(3))
    slot_ref, wg_ref, wu_ref, wd_ref, gg_ref, gu_ref, part_ref = refs[3 * local :]
    seqs = part_ref.shape[0]
    parts = [None] * seqs
    for j in range(wd_ref.shape[0]):
        grad_act = dot(gr_refs[j][0], wd_ref[j], 1, 1)
        gate_in = g_refs[j][0]
        sigma = jax.nn.sigmoid(gate_in)
        grad_up = (grad_act * (gate_in * sigma)).astype(bf16)
        grad_gate = (grad_act * u_refs[j][0] * sigma * (1.0 + gate_in * (1.0 - sigma))).astype(bf16)
        gg_ref[j] = grad_gate
        gu_ref[j] = grad_up
        rows = dot(grad_gate, wg_ref[j], 1, 1) + dot(grad_up, wu_ref[j], 1, 1)
        for s in range(seqs):
            one_hot = jnp.where(slot_matrix(slot_ref[j, s], capacity), 1.0, 0.0).astype(bf16)
            term = dot(one_hot, rows[s * capacity : (s + 1) * capacity].astype(bf16), 0, 0)
            parts[s] = term if j == 0 else parts[s] + term
    for s in range(seqs):
        part_ref[s] = parts[s].astype(bf16)


def expert_back(grad_recv, gate_in, up_in, slot_of, w_gate, w_up, w_down, groups, tok_rows, capacity):
    local, width, ff = w_gate.shape
    seqs = step_rows(groups)
    slots = seqs * capacity
    total = groups * capacity
    tok = pl.BlockSpec((seqs, tok_rows, width), lambda i: (i, 0, 0))
    route = pl.BlockSpec((local, seqs, 1, tok_rows), lambda i: (0, i, 0, 0))
    once = pl.Buffered(1)
    weight = pl.BlockSpec((local, width, ff), lambda i: (0, 0, 0), pipeline_mode=once)
    down = pl.BlockSpec((local, ff, width), lambda i: (0, 0, 0), pipeline_mode=once)
    wide = pl.BlockSpec((1, slots, width), lambda i: (0, i, 0))
    one = pl.BlockSpec((1, slots, ff), lambda i: (0, i, 0))
    slim = pl.BlockSpec((local, slots, ff), lambda i: (0, i, 0))
    return pl.pallas_call(
        functools.partial(expert_back_kernel, capacity),
        out_shape=[
            jax.ShapeDtypeStruct((local, total, ff), bf16),
            jax.ShapeDtypeStruct((local, total, ff), bf16),
            jax.ShapeDtypeStruct((groups, tok_rows, width), bf16),
        ],
        grid=(groups // seqs,),
        in_specs=[wide] * local + [one] * (2 * local) + [route, weight, weight, down],
        out_specs=[slim, slim, tok],
        compiler_params=pltpu.CompilerParams(vmem_limit_bytes=kernel_vmem),
        cost_estimate=small_cost,
        name="expert_back",
    )(*grad_recv, *gate_in, *up_in, slot_of[:, :, None, :], w_gate, w_up, w_down)


def assemble_kernel(
    order_ref, x_ref, grad_ref, out_ref, last_ref, q_ref, k_ref, v_ref, o_ref, grad_input_ref, output_ref, up_ref
):
    wide = x_ref.shape[3] // 4
    for i, to in enumerate((q_ref, k_ref, v_ref, o_ref)):
        for s in range(x_ref.shape[1]):
            to[:, s * wide : (s + 1) * wide] = x_ref[0, s, :, i * wide : (i + 1) * wide].astype(f32)
    grad_input_ref[...] = grad_ref[0].astype(f32)
    output_ref[...] = out_ref[0]
    up_ref[...] = last_ref[...]


def assemble(order_row, x, grad_home, out_home, last):
    shares, blocks, rows, columns = x.shape
    _, dealt, width = grad_home.shape
    local, up_rows, ff = last.shape
    weight = jax.ShapeDtypeStruct((shares * rows, width), f32)
    at = lambda p, order: (p, 0)
    home = pl.BlockSpec((1, dealt, width), lambda p, order: (order[p], 0, 0))
    part = up_rows // shares
    return pl.pallas_call(
        assemble_kernel,
        out_shape=[weight] * 4
        + [
            jax.ShapeDtypeStruct((shares * dealt, width), f32),
            jax.ShapeDtypeStruct((shares * dealt, width), bf16),
            jax.ShapeDtypeStruct((local, up_rows, ff), f32),
        ],
        grid_spec=pltpu.PrefetchScalarGridSpec(
            num_scalar_prefetch=1,
            grid=(shares,),
            in_specs=[pl.BlockSpec((1, blocks, rows, columns), lambda p, order: (p, 0, 0, 0)), home, home]
            + [pl.BlockSpec((local, part, ff), lambda p, order: (0, p, 0))],
            out_specs=[pl.BlockSpec((rows, width), at)] * 4
            + [pl.BlockSpec((dealt, width), at)] * 2
            + [pl.BlockSpec((local, part, ff), lambda p, order: (0, p, 0))],
        ),
        compiler_params=pltpu.CompilerParams(vmem_limit_bytes=kernel_vmem),
        cost_estimate=small_cost,
        name="assemble",
    )(order_row, x, grad_home, out_home, last)


def pad_rows(flat, tile):
    rows = -(-flat.shape[0] // (128 * tile)) * tile
    return jnp.pad(flat, (0, rows * 128 - flat.shape[0])).reshape(rows, 128)


def einf(spec, left, right):
    return jnp.einsum(spec, left, right, preferred_element_type=f32)


def body(
    tokens,
    cotangent,
    lengths,
    deal_order,
    routes,
    balance_coef,
    w_query,
    w_key,
    w_value,
    w_out,
    w_router,
    attn_gain,
    mlp_gain,
    query_gain,
    key_gain,
    w_gate,
    w_up,
    w_down,
):
    groups = lax.axis_size("expert")
    replicas = lax.axis_size("dp")
    me = lax.axis_index("expert")
    tok_rows, width = tokens.shape
    block_rows = tok_rows // replicas
    total_slots = float(tok_rows * replicas * groups)
    shard_rows = w_query.shape[0]
    local_experts = w_gate.shape[0]
    experts = local_experts * groups
    top_k = routes.shape[1]
    capacity = tok_rows * top_k * 9 // (8 * experts)

    order_row = lax.dynamic_index_in_dim(deal_order, me, 0, keepdims=False)
    dp_ids = jnp.arange(replicas, dtype=jnp.int32)
    matched = (order_row[:, None] == dp_ids[None, :]).astype(jnp.int32)
    inverse_order = jnp.sum(matched * dp_ids[:, None], axis=0)

    def blocks_to_deal(values):
        return values.reshape(replicas, block_rows, width)[inverse_order]

    small = jnp.concatenate(
        [w_router.reshape(-1), attn_gain, mlp_gain, query_gain, key_gain]
    )
    ints = jnp.concatenate([routes.reshape(-1), jnp.broadcast_to(lengths, (top_k,))])
    small_all, ints_all, seq_tokens, w_qkv = front(
        groups,
        replicas,
        0,
        pad_rows(small, 16),
        pad_rows(ints, 8),
        blocks_to_deal(tokens),
        w_query,
        w_key,
        w_value,
    )
    small_all, ints_all = small_all.reshape(groups, -1), ints_all.reshape(groups, -1)
    w_qkv = w_qkv.reshape(width, -1)
    n_router = shard_rows * experts
    cuts = [0, n_router]
    for gain in (attn_gain, mlp_gain, query_gain, key_gain):
        cuts.append(cuts[-1] + gain.shape[0])
    router_full = small_all[:, :n_router].reshape(width, experts)
    attn_g, mlp_g, query_g, key_g = (
        small_all[:, cuts[i] : cuts[i + 1]].reshape(-1).astype(f32) for i in range(1, 5)
    )
    head_dim = query_g.shape[0]
    local_width = w_query.shape[1] // groups

    routes_all = ints_all[:, : tok_rows * top_k].reshape(groups, tok_rows, top_k)
    lengths_all = ints_all[:, tok_rows * top_k]
    positions = jnp.arange(tok_rows, dtype=jnp.int32)
    live_all = (positions[None, :] < lengths_all[:, None]).astype(f32)
    live_rows = (positions < lengths[0]).astype(f32)

    inputs = seq_tokens.astype(f32)
    normed, inv_first = norm_fwd(inputs, attn_g)
    attn_in = normed.astype(bf16)
    attn_all, seq_cot = gather_rows(
        attn_in, groups, replicas, 1, riders=[Deal(blocks_to_deal(cotangent), groups, replicas)]
    )
    grad_output = seq_cot.astype(f32) * live_rows[:, None]
    cot_all = lax.all_gather(grad_output.astype(bf16), "expert", axis=0, tiled=False)

    cosine, signed_sine = rotary_tables(tok_rows, head_dim)
    mixed, hidden_part = attend(
        lengths_all, attn_all, w_qkv, w_out, query_g, key_g, cosine, signed_sine
    )
    hidden = inputs + scatter_sum(hidden_part, groups, replicas, 8)[0]
    mlp_normed, inv_second = norm_fwd(hidden, mlp_g)
    mlp_in = mlp_normed.astype(bf16)
    logits = einf("td,de->te", mlp_in, router_full)
    my_router = jax.nn.softmax(logits, axis=-1)
    mlp_all, router = gather_rows(
        mlp_in,
        groups,
        replicas,
        2,
        riders=[SmallGather(pad_rows(my_router.reshape(-1), 8), groups, replicas)],
    )
    router = router.reshape(groups, -1)[:, : tok_rows * experts].reshape(groups, tok_rows, experts)
    expert_ids = jnp.arange(experts, dtype=jnp.int32)
    picked = jnp.sum(
        (routes_all[:, :, :, None] == expert_ids).astype(f32), axis=2
    )
    chosen_sum = jnp.sum(picked * router, axis=-1, keepdims=True)
    gates = picked * router / chosen_sum
    counts = jnp.sum(picked * live_all[:, :, None], axis=(0, 1))
    prob_sums = jnp.sum(router * live_all[:, :, None], axis=(0, 1))
    live_count = jnp.sum(live_all)[None]
    stats = pad_rows(jnp.concatenate([counts, prob_sums, live_count]), 8)

    first = me * local_experts
    own_picked = lax.dynamic_slice_in_dim(picked, first, local_experts, 2)
    own_gates = lax.dynamic_slice_in_dim(gates, first, local_experts, 2)
    before = (positions[:, None] > positions[None, :]).astype(bf16)
    rank = einf("tu,suj->jst", before, own_picked.astype(bf16))
    own_picked = own_picked.transpose(2, 0, 1)
    own_gates = own_gates.transpose(2, 0, 1)
    slot_of = jnp.where(own_picked > 0.5, rank.astype(jnp.int32), -1)
    expert_in, grad_recv, act_low, gate_in, up_in, total_down = [], [], [], [], [], []
    for j in range(local_experts):
        taken, recv, act, gate, up = expert_forward(
            mlp_all, cot_all, slot_of, own_gates, w_gate, w_up, capacity, j
        )
        grad_down_w = einf("rf,rd->fd", act[0], recv[0]).astype(bf16)
        act, recv, mlp_all, grad_down_w = lax.optimization_barrier((act, recv, mlp_all, grad_down_w))
        total_down.append(lax.psum_scatter(grad_down_w, "dp", scatter_dimension=0, tiled=True))
        for values, value in zip(
            (expert_in, grad_recv, act_low, gate_in, up_in), (taken, recv, act, gate, up)
        ):
            values.append(value)
    grad_gate_in, grad_up_in, grad_part = expert_back(
        grad_recv, gate_in, up_in, slot_of, w_gate, w_up, w_down, groups, tok_rows, capacity
    )
    grad_gate_w = jnp.stack(
        [einf("rd,rf->df", expert_in[j][0], grad_gate_in[j]).astype(bf16) for j in range(local_experts)]
    )
    grad_part, act_low, grad_gate_w = lax.optimization_barrier((grad_part, act_low, grad_gate_w))
    total_gate = lax.psum_scatter(grad_gate_w, "dp", scatter_dimension=1, tiled=True)
    sum_part, own_grad_gates = expert_combine(act_low, cot_all, slot_of, own_gates, w_down, capacity)
    gate_rows = own_grad_gates.transpose(1, 0, 2, 3).reshape(groups, -1, 128)
    grad_mlp_in, gate_back, sums = scatter_sum(
        grad_part,
        groups,
        replicas,
        3,
        riders=[Exchange(gate_rows, groups, replicas), DpSum(stats, groups, replicas)],
    )
    sums = sums.reshape(-1)
    counts, prob_sums = sums[:experts], sums[experts : 2 * experts]
    live_count = sums[2 * experts : 2 * experts + 1]
    fraction = counts / (live_count * top_k)
    balance_loss = balance_coef * (experts * jnp.sum(fraction * prob_sums / total_slots))

    grad_gates = gate_back.reshape(experts, tok_rows).T
    my_picked = lax.dynamic_index_in_dim(picked, me, 0, keepdims=False)
    my_gates = lax.dynamic_index_in_dim(gates, me, 0, keepdims=False)
    my_sum = lax.dynamic_index_in_dim(chosen_sum, me, 0, keepdims=False)
    grad_prob = (
        my_picked * (grad_gates - jnp.sum(grad_gates * my_gates, axis=1, keepdims=True)) / my_sum
        + live_rows[:, None] * (balance_coef * experts / total_slots) * fraction[None, :]
    )
    grad_logits = (
        my_router * (grad_prob - jnp.sum(my_router * grad_prob, axis=-1, keepdims=True))
    ).astype(bf16)
    grad_router_w = einf("td,te->de", mlp_in, grad_logits)
    grad_mlp_in = grad_mlp_in + einf("te,de->td", grad_logits, router_full)

    grad_hidden_norm, grad_mlp_g = norm_back(hidden, inv_second, mlp_g, grad_mlp_in, 0)
    grad_hidden = grad_output + grad_hidden_norm
    grad_hidden_low = grad_hidden.astype(bf16)
    grad_hidden_low, total_down = lax.optimization_barrier((grad_hidden_low, total_down))
    (hidden_all,) = gather_rows(grad_hidden_low, groups, replicas, 4)
    grad_attn_part, grad_attn_w, grad_gains = attend_back(
        lengths_all, attn_all, hidden_all, mixed, w_qkv, w_out, query_g, key_g, cosine, signed_sine
    )
    grad_query_g, grad_key_g = grad_gains[0], grad_gains[1]
    attn_share = lax.psum_scatter(
        grad_attn_w.reshape(groups, shard_rows, 4 * local_width), "dp", scatter_dimension=1, tiled=True
    )
    sum_part, grad_attn_part = lax.optimization_barrier((sum_part, grad_attn_part))
    (expert_sum,) = scatter_sum(sum_part, groups, replicas, 6)
    out_seq = (live_rows[:, None] * (hidden + expert_sum)).astype(bf16)

    def to_deal(values):
        return values.reshape(replicas, block_rows, width)

    grad_up_in, out_seq, total_gate = lax.optimization_barrier((grad_up_in, out_seq, total_gate))
    total_gate = total_gate.astype(f32)
    total_gate, grad_attn_part = lax.optimization_barrier((total_gate, grad_attn_part))
    grad_up_w = [
        einf("rd,rf->df", expert_in[j][0], grad_up_in[j]).astype(bf16) for j in range(local_experts)
    ]
    grad_up_w, grad_attn_part = lax.optimization_barrier((grad_up_w, grad_attn_part))
    grad_attn_in, out_home = scatter_sum(
        grad_attn_part, groups, replicas, 5, riders=[Deal(to_deal(out_seq), groups, replicas)]
    )
    grad_input_norm, grad_attn_g = norm_back(inputs, inv_first, attn_g, grad_attn_in, 0)
    grad_seq = (grad_hidden + grad_input_norm).astype(bf16)

    pieces = [grad_router_w.reshape(groups, n_router)] + [
        value.reshape(groups, -1) for value in (grad_attn_g, grad_mlp_g, grad_query_g, grad_key_g)
    ]
    pieces = jnp.concatenate(pieces, axis=1)
    pad = -pieces.shape[1] % 1024
    pieces = jnp.pad(pieces, ((0, 0), (0, pad))).reshape(groups, -1, 128)

    pieces, grad_seq, attn_share = lax.optimization_barrier((pieces, grad_seq, attn_share))
    attn_sum, total_up, sum_small, grad_home = close(
        attn_share,
        3 * local_width,
        grad_up_w,
        groups,
        replicas,
        7,
        [SmallSum(pieces, groups, replicas), Deal(to_deal(grad_seq), groups, replicas)],
    )
    sum_q, sum_k, sum_v, sum_o, grad_input, output, total_up = assemble(
        order_row, attn_sum, to_deal(grad_home), to_deal(out_home), total_up
    )
    sum_small = sum_small.reshape(-1)
    sum_r = sum_small[:n_router].reshape(shard_rows, experts)
    sum_ga, sum_gm, sum_gq, sum_gk = (sum_small[cuts[i] : cuts[i + 1]] for i in range(1, 5))
    total_down = jnp.stack(total_down).astype(f32)
    return (
        output,
        balance_loss,
        grad_input,
        sum_q,
        sum_k,
        sum_v,
        sum_o,
        sum_r,
        sum_ga,
        sum_gm,
        sum_gq,
        sum_gk,
        total_gate,
        total_up,
        total_down,
    )


def solution(mesh):
    rows = P(("dp", "expert"), None)
    weight = P("expert", None)
    gain = P("expert")
    cube = P("expert", None, None)
    cube_out = P("expert", "dp", None)
    return jax.shard_map(
        body,
        mesh=mesh,
        in_specs=(
            (rows, rows, P(("dp", "expert")), P(), rows, P())
            + (weight,) * 5
            + (gain,) * 4
            + (cube,) * 3
        ),
        out_specs=(
            (rows, P(), rows) + (weight,) * 5 + (gain,) * 4 + (cube_out,) * 3
        ),
        check_vma=False,
    )
```
